32 devices in a mesh: groups: 2 (over y), seq: 4 (over z), head: 2 (over x), rep: 2 (over core).
Axes of the slice: x: 2, y: 2, z: 4, core: 2. Of those that a mesh axis runs over, the one named last changes fastest.
Arguments:
- queries: bfloat16 [2048, 4096], P(('groups', 'seq'), ('head', 'rep')), parts along dimension 0, may hold values from -5 to 5
- keys: bfloat16 [2048, 4096], P(('groups', 'seq'), ('head', 'rep')), parts along dimension 0, may hold values from -5 to 5
- values: bfloat16 [2048, 4096], P(('groups', 'seq'), ('head', 'rep')), parts along dimension 0, may hold values from -10 to 10
- out_weight: bfloat16 [4096, 4096], P(None, ('head', 'rep')), may hold values from -0.125 to 0.125
- level_mask: int32 [16, 5], P(('groups', 'seq')), parts along dimension 0, may hold values 0 or 1
- cotangent: bfloat16 [2048, 4096], P(('groups', 'seq'), ('head', 'rep')), parts along dimension 0, may hold values from -6 to 6
Outputs:
- attended: bfloat16 [2048, 4096], P(('groups', 'seq'), ('head', 'rep')), parts along dimension 0
- q_grad: bfloat16 [2048, 4096], P(('groups', 'seq'), ('head', 'rep')), parts along dimension 0
- k_grad: bfloat16 [2048, 4096], P(('groups', 'seq'), ('head', 'rep')), parts along dimension 0
- v_grad: bfloat16 [2048, 4096], P(('groups', 'seq'), ('head', 'rep')), parts along dimension 0
- weight_grad: bfloat16 [8192, 4096], P(('groups', 'seq'), ('head', 'rep')), parts along dimension 0
The draws below stay inside these ranges and needn't reach their ends.
There are 2 independent parts, one for each index of `groups`. The reference program is written for one: setup_inputs(seed, part) draws one part's arguments, and reference() takes and returns one part's arrays. A program takes and returns all parts, laid end to end along the dimension named above; an argument that names none is the same for every part. Nothing has to cross between parts.
All inputs are finite; a program needn't handle non-finite values. No bound on the sum of `level_mask` on one device may be relied on, other than what follows from the above.
Results may differ from the reference program's by a relative error of at most 0.0095.
Values may be sent and summed in bfloat16 or wider, within the bound.
No kernel may reach another device: no remote copies, remote signals or barrier semaphores. Data moves between devices by JAX's collectives and lax.ppermute only.
A program may use at most 128 MiB of HBM per device.

```python
import jax
import jax.numpy as jnp
from jax import lax

D = 4096
HEADS = 32
HEAD_DIM = 128
BLOCK = 128
LEVELS = 5
HEAD_COLS = 4096
NBLK = 8
SEQ_LEN = 1024
N_SEQ = 4
N_HEAD = 2
N_REP = 2


def entries_field(base_key, spread):
    drawn = spread * jax.random.normal(base_key, (SEQ_LEN, HEADS * HEAD_DIM), jnp.float32)
    return jnp.clip(drawn, -5.0, 5.0)


def draw_queries(key, part):
    drawn_field = entries_field(jax.random.fold_in(key, 1), 2.0)
    return drawn_field.astype(jnp.bfloat16)


def draw_keys(key, part):
    drawn_field = entries_field(jax.random.fold_in(key, 2), 1.0)
    return drawn_field.astype(jnp.bfloat16)


def with_ends(result, rng, least, top_value):
    place = [jax.random.randint(jax.random.fold_in(rng, axis), (), 0, length) for axis, length in enumerate(result.shape)]
    main_axis = result.shape.index(max(result.shape))
    beside = place[:main_axis] + [(place[main_axis] + 1) % result.shape[main_axis]] + place[main_axis + 1:]
    return result.at[tuple(place)].set(least).at[tuple(beside)].set(top_value)


def spiked(result, stream_key, source, target, shards_of, factor):
    owner, partner = [(jnp.arange(result.shape[position]) // (result.shape[position] // shards_of)).reshape([-1 if axis == position else 1 for axis in range(result.ndim)]) for position in (source, target)]
    chosen = jax.random.permutation(stream_key, shards_of)[partner]
    strong = (owner == chosen) | (owner == (partner + shards_of // 2) % shards_of)
    return jnp.where(strong, factor * result, result)


def steps_of(stream_key, dims, cuts, least, top_value):
    factor_of, own = 1.0, jax.random.fold_in(stream_key, 6)
    for dim, blocks in cuts:
        steps = jnp.exp(jax.random.uniform(jax.random.fold_in(own, dim), (blocks,), jnp.float32, least / len(cuts), top_value / len(cuts)))
        factor_of = factor_of * jnp.repeat(steps, dims[dim] // blocks).reshape([-1 if axis == dim else 1 for axis in range(len(dims))])
    return factor_of


def gaussian(own_key, extent, scale, most, pieces=(), held_as=jnp.bfloat16):
    level = steps_of(own_key, extent, pieces, -0.22, 0.18) if pieces else 1.0
    values = jax.random.normal(own_key, extent, jnp.float32) * scale * level
    return jnp.minimum(jnp.maximum(values, -most), most).astype(held_as)


def gaussian_with(rng, extent, deviation, most, split, heavy, kind=jnp.bfloat16):
    values = deviation * jax.random.normal(rng, extent, jnp.float32)
    if split:
        values = values * steps_of(rng, extent, split, -0.22, 0.18)
    return jnp.clip(spiked(values, jax.random.fold_in(rng, 3), *heavy), -most, most).astype(kind)


def setup_inputs(seed: int = 0, part: int = 0) -> dict:
    seeds = jax.random.split(jax.random.key(seed), 7)
    part_keys = jax.random.split(jax.random.fold_in(seeds[6], part), 7)
    queries = draw_queries(jax.random.fold_in(jax.random.fold_in(seeds[6], part), 71), part)
    keys = draw_keys(jax.random.fold_in(jax.random.fold_in(seeds[6], part), 71), part)
    values = gaussian(part_keys[2], (SEQ_LEN, HEAD_COLS), 2.0, 10.0, ((0, 4), (1, 4)))
    out_weight = gaussian_with(seeds[3], (D, HEAD_COLS), HEAD_COLS ** -0.5, 0.125, ((1, 4),), (1, 0, 4, 2.0))
    level_mask = with_ends((jax.random.randint(part_keys[4], (NBLK, LEVELS), 0, 4) < 3).astype(jnp.int32), jax.random.fold_in(part_keys[4], 1), 0, 1)
    cotangent = gaussian_with(part_keys[5], (SEQ_LEN, D), 1.0, 6.0, ((0, 4), (1, 4)), (0, 1, 4, 2.0))
    return dict(queries=queries, keys=keys, values=values, out_weight=out_weight, level_mask=level_mask, cotangent=cotangent)


masked_score = -1e30


def reference(queries, keys, values, out_weight, level_mask, cotangent):
    blocks_all = SEQ_LEN // BLOCK
    columns = HEADS * HEAD_DIM
    score_scale = HEAD_DIM ** -0.5
    query_blocks = queries.reshape(blocks_all, BLOCK, HEADS, HEAD_DIM)
    key_blocks = keys.reshape(blocks_all, BLOCK, HEADS, HEAD_DIM)
    value_blocks = values.reshape(blocks_all, BLOCK, HEADS, HEAD_DIM)
    grad_rows = None
    offsets = jnp.array([2 ** level_index for level_index in range(LEVELS)], jnp.int32)
    causal = jnp.arange(BLOCK)[:, None] >= jnp.arange(BLOCK)[None, :]
    block_range = jnp.arange(blocks_all, dtype=jnp.int32)

    def attention_probs(block_index):
        targets = block_index - offsets
        usable = (targets >= 0) & (level_mask[block_index] == 1)
        clipped = jnp.maximum(targets, 0).astype(jnp.int32)
        near_keys = jnp.concatenate([key_blocks[block_index][None], key_blocks[clipped]], 0)
        near_keys = near_keys.reshape((LEVELS + 1) * BLOCK, HEADS, HEAD_DIM)
        near_values = jnp.concatenate([value_blocks[block_index][None], value_blocks[clipped]], 0)
        near_values = near_values.reshape((LEVELS + 1) * BLOCK, HEADS, HEAD_DIM)
        far_allowed = jnp.broadcast_to(jnp.repeat(usable, BLOCK)[None, :], (BLOCK, LEVELS * BLOCK))
        allowed = jnp.concatenate([causal, far_allowed], 1)
        query_f = query_blocks[block_index].astype(jnp.float32)
        scores = jnp.einsum('qhd,khd->hqk', query_f, near_keys.astype(jnp.float32)) * score_scale
        scores = jnp.where(allowed[None], scores, masked_score)
        row_max = jnp.max(scores, -1, keepdims=True)
        exponent = jnp.exp(scores - row_max)
        attn_prob = exponent / jnp.sum(exponent, -1, keepdims=True)
        return attn_prob, near_keys, near_values, clipped, query_f

    def forward_block(block_index):
        attn_prob, near_keys, near_values, clipped, query_f = attention_probs(block_index)
        attn_low = lax.optimization_barrier(attn_prob.astype(jnp.bfloat16)).astype(jnp.float32)
        mixed_block = jnp.einsum('hqk,khd->qhd', attn_low, near_values.astype(jnp.float32))
        return mixed_block.astype(jnp.bfloat16)

    mixed_heads = lax.map(forward_block, block_range).reshape(SEQ_LEN, columns)

    group_count = N_HEAD * N_REP
    group_cols = columns // group_count
    attended = jnp.zeros((SEQ_LEN, D), jnp.float32)
    for group_index in range(group_count):
        lower = group_index * group_cols
        partial_value = lax.dot_general(mixed_heads[:, lower:lower + group_cols], out_weight[:, lower:lower + group_cols],
                                  (((1,), (1,)), ((), ())), preferred_element_type=jnp.float32)
        attended = attended + lax.optimization_barrier(partial_value.astype(jnp.bfloat16)).astype(jnp.float32)
    attended = attended.astype(jnp.bfloat16)

    mixed_grad = jnp.dot(cotangent, out_weight, preferred_element_type=jnp.float32).astype(jnp.bfloat16)

    rows_each = SEQ_LEN // N_SEQ
    weight_grad = jnp.zeros((D, columns), jnp.float32)
    for shard_index in range(N_SEQ):
        lower = shard_index * rows_each
        partial_value = lax.dot_general(cotangent[lower:lower + rows_each], mixed_heads[lower:lower + rows_each],
                                  (((0,), (0,)), ((), ())), preferred_element_type=jnp.float32)
        weight_grad = weight_grad + lax.optimization_barrier(partial_value.astype(jnp.bfloat16)).astype(jnp.float32)
    weight_grad = weight_grad.astype(jnp.bfloat16)

    grad_blocks = mixed_grad.reshape(blocks_all, BLOCK, HEADS, HEAD_DIM)

    def backward_block(carry, block_index):
        key_acc, value_acc = carry
        attn_prob, near_keys, near_values, clipped, query_f = attention_probs(block_index)
        attn_low = lax.optimization_barrier(attn_prob.astype(jnp.bfloat16)).astype(jnp.float32)
        grad_f = grad_blocks[block_index].astype(jnp.float32)
        prob_grad = jnp.einsum('qhd,khd->hqk', grad_f, near_values.astype(jnp.float32))
        row_dot = jnp.sum(attn_prob * prob_grad, -1, keepdims=True)
        score_grad = (attn_prob * (prob_grad - row_dot) * score_scale).astype(jnp.bfloat16)
        score_grad = lax.optimization_barrier(score_grad).astype(jnp.float32)
        query_grad = jnp.einsum('hqk,khd->qhd', score_grad, near_keys.astype(jnp.float32)).astype(jnp.bfloat16)
        key_part = jnp.einsum('hqk,qhd->khd', score_grad, query_f).reshape(LEVELS + 1, BLOCK, HEADS, HEAD_DIM)
        value_part = jnp.einsum('hqk,qhd->khd', attn_low, grad_f).reshape(LEVELS + 1, BLOCK, HEADS, HEAD_DIM)
        targets_all = jnp.concatenate([block_index[None].astype(jnp.int32), clipped]).astype(jnp.int32)
        key_acc = key_acc.at[targets_all].add(key_part)
        value_acc = value_acc.at[targets_all].add(value_part)
        return (key_acc, value_acc), query_grad

    empty_acc = jnp.zeros((blocks_all, BLOCK, HEADS, HEAD_DIM), jnp.float32)
    (key_acc, value_acc), query_grads = lax.scan(backward_block, (empty_acc, empty_acc), block_range)
    q_grad = query_grads.reshape(SEQ_LEN, columns)
    k_grad = key_acc.astype(jnp.bfloat16).reshape(SEQ_LEN, columns)
    v_grad = value_acc.astype(jnp.bfloat16).reshape(SEQ_LEN, columns)
    return (attended, q_grad, k_grad, v_grad, weight_grad)
```

```python
import functools
import math

import jax
import jax.numpy as jnp
from jax import lax
from jax.experimental import pallas as pl
from jax.experimental.pallas import tpu as pltpu
from jax.sharding import PartitionSpec as P

HEAD_DIM = 128
BLOCK = 128
LEVELS = 5
SCALE = HEAD_DIM ** (-0.5)
LOG2_SCALE = SCALE * math.log2(math.e)
MASKED = -1e30

F32 = jnp.float32
BF16 = jnp.bfloat16
NT = (((1,), (1,)), ((), ()))


def shift(value, by):
    peers = lax.axis_size("seq")
    return lax.ppermute(
        value, "seq", [(i, i + by) for i in range(peers) if 0 <= i + by < peers]
    )


def cyclic(value, by):
    peers = lax.axis_size("seq")
    return lax.ppermute(value, "seq", [(i, (i + by) % peers) for i in range(peers)])


def swap(value, axis):
    return lax.ppermute(value, axis, [(0, 1), (1, 0)])


def dot(a, b):
    return jnp.dot(a, b, preferred_element_type=F32)


def dot_nt(a, b):
    return lax.dot_general(a, b, NT, preferred_element_type=F32)


def seen_tiles(blocks, peers):
    tiles = []
    for n in range(blocks):
        mine = [(0, n, None)]
        for level in range(LEVELS):
            target = n - 2**level
            distance = -(target // blocks)
            if distance < peers:
                mine.append((distance, target % blocks, level))
        tiles.append(mine)
    return tiles


def whole(shape):
    return pl.BlockSpec(shape, lambda h, *_: (0,) * len(shape))


def head_cols(rows):
    return pl.BlockSpec((rows, HEAD_DIM), lambda h, *_: (0, h))


def block_rows(n):
    return pl.ds(n * BLOCK, BLOCK)


def cat(parts, axis=0):
    return parts[0] if len(parts) == 1 else jnp.concatenate(parts, axis)


def causal_tile(transposed):
    rows = lax.broadcasted_iota(jnp.int32, (BLOCK, BLOCK), 0)
    cols = lax.broadcasted_iota(jnp.int32, (BLOCK, BLOCK), 1)
    return rows <= cols if transposed else rows >= cols


def forward_kernel(tiles, count, use_ref, q_ref, *refs):
    k_refs, v_refs = refs[:count], refs[count : 2 * count]
    mixed_ref, lse_ref = refs[2 * count :]
    head = pl.program_id(0)
    lane = lax.broadcasted_iota(jnp.int32, (BLOCK, HEAD_DIM), 1)
    causal = causal_tile(False)
    for n, mine in enumerate(tiles):
        keys = cat([k_refs[d][block_rows(b), :] for d, b, _ in mine])
        vals = cat([v_refs[d][block_rows(b), :] for d, b, _ in mine])
        raw = dot_nt(q_ref[block_rows(n), :], keys)
        parts = []
        for i, (_, _, level) in enumerate(mine):
            part = raw[:, i * BLOCK : (i + 1) * BLOCK]
            if level is None:
                part = jnp.where(causal, part, MASKED)
            else:
                part = jnp.where(use_ref[n * LEVELS + level] == 1, part, MASKED)
            parts.append(part)
        raw = cat(parts, 1)
        top = jnp.max(raw, 1, keepdims=True)
        grown = jnp.exp2((raw - top) * LOG2_SCALE)
        total = jnp.sum(grown, 1, keepdims=True)
        prob = grown * (1.0 / total)
        mixed_ref[block_rows(n), :] = dot(prob.astype(BF16), vals).astype(BF16)
        lse = top * LOG2_SCALE + jnp.log2(total)
        old = jnp.where(head == 0, 0.0, lse_ref[block_rows(n), :])
        lse_ref[block_rows(n), :] = jnp.where(lane == head, lse, old)


def query_kernel(tiles, count, heads_up, use_ref, q_ref, g_ref, lse_ref, *refs):
    k_refs, v_refs = refs[:count], refs[count : 2 * count]
    dq_ref, stats_ref, delta_ref = refs[2 * count :]
    head = pl.program_id(0)
    lane = lax.broadcasted_iota(jnp.int32, (BLOCK, HEAD_DIM), 1)
    causal = causal_tile(False)
    for n, mine in enumerate(tiles):
        rows = block_rows(n)
        keys = cat([k_refs[d][block_rows(b), :] for d, b, _ in mine])
        vals = cat([v_refs[d][block_rows(b), :] for d, b, _ in mine])
        lse = jnp.sum(jnp.where(lane == head, lse_ref[rows, :], 0.0), 1, keepdims=True)
        logits = dot_nt(q_ref[rows, :], keys) * LOG2_SCALE - lse
        parts = []
        for i, (_, _, level) in enumerate(mine):
            part = logits[:, i * BLOCK : (i + 1) * BLOCK]
            if level is None:
                part = jnp.where(causal, part, MASKED)
            else:
                part = jnp.where(use_ref[n * LEVELS + level] == 1, part, MASKED)
            parts.append(part)
        prob = jnp.exp2(cat(parts, 1))
        prob_grad = dot_nt(g_ref[rows, :], vals)
        delta = jnp.sum(prob * prob_grad, 1, keepdims=True)
        score_grad = (prob * (prob_grad - delta) * SCALE).astype(BF16)
        dq_ref[rows, :] = dot(score_grad, keys).astype(BF16)
        old = jnp.where(head == 0, 0.0, delta_ref[rows, :])
        delta_ref[rows, :] = jnp.where(lane == head, delta, old)

    @pl.when(head == pl.num_programs(0) - 1)
    def _():
        stats_ref[:heads_up, :] = lse_ref[...].T[:heads_up, :]
        stats_ref[heads_up : 2 * heads_up, :] = delta_ref[...].T[:heads_up, :]
        level_row = lax.broadcasted_iota(jnp.int32, (8, BLOCK), 0)
        for n in range(len(tiles)):
            rows = jnp.zeros((8, BLOCK), F32)
            for level in range(LEVELS):
                flag = jnp.where(use_ref[n * LEVELS + level] == 1, 1.0, 0.0)
                rows = jnp.where(level_row == level, flag, rows)
            stats_ref[2 * heads_up :, n * BLOCK : (n + 1) * BLOCK] = rows


def key_kernel(tiles, count, heads_up, k_ref, v_ref, *refs):
    q_refs, g_refs, s_refs = refs[:count], refs[count : 2 * count], refs[2 * count : 3 * count]
    dk_ref, dv_ref = refs[3 * count :]
    head = pl.program_id(0)
    causal = causal_tile(True)
    head_row = lax.broadcasted_iota(jnp.int32, (heads_up, BLOCK), 0)

    def of_head(stat):
        return jnp.sum(jnp.where(head_row == head, stat, 0.0), 0, keepdims=True)

    for b in range(len(tiles)):
        rows = block_rows(b)
        seers = [
            (d, n, level)
            for n, mine in enumerate(tiles)
            for d, block, level in mine
            if block == b
        ]
        ques = cat([q_refs[d][block_rows(n), :] for d, n, _ in seers])
        grads = cat([g_refs[d][block_rows(n), :] for d, n, _ in seers])
        raw = dot_nt(k_ref[rows, :], ques)
        prob_grad = dot_nt(v_ref[rows, :], grads)
        probs, score_grads = [], []
        for i, (d, n, level) in enumerate(seers):
            cols = slice(i * BLOCK, (i + 1) * BLOCK)
            here = slice(n * BLOCK, (n + 1) * BLOCK)
            lse = of_head(s_refs[d][:heads_up, here])
            delta = of_head(s_refs[d][heads_up : 2 * heads_up, here])
            if level is None:
                logits = jnp.where(causal, raw[:, cols] * LOG2_SCALE - lse, MASKED)
            else:
                row = 2 * heads_up + level
                off = lse + (1.0 - s_refs[d][row : row + 1, here]) * (-MASKED)
                logits = raw[:, cols] * LOG2_SCALE - off
            prob = jnp.exp2(logits)
            probs.append(prob.astype(BF16))
            score_grads.append((prob * (prob_grad[:, cols] - delta) * SCALE).astype(BF16))
        dv_ref[rows, :] = dot(cat(probs, 1), grads).astype(BF16)
        dk_ref[rows, :] = dot(cat(score_grads, 1), ques).astype(BF16)


def mixed_grad_kernel(count, place_ref, *refs):
    c_refs, w_ref, out_ref, acc_ref = refs[:count], refs[count], refs[count + 1], refs[count + 2]
    step = pl.program_id(0)
    for i in range(count):

        @pl.when(step == i)
        def _(i=i):
            part = dot(c_refs[i][...], w_ref[...])
            acc_ref[...] = part if i == 0 else acc_ref[...] + part

    @pl.when(step == count - 1)
    def _():
        out_ref[...] = acc_ref[...].astype(BF16)


def weight_grad_kernel(count, place_ref, c_ref, *refs):
    m_refs, out_ref = refs[:count], refs[count]
    total = None
    for p in range(count):
        part = dot(c_ref[place_ref[p]], m_refs[p][...])
        total = part if total is None else total + part
    out_ref[...] = total.astype(BF16)


VMEM_LIMIT = 48 * 1024 * 1024


def params():
    return pltpu.CompilerParams(
        dimension_semantics=("arbitrary",), vmem_limit_bytes=VMEM_LIMIT
    )


def cost(flops, bytes_accessed, exps=0):
    return pl.CostEstimate(
        flops=int(flops), bytes_accessed=int(bytes_accessed), transcendentals=int(exps)
    )


def features_here(value):
    heads, reps = lax.axis_size("head"), lax.axis_size("rep")
    if heads == 2 and reps == 2:
        h, r = lax.axis_index("head"), lax.axis_index("rep")
        across = swap(value, "head")
        blocks = [value, swap(value, "rep"), across, swap(across, "rep")]
        places = [2 * h + r, 2 * h + 1 - r, 2 * (1 - h) + r, 2 * (1 - h) + 1 - r]
        return blocks, jnp.stack(places).astype(jnp.int32)
    gathered = lax.all_gather(value, ("head", "rep"), axis=0)
    count = heads * reps
    return [gathered[i] for i in range(count)], jnp.arange(count, dtype=jnp.int32)


def summed_share(partial_value):
    heads, reps = lax.axis_size("head"), lax.axis_size("rep")
    if heads == 2 and reps == 2:
        rows, features = partial_value.shape
        h, r = lax.axis_index("head"), lax.axis_index("rep")
        parts = partial_value.reshape(rows, 2, 2, features // 4)
        give = lax.dynamic_index_in_dim(parts, 1 - r, 2, False).astype(BF16)
        keep = lax.dynamic_index_in_dim(parts, r, 2, False).astype(F32)
        keep = keep + swap(give, "rep").astype(F32)
        give = lax.dynamic_index_in_dim(keep, 1 - h, 1, False).astype(BF16)
        keep = lax.dynamic_index_in_dim(keep, h, 1, False)
        return (keep + swap(give, "head").astype(F32)).astype(BF16)
    return lax.psum_scatter(
        partial_value.astype(BF16), ("head", "rep"), scatter_dimension=1, tiled=True
    )


def per_device(queries, keys, values, out_weight, level_mask, cotangent):
    rows, columns = queries.shape
    features = out_weight.shape[0]
    heads = columns // HEAD_DIM
    heads_up = -(-heads // 8) * 8
    blocks = rows // BLOCK
    peers = lax.axis_size("seq")
    place = lax.axis_index("seq")
    tiles = seen_tiles(blocks, peers)
    distances = sorted({d for mine in tiles for d, _, _ in mine})
    count = len(distances)
    slot = {d: i for i, d in enumerate(distances)}
    tiles = [[(slot[d], b, level) for d, b, level in mine] for mine in tiles]
    pairs = sum(len(mine) for mine in tiles)

    def reached(value, sign):
        got = [value]
        for near, far in zip(distances, distances[1:]):
            got.append(shift(got[-1], sign * (far - near)))
        return got

    block_ids = place * blocks + jnp.arange(blocks, dtype=jnp.int32)
    offsets = 2 ** jnp.arange(LEVELS, dtype=jnp.int32)
    use = ((block_ids[:, None] >= offsets[None]) & (level_mask == 1)).astype(jnp.int32)
    use = use.reshape(-1)

    key_all = reached(keys, 1)
    value_all = reached(values, 1)
    query_all = reached(queries, -1)

    c_blocks, c_places = features_here(cotangent)
    group_count = len(c_blocks)
    part_cols = cotangent.shape[1]
    mixed_grad = pl.pallas_call(
        functools.partial(mixed_grad_kernel, group_count),
        grid_spec=pltpu.PrefetchScalarGridSpec(
            num_scalar_prefetch=1,
            grid=(group_count,),
            in_specs=[whole((rows, part_cols))] * group_count
            + [pl.BlockSpec((part_cols, columns), lambda i, at: (at[i], 0))],
            out_specs=whole((rows, columns)),
            scratch_shapes=[pltpu.VMEM((rows, columns), F32)],
        ),
        out_shape=jax.ShapeDtypeStruct((rows, columns), BF16),
        compiler_params=params(),
        cost_estimate=cost(2 * rows * columns * features, 2 * columns * features),
        name="mixed_grad",
    )(c_places, *c_blocks, out_weight)
    grad_all = reached(mixed_grad, -1)

    attention_flops = 2 * heads * pairs * BLOCK * BLOCK * HEAD_DIM
    array_bytes = 2 * rows * columns
    exps = heads * pairs * BLOCK * BLOCK
    smem = pl.BlockSpec(memory_space=pltpu.SMEM)
    cols = head_cols(rows)
    mixed_heads, lse = pl.pallas_call(
        functools.partial(forward_kernel, tiles, count),
        grid=(heads,),
        in_specs=[smem, cols] + [cols] * (2 * count),
        out_specs=[cols, whole((rows, HEAD_DIM))],
        out_shape=[
            jax.ShapeDtypeStruct((rows, columns), BF16),
            jax.ShapeDtypeStruct((rows, HEAD_DIM), F32),
        ],
        compiler_params=params(),
        cost_estimate=cost(2 * attention_flops, (2 * count + 2) * array_bytes, exps),
        name="attention_forward",
    )(use, queries, *key_all, *value_all)

    if peers <= 4:
        mixed_all = [mixed_heads] + [cyclic(mixed_heads, k) for k in range(1, peers)]
    else:
        gathered = lax.all_gather(mixed_heads, "seq", axis=0)
        mixed_all = [
            lax.dynamic_index_in_dim(gathered, (place - k) % peers, 0, False)
            for k in range(peers)
        ]

    partial_value = lax.dot_general(
        mixed_heads, out_weight, NT, preferred_element_type=F32
    ).astype(BF16)
    attended = summed_share(partial_value)

    stats_shape = (2 * heads_up + 8, rows)
    q_grad, stats = pl.pallas_call(
        functools.partial(query_kernel, tiles, count, heads_up),
        grid=(heads,),
        in_specs=[smem, cols, cols, whole((rows, HEAD_DIM))] + [cols] * (2 * count),
        out_specs=[cols, whole(stats_shape)],
        out_shape=[
            jax.ShapeDtypeStruct((rows, columns), BF16),
            jax.ShapeDtypeStruct(stats_shape, F32),
        ],
        scratch_shapes=[pltpu.VMEM((rows, HEAD_DIM), F32)],
        compiler_params=params(),
        cost_estimate=cost(3 * attention_flops, (2 * count + 3) * array_bytes, exps),
        name="attention_query_grad",
    )(use, queries, mixed_grad, lse, *key_all, *value_all)

    stats_all = [stats] + [shift(stats, -d) for d in distances[1:]]
    k_grad, v_grad = pl.pallas_call(
        functools.partial(key_kernel, tiles, count, heads_up),
        grid=(heads,),
        in_specs=[cols] * (2 + 2 * count) + [whole(stats_shape)] * count,
        out_specs=[cols, cols],
        out_shape=[jax.ShapeDtypeStruct((rows, columns), BF16)] * 2,
        compiler_params=params(),
        cost_estimate=cost(4 * attention_flops, (2 * count + 4) * array_bytes, exps),
        name="attention_key_grad",
    )(keys, values, *query_all, *grad_all, *stats_all)

    h, r = lax.axis_index("head"), lax.axis_index("rep")
    n_head, n_rep = lax.axis_size("head"), lax.axis_size("rep")
    step_of = lambda i: (i // n_rep) + n_head * (i % n_rep)
    mine = h * n_rep + r
    wanted = (place + step_of(mine)) % peers
    out_block = sum(
        jnp.where(c_places[i] == wanted, c_blocks[i], 0) for i in range(group_count)
    )
    links = []
    for s in range(peers):
        for q in range(group_count):
            links.append((s * group_count + q, ((s + step_of(q)) % peers) * group_count + q))
    got = lax.ppermute(out_block, ("seq", "head", "rep"), links)
    ct_blocks, ct_places = features_here(got)
    ct = jnp.stack([block.T for block in ct_blocks])
    steps = step_of(ct_places)
    ct_at = jnp.sum(
        jnp.where(steps[None] == jnp.arange(peers)[:, None], jnp.arange(group_count)[None], 0), 1
    ).astype(jnp.int32)
    f_rows = min(256, part_cols)
    weight_grad = pl.pallas_call(
        functools.partial(weight_grad_kernel, peers),
        grid_spec=pltpu.PrefetchScalarGridSpec(
            num_scalar_prefetch=1,
            grid=(part_cols // f_rows,),
            in_specs=[pl.BlockSpec((group_count, f_rows, rows), lambda i, at: (0, i, 0))]
            + [whole((rows, columns))] * peers,
            out_specs=pl.BlockSpec((f_rows, columns), lambda i, at: (i, 0)),
        ),
        out_shape=jax.ShapeDtypeStruct((part_cols, columns), BF16),
        compiler_params=params(),
        cost_estimate=cost(
            2 * part_cols * columns * rows * peers, 2 * array_bytes * peers + 2 * part_cols * columns
        ),
        name="weight_grad",
    )(ct_at, ct, *mixed_all)
    return (attended, q_grad, k_grad, v_grad, weight_grad)


def solution(mesh):
    shared = P(("groups", "seq"), ("head", "rep"))
    return jax.shard_map(
        per_device,
        mesh=mesh,
        in_specs=(shared, shared, shared, P(None, ("head", "rep")), P(("groups", "seq"), None), shared),
        out_specs=(shared,) * 5,
        check_vma=False,
    )
```

```python
import functools
import math

import jax
import jax.numpy as jnp
from jax import lax
from jax.experimental import pallas as pl
from jax.experimental.pallas import tpu as pltpu
from jax.sharding import PartitionSpec as P

HEAD_DIM = 128
BLOCK = 128
LEVELS = 5
SCALE = HEAD_DIM ** (-0.5)
LOG2_SCALE = SCALE * math.log2(math.e)
MASKED = -1e30

F32 = jnp.float32
BF16 = jnp.bfloat16
NT = (((1,), (1,)), ((), ()))
TN = (((0,), (0,)), ((), ()))


def shift(value, by):
    peers = lax.axis_size("seq")
    return lax.ppermute(
        value, "seq", [(i, i + by) for i in range(peers) if 0 <= i + by < peers]
    )


def cyclic(value, by):
    peers = lax.axis_size("seq")
    return lax.ppermute(value, "seq", [(i, (i + by) % peers) for i in range(peers)])


def swap(value, axis):
    return lax.ppermute(value, axis, [(0, 1), (1, 0)])


def dot(a, b):
    return jnp.dot(a, b, preferred_element_type=F32)


def dot_nt(a, b):
    return lax.dot_general(a, b, NT, preferred_element_type=F32)


def dot_tn(a, b):
    return lax.dot_general(a, b, TN, preferred_element_type=F32)


def after(value, *others):
    return lax.optimization_barrier((value, others))[0]


def seen_tiles(blocks, peers):
    tiles = []
    for n in range(blocks):
        mine = [(0, n, None)]
        for level in range(LEVELS):
            target = n - 2**level
            distance = -(target // blocks)
            if distance < peers:
                mine.append((distance, target % blocks, level))
        tiles.append(mine)
    return tiles


def block_rows(n):
    return pl.ds(n * BLOCK, BLOCK)


def head_cols(j):
    return slice(j * HEAD_DIM, (j + 1) * HEAD_DIM)


def cat(parts, axis=0):
    return parts[0] if len(parts) == 1 else jnp.concatenate(parts, axis)


def causal_tile():
    rows = lax.broadcasted_iota(jnp.int32, (BLOCK, BLOCK), 0)
    cols = lax.broadcasted_iota(jnp.int32, (BLOCK, BLOCK), 1)
    return rows <= cols


def forward_kernel(tiles, count, heads, use_ref, q_ref, *refs):
    k_refs, v_refs = refs[:count], refs[count : 2 * count]
    mixed_ref, lse_ref = refs[2 * count :]
    causal = causal_tile()
    for n, mine in enumerate(tiles):
        rows = block_rows(n)
        for j in range(heads):
            cols = head_cols(j)
            keys = cat([k_refs[d][block_rows(b), cols] for d, b, _ in mine])
            vals = cat([v_refs[d][block_rows(b), cols] for d, b, _ in mine])
            raw = dot_nt(keys, q_ref[rows, cols])
            parts = []
            for i, (_, _, level) in enumerate(mine):
                part = raw[i * BLOCK : (i + 1) * BLOCK]
                if level is None:
                    part = jnp.where(causal, part, MASKED)
                else:
                    part = part + jnp.where(use_ref[n * LEVELS + level] == 1, 0.0, MASKED)
                parts.append(part)
            top = jnp.max(functools.reduce(jnp.maximum, parts), 0, keepdims=True) * LOG2_SCALE
            grown = [jnp.exp2(part * LOG2_SCALE - top) for part in parts]
            total = jnp.sum(functools.reduce(jnp.add, grown), 0, keepdims=True)
            share = 1.0 / total
            prob = cat([(part * share).astype(BF16) for part in grown])
            mixed_ref[rows, cols] = dot_tn(prob, vals).astype(BF16)
            lse_ref[j : j + 1, rows] = top + jnp.log2(total)


def query_kernel(tiles, count, heads, heads_up, use_ref, q_ref, g_ref, lse_ref, *refs):
    k_refs, v_refs = refs[:count], refs[count : 2 * count]
    dq_ref, stats_ref = refs[2 * count :]
    causal = causal_tile()
    for n, mine in enumerate(tiles):
        rows = block_rows(n)
        for j in range(heads):
            cols = head_cols(j)
            keys = cat([k_refs[d][block_rows(b), cols] for d, b, _ in mine])
            vals = cat([v_refs[d][block_rows(b), cols] for d, b, _ in mine])
            lse = lse_ref[j : j + 1, rows]
            raw = dot_nt(keys, q_ref[rows, cols])
            prob_grad = dot_nt(vals, g_ref[rows, cols])
            probs, weighted = [], None
            for i, (_, _, level) in enumerate(mine):
                here = slice(i * BLOCK, (i + 1) * BLOCK)
                if level is None:
                    logits = jnp.where(causal, raw[here] * LOG2_SCALE - lse, MASKED)
                else:
                    off = lse + jnp.where(use_ref[n * LEVELS + level] == 1, 0.0, -MASKED)
                    logits = raw[here] * LOG2_SCALE - off
                prob = jnp.exp2(logits)
                probs.append(prob)
                part = prob * prob_grad[here]
                weighted = part if weighted is None else weighted + part
            delta = jnp.sum(weighted, 0, keepdims=True)
            score_grad = [
                (prob * SCALE * (prob_grad[i * BLOCK : (i + 1) * BLOCK] - delta)).astype(BF16)
                for i, prob in enumerate(probs)
            ]
            dq_ref[rows, cols] = dot_tn(cat(score_grad), keys).astype(BF16)
            stats_ref[j : j + 1, rows] = lse
            stats_ref[heads_up + j : heads_up + j + 1, rows] = delta
        flags = jnp.zeros((8, BLOCK), F32)
        level_row = lax.broadcasted_iota(jnp.int32, (8, BLOCK), 0)
        for level in range(LEVELS):
            flag = jnp.where(use_ref[n * LEVELS + level] == 1, 1.0, 0.0)
            flags = jnp.where(level_row == level, flag, flags)
        stats_ref[2 * heads_up :, rows] = flags
    for row in range(heads, heads_up):
        for first in (0, heads_up):
            stats_ref[first + row : first + row + 1, :] = jnp.zeros((1, stats_ref.shape[1]), F32)


def key_kernel(tiles, count, heads, heads_up, k_ref, v_ref, *refs):
    q_refs, g_refs, s_refs = refs[:count], refs[count : 2 * count], refs[2 * count : 3 * count]
    dk_ref, dv_ref = refs[3 * count :]
    causal = causal_tile()
    for b in range(len(tiles)):
        rows = block_rows(b)
        seers = [
            (d, n, level)
            for n, mine in enumerate(tiles)
            for d, block, level in mine
            if block == b
        ]
        for j in range(heads):
            cols = head_cols(j)
            ques = cat([q_refs[d][block_rows(n), cols] for d, n, _ in seers])
            grads = cat([g_refs[d][block_rows(n), cols] for d, n, _ in seers])
            raw = dot_nt(k_ref[rows, cols], ques)
            prob_grad = dot_nt(v_ref[rows, cols], grads)
            probs, score_grads = [], []
            for i, (d, n, level) in enumerate(seers):
                here = slice(i * BLOCK, (i + 1) * BLOCK)
                lse = s_refs[d][j : j + 1, block_rows(n)]
                delta = s_refs[d][heads_up + j : heads_up + j + 1, block_rows(n)]
                if level is None:
                    logits = jnp.where(causal, raw[:, here] * LOG2_SCALE - lse, MASKED)
                else:
                    row = 2 * heads_up + level
                    off = lse + (1.0 - s_refs[d][row : row + 1, block_rows(n)]) * (-MASKED)
                    logits = raw[:, here] * LOG2_SCALE - off
                prob = jnp.exp2(logits)
                probs.append(prob.astype(BF16))
                score_grads.append((prob * SCALE * (prob_grad[:, here] - delta)).astype(BF16))
            dv_ref[rows, cols] = dot(cat(probs, 1), grads).astype(BF16)
            dk_ref[rows, cols] = dot(cat(score_grads, 1), ques).astype(BF16)


def mixed_grad_kernel(count, place_ref, *refs):
    c_refs, w_ref, out_ref = refs[:count], refs[count], refs[count + 1]
    depth = c_refs[0].shape[1]
    columns = out_ref.shape[1]
    width = min(512, columns)
    for first in range(0, columns, width):
        total = None
        for i in range(count):
            rows = pl.ds(pl.multiple_of(place_ref[i] * depth, depth), depth)
            part = dot(c_refs[i][...], w_ref[rows, first : first + width])
            total = part if total is None else total + part
        out_ref[:, first : first + width] = total.astype(BF16)


def partial_kernel(place_ref, m_ref, w_ref, keep_ref, give_ref):
    depth = keep_ref.shape[2]
    half = depth // 2
    for out_ref, base in ((give_ref, 2), (keep_ref, 0)):
        for i in range(2):
            for part in range(2):
                first = pl.multiple_of(place_ref[base + i] * depth + part * half, half)
                out_ref[i, :, part * half : (part + 1) * half] = dot_nt(
                    m_ref[...], w_ref[pl.ds(first, half), :]
                ).astype(BF16)


def weight_grad_kernel(count, place_ref, c_ref, *refs):
    m_refs, out_ref = refs[:count], refs[count]
    features = out_ref.shape[0]
    height = min(512, features)
    for first in range(0, features, height):
        total = None
        for p in range(count):
            part = dot_tn(c_ref[place_ref[p], :, first : first + height], m_refs[p][...])
            total = part if total is None else total + part
        out_ref[first : first + height, :] = total.astype(BF16)


def cost(flops, bytes_accessed, exps=0):
    return pl.CostEstimate(
        flops=int(flops), bytes_accessed=int(bytes_accessed), transcendentals=int(exps)
    )


def kernel_call(body, name, scalars, arrays, out_shape, estimate):
    smem = pl.BlockSpec(memory_space=pltpu.SMEM)
    vmem = pl.BlockSpec(memory_space=pltpu.VMEM)
    return pl.pallas_call(
        body,
        in_specs=[smem] * len(scalars) + [vmem] * len(arrays),
        out_specs=jax.tree.map(lambda _: vmem, out_shape),
        out_shape=out_shape,
        compiler_params=pltpu.CompilerParams(vmem_limit_bytes=VMEM_LIMIT),
        cost_estimate=estimate,
        name=name,
    )(*scalars, *arrays)


VMEM_LIMIT = 16 * 1024 * 1024


def features_here(value):
    heads, reps = lax.axis_size("head"), lax.axis_size("rep")
    if heads == 2 and reps == 2:
        h, r = lax.axis_index("head"), lax.axis_index("rep")
        across = swap(value, "head")
        blocks = [value, swap(value, "rep"), across, swap(across, "rep")]
        places = [2 * h + r, 2 * h + 1 - r, 2 * (1 - h) + r, 2 * (1 - h) + 1 - r]
        return blocks, jnp.stack(places).astype(jnp.int32)
    gathered = lax.all_gather(value, ("head", "rep"), axis=0)
    count = heads * reps
    return [gathered[i] for i in range(count)], jnp.arange(count, dtype=jnp.int32)


def attended_share(mixed_heads, out_weight, places, estimate):
    heads, reps = lax.axis_size("head"), lax.axis_size("rep")
    rows = mixed_heads.shape[0]
    if heads == 2 and reps == 2:
        share = out_weight.shape[0] // 4
        order = jnp.stack([places[0], places[2], places[1], places[3]])
        keep, give = kernel_call(
            partial_kernel,
            "attended_partial",
            [order],
            [mixed_heads, out_weight],
            [jax.ShapeDtypeStruct((2, rows, share), BF16)] * 2,
            estimate,
        )
        got = swap(give, "rep")
        across = (keep[1].astype(F32) + got[1].astype(F32)).astype(BF16)
        across = swap(across, "head")
        return (keep[0].astype(F32) + got[0].astype(F32) + across.astype(F32)).astype(BF16)
    partial_value = lax.dot_general(mixed_heads, out_weight, NT, preferred_element_type=F32)
    return lax.psum_scatter(
        partial_value.astype(BF16), ("head", "rep"), scatter_dimension=1, tiled=True
    )


def per_device(queries, keys, values, out_weight, level_mask, cotangent):
    rows, columns = queries.shape
    features = out_weight.shape[0]
    heads = columns // HEAD_DIM
    heads_up = -(-heads // 8) * 8
    blocks = rows // BLOCK
    peers = lax.axis_size("seq")
    place = lax.axis_index("seq")
    tiles = seen_tiles(blocks, peers)
    distances = sorted({d for mine in tiles for d, _, _ in mine})
    count = len(distances)
    slot = {d: i for i, d in enumerate(distances)}
    tiles = [[(slot[d], b, level) for d, b, level in mine] for mine in tiles]
    pairs = sum(len(mine) for mine in tiles)
    attention_flops = 2 * heads * pairs * BLOCK * BLOCK * HEAD_DIM
    array_bytes = 2 * rows * columns
    exps = heads * pairs * BLOCK * BLOCK
    like_queries = jax.ShapeDtypeStruct((rows, columns), BF16)

    def further(got, sign, *others):
        near, far = distances[len(got) - 1], distances[len(got)]
        return got + [shift(after(got[-1], *others), sign * (far - near))]

    block_ids = place * blocks + jnp.arange(blocks, dtype=jnp.int32)
    offsets = 2 ** jnp.arange(LEVELS, dtype=jnp.int32)
    use = ((block_ids[:, None] >= offsets[None]) & (level_mask == 1)).astype(jnp.int32)
    use = use.reshape(-1)

    key_all, value_all, query_all = [keys], [values], [queries]
    key_all = further(key_all, 1)
    value_all = further(value_all, 1)
    query_all = further(query_all, -1)
    c_blocks, c_places = features_here(cotangent)
    group_count = len(c_blocks)
    part_cols = cotangent.shape[1]
    key_all = further(key_all, 1)
    value_all = further(value_all, 1, query_all[1])
    query_all = further(query_all, -1)

    mixed_grad = kernel_call(
        functools.partial(mixed_grad_kernel, group_count),
        "mixed_grad",
        [c_places],
        [*c_blocks, out_weight],
        like_queries,
        cost(2 * rows * columns * features, 2 * columns * features),
    )
    grad_all = further([mixed_grad], -1)

    h, r = lax.axis_index("head"), lax.axis_index("rep")
    n_head, n_rep = lax.axis_size("head"), lax.axis_size("rep")
    step_of = lambda i: (i // n_rep) + n_head * (i % n_rep)
    wanted = (place + step_of(h * n_rep + r)) % peers
    out_block = c_blocks[0]
    for i in range(1, group_count):
        out_block = jnp.where(c_places[i] == wanted, c_blocks[i], out_block)
    links = []
    for s in range(peers):
        for q in range(group_count):
            links.append((s * group_count + q, ((s + step_of(q)) % peers) * group_count + q))
    arrived = lax.ppermute(out_block, ("seq", "head", "rep"), links)

    while len(key_all) < count:
        key_all = further(key_all, 1)
        value_all = further(value_all, 1)
        query_all = further(query_all, -1)
    held_queries = after(queries, query_all[-1], grad_all[1], arrived)
    mixed_heads, lse = kernel_call(
        functools.partial(forward_kernel, tiles, count, heads),
        "attention_forward",
        [use],
        [held_queries, *key_all, *value_all],
        [like_queries, jax.ShapeDtypeStruct((heads_up, rows), F32)],
        cost(2 * attention_flops, (2 * count + 2) * array_bytes, exps),
    )
    while len(grad_all) < count:
        grad_all = further(grad_all, -1)

    if peers <= 4:
        mixed_all = [mixed_heads] + [cyclic(mixed_heads, k) for k in range(1, peers)]
    else:
        gathered = lax.all_gather(mixed_heads, "seq", axis=0)
        mixed_all = [
            lax.dynamic_index_in_dim(gathered, (place - k) % peers, 0, False)
            for k in range(peers)
        ]

    attended = attended_share(
        mixed_heads, out_weight, c_places, cost(2 * rows * columns * features, 2 * rows * features)
    )

    stats_shape = jax.ShapeDtypeStruct((2 * heads_up + 8, rows), F32)
    q_grad, stats = kernel_call(
        functools.partial(query_kernel, tiles, count, heads, heads_up),
        "attention_query_grad",
        [use],
        [queries, mixed_grad, lse, *key_all, *value_all],
        [like_queries, stats_shape],
        cost(3 * attention_flops, (2 * count + 3) * array_bytes, exps),
    )
    stats_all = [stats] + [shift(stats, -d) for d in distances[1:]]
    k_grad, v_grad = kernel_call(
        functools.partial(key_kernel, tiles, count, heads, heads_up),
        "attention_key_grad",
        [],
        [keys, values, *query_all, *grad_all, *stats_all],
        [like_queries] * 2,
        cost(4 * attention_flops, (2 * count + 4) * array_bytes, exps),
    )

    ct_blocks, ct_places = features_here(arrived)
    steps = step_of(ct_places)
    ct_at = jnp.sum(
        jnp.where(steps[None] == jnp.arange(peers)[:, None], jnp.arange(group_count)[None], 0), 1
    ).astype(jnp.int32)
    weight_grad = kernel_call(
        functools.partial(weight_grad_kernel, peers),
        "weight_grad",
        [ct_at],
        [jnp.stack(ct_blocks), *mixed_all],
        jax.ShapeDtypeStruct((part_cols, columns), BF16),
        cost(2 * part_cols * columns * rows * peers, 2 * array_bytes * peers),
    )
    return (attended, q_grad, k_grad, v_grad, weight_grad)


def solution(mesh):
    shared = P(("groups", "seq"), ("head", "rep"))
    return jax.shard_map(
        per_device,
        mesh=mesh,
        in_specs=(shared, shared, shared, P(None, ("head", "rep")), P(("groups", "seq"), None), shared),
        out_specs=(shared,) * 5,
        check_vma=False,
    )
```

```python
import functools
import math

import jax
import jax.numpy as jnp
from jax import lax
from jax.experimental import pallas as pl
from jax.experimental.pallas import tpu as pltpu
from jax.sharding import PartitionSpec as P

HEAD_DIM = 128
BLOCK = 128
LEVELS = 5
SCALE = HEAD_DIM ** (-0.5)
LOG2_SCALE = SCALE * math.log2(math.e)
MASKED = -1e30

F32 = jnp.float32
BF16 = jnp.bfloat16
NT = (((1,), (1,)), ((), ()))
TN = (((0,), (0,)), ((), ()))


def shift(value, by):
    peers = lax.axis_size("seq")
    return lax.ppermute(
        value, "seq", [(i, i + by) for i in range(peers) if 0 <= i + by < peers]
    )


def cyclic(value, by):
    peers = lax.axis_size("seq")
    return lax.ppermute(value, "seq", [(i, (i + by) % peers) for i in range(peers)])


def swap(value, axis):
    return lax.ppermute(value, axis, [(0, 1), (1, 0)])


def dot(a, b):
    return jnp.dot(a, b, preferred_element_type=F32)


def dot_nt(a, b):
    return lax.dot_general(a, b, NT, preferred_element_type=F32)


def dot_tn(a, b):
    return lax.dot_general(a, b, TN, preferred_element_type=F32)


def after(value, *others):
    return lax.optimization_barrier((value, others))[0]


def seen_tiles(blocks, peers):
    tiles = []
    for n in range(blocks):
        mine = [(0, n, None)]
        for level in range(LEVELS):
            target = n - 2**level
            distance = -(target // blocks)
            if distance < peers:
                mine.append((distance, target % blocks, level))
        tiles.append(mine)
    return tiles


def block_rows(n):
    return pl.ds(n * BLOCK, BLOCK)


def head_cols(j):
    return slice(j * HEAD_DIM, (j + 1) * HEAD_DIM)


def cat(parts, axis=0):
    return parts[0] if len(parts) == 1 else jnp.concatenate(parts, axis)


def causal_tile():
    rows = lax.broadcasted_iota(jnp.int32, (BLOCK, BLOCK), 0)
    cols = lax.broadcasted_iota(jnp.int32, (BLOCK, BLOCK), 1)
    return rows <= cols


def forward_kernel(tiles, count, heads, use_ref, q_ref, *refs):
    k_refs, v_refs = refs[:count], refs[count : 2 * count]
    mixed_ref, lse_ref = refs[2 * count :]
    causal = causal_tile()
    for n, mine in enumerate(tiles):
        rows = block_rows(n)
        for j in range(heads):
            cols = head_cols(j)
            keys = cat([k_refs[d][block_rows(b), cols] for d, b, _ in mine])
            vals = cat([v_refs[d][block_rows(b), cols] for d, b, _ in mine])
            raw = dot_nt(keys, q_ref[rows, cols])
            parts = []
            for i, (_, _, level) in enumerate(mine):
                part = raw[i * BLOCK : (i + 1) * BLOCK]
                if level is None:
                    part = jnp.where(causal, part, MASKED)
                else:
                    part = part + jnp.where(use_ref[n * LEVELS + level] == 1, 0.0, MASKED)
                parts.append(part)
            top = jnp.max(functools.reduce(jnp.maximum, parts), 0, keepdims=True) * LOG2_SCALE
            grown = [jnp.exp2(part * LOG2_SCALE - top) for part in parts]
            total = jnp.sum(functools.reduce(jnp.add, grown), 0, keepdims=True)
            share = 1.0 / total
            prob = cat([(part * share).astype(BF16) for part in grown])
            mixed_ref[rows, cols] = dot_tn(prob, vals).astype(BF16)
            lse_ref[j : j + 1, rows] = top + jnp.log2(total)


def query_kernel(tiles, count, heads, heads_up, use_ref, q_ref, g_ref, lse_ref, *refs):
    k_refs, v_refs = refs[:count], refs[count : 2 * count]
    dq_ref, stats_ref = refs[2 * count :]
    causal = causal_tile()
    for n, mine in enumerate(tiles):
        rows = block_rows(n)
        for j in range(heads):
            cols = head_cols(j)
            keys = cat([k_refs[d][block_rows(b), cols] for d, b, _ in mine])
            vals = cat([v_refs[d][block_rows(b), cols] for d, b, _ in mine])
            lse = lse_ref[j : j + 1, rows]
            raw = dot_nt(keys, q_ref[rows, cols])
            prob_grad = dot_nt(vals, g_ref[rows, cols])
            probs, weighted = [], None
            for i, (_, _, level) in enumerate(mine):
                here = slice(i * BLOCK, (i + 1) * BLOCK)
                if level is None:
                    logits = jnp.where(causal, raw[here] * LOG2_SCALE - lse, MASKED)
                else:
                    off = lse + jnp.where(use_ref[n * LEVELS + level] == 1, 0.0, -MASKED)
                    logits = raw[here] * LOG2_SCALE - off
                prob = jnp.exp2(logits)
                probs.append(prob)
                part = prob * prob_grad[here]
                weighted = part if weighted is None else weighted + part
            delta = jnp.sum(weighted, 0, keepdims=True)
            score_grad = [
                (prob * SCALE * (prob_grad[i * BLOCK : (i + 1) * BLOCK] - delta)).astype(BF16)
                for i, prob in enumerate(probs)
            ]
            dq_ref[rows, cols] = dot_tn(cat(score_grad), keys).astype(BF16)
            stats_ref[j : j + 1, rows] = lse
            stats_ref[heads_up + j : heads_up + j + 1, rows] = delta
        flags = jnp.zeros((8, BLOCK), F32)
        level_row = lax.broadcasted_iota(jnp.int32, (8, BLOCK), 0)
        for level in range(LEVELS):
            flag = jnp.where(use_ref[n * LEVELS + level] == 1, 1.0, 0.0)
            flags = jnp.where(level_row == level, flag, flags)
        stats_ref[2 * heads_up :, rows] = flags
    for row in range(heads, heads_up):
        for first in (0, heads_up):
            stats_ref[first + row : first + row + 1, :] = jnp.zeros((1, stats_ref.shape[1]), F32)


def key_kernel(tiles, count, heads, heads_up, k_ref, v_ref, *refs):
    q_refs, g_refs, s_refs = refs[:count], refs[count : 2 * count], refs[2 * count : 3 * count]
    dk_ref, dv_ref = refs[3 * count :]
    causal = causal_tile()
    for b in range(len(tiles)):
        rows = block_rows(b)
        seers = [
            (d, n, level)
            for n, mine in enumerate(tiles)
            for d, block, level in mine
            if block == b
        ]
        for j in range(heads):
            cols = head_cols(j)
            ques = cat([q_refs[d][block_rows(n), cols] for d, n, _ in seers])
            grads = cat([g_refs[d][block_rows(n), cols] for d, n, _ in seers])
            raw = dot_nt(k_ref[rows, cols], ques)
            prob_grad = dot_nt(v_ref[rows, cols], grads)
            probs, score_grads = [], []
            for i, (d, n, level) in enumerate(seers):
                here = slice(i * BLOCK, (i + 1) * BLOCK)
                lse = s_refs[d][j : j + 1, block_rows(n)]
                delta = s_refs[d][heads_up + j : heads_up + j + 1, block_rows(n)]
                if level is None:
                    logits = jnp.where(causal, raw[:, here] * LOG2_SCALE - lse, MASKED)
                else:
                    row = 2 * heads_up + level
                    off = lse + (1.0 - s_refs[d][row : row + 1, block_rows(n)]) * (-MASKED)
                    logits = raw[:, here] * LOG2_SCALE - off
                prob = jnp.exp2(logits)
                probs.append(prob.astype(BF16))
                score_grads.append((prob * SCALE * (prob_grad[:, here] - delta)).astype(BF16))
            dv_ref[rows, cols] = dot(cat(probs, 1), grads).astype(BF16)
            dk_ref[rows, cols] = dot(cat(score_grads, 1), ques).astype(BF16)


def mixed_grad_kernel(count, place_ref, *refs):
    c_refs, w_ref, out_ref, held, sems = refs[:count], refs[count], *refs[count + 1 :]
    depth = c_refs[0].shape[1]
    copies = []
    for i in range(count):
        rows = pl.ds(pl.multiple_of(place_ref[i] * depth, depth), depth)
        copies.append(pltpu.make_async_copy(w_ref.at[rows, :], held.at[i], sems.at[i]))
    for copy in copies:
        copy.start()
    total = None
    for i, copy in enumerate(copies):
        copy.wait()
        part = dot(c_refs[i][...], held[i])
        total = part if total is None else total + part
    out_ref[...] = total.astype(BF16)


def partial_kernel(place_ref, m_ref, w_ref, keep_ref, give_ref, held, sems):
    depth = keep_ref.shape[2]
    copies = []
    for i in range(4):
        rows = pl.ds(pl.multiple_of(place_ref[i] * depth, depth), depth)
        copies.append(pltpu.make_async_copy(w_ref.at[rows, :], held.at[i], sems.at[i]))
    for copy in copies:
        copy.start()
    outs = [(give_ref, 0), (give_ref, 1), (keep_ref, 0), (keep_ref, 1)]
    for i, copy in enumerate(copies):
        copy.wait()
        out_ref, at = outs[i]
        out_ref[at] = dot_nt(m_ref[...], held[i]).astype(BF16)


def weight_grad_kernel(count, place_ref, c_ref, *refs):
    m_refs, out_ref = refs[:count], refs[count]
    features = out_ref.shape[0]
    height = min(512, features)
    for first in range(0, features, height):
        total = None
        for p in range(count):
            part = dot_tn(c_ref[place_ref[p], :, first : first + height], m_refs[p][...])
            total = part if total is None else total + part
        out_ref[first : first + height, :] = total.astype(BF16)


def cost(flops, bytes_accessed, exps=0):
    return pl.CostEstimate(
        flops=int(flops * ORDER_WEIGHT),
        bytes_accessed=int(bytes_accessed * ORDER_WEIGHT),
        transcendentals=int(exps),
    )


def kernel_call(body, name, scalars, arrays, out_shape, estimate, outside=(), scratch=()):
    smem = pl.BlockSpec(memory_space=pltpu.SMEM)
    vmem = pl.BlockSpec(memory_space=pltpu.VMEM)
    return pl.pallas_call(
        body,
        in_specs=[smem] * len(scalars)
        + [vmem] * len(arrays)
        + [pl.BlockSpec(memory_space=pltpu.HBM)] * len(outside),
        out_specs=jax.tree.map(lambda _: vmem, out_shape),
        out_shape=out_shape,
        scratch_shapes=list(scratch),
        compiler_params=pltpu.CompilerParams(
            vmem_limit_bytes=STREAM_LIMIT if outside else VMEM_LIMIT
        ),
        cost_estimate=estimate,
        name=name,
    )(*scalars, *arrays, *outside)


def weight_scratch(count, depth, columns):
    return [pltpu.VMEM((count, depth, columns), BF16), pltpu.SemaphoreType.DMA((count,))]


VMEM_LIMIT = 20 * 1024 * 1024
ORDER_WEIGHT = 100
STREAM_LIMIT = 54 * 1024 * 1024


def features_here(value, *others, serial=False):
    heads, reps = lax.axis_size("head"), lax.axis_size("rep")
    if heads == 2 and reps == 2:
        h, r = lax.axis_index("head"), lax.axis_index("rep")
        across = swap(after(value, *others), "head")
        beside = swap(after(value, across) if serial else value, "rep")
        corner = swap(after(across, beside) if serial else across, "rep")
        blocks = [value, beside, across, corner]
        places = [2 * h + r, 2 * h + 1 - r, 2 * (1 - h) + r, 2 * (1 - h) + 1 - r]
        return blocks, jnp.stack(places).astype(jnp.int32)
    gathered = lax.all_gather(value, ("head", "rep"), axis=0)
    count = heads * reps
    return [gathered[i] for i in range(count)], jnp.arange(count, dtype=jnp.int32)


def attended_share(mixed_heads, out_weight, places, estimate, *others):
    heads, reps = lax.axis_size("head"), lax.axis_size("rep")
    rows = mixed_heads.shape[0]
    if heads == 2 and reps == 2:
        share = out_weight.shape[0] // 4
        order = jnp.stack([places[1], places[3], places[0], places[2]])
        keep, give = kernel_call(
            partial_kernel,
            "attended_partial",
            [order],
            [mixed_heads],
            [jax.ShapeDtypeStruct((2, rows, share), BF16)] * 2,
            estimate,
            [out_weight],
            weight_scratch(4, share, mixed_heads.shape[1]),
        )
        got = swap(after(give, *others), "rep")
        across = (keep[1].astype(F32) + got[1].astype(F32)).astype(BF16)
        across = swap(across, "head")
        return (keep[0].astype(F32) + got[0].astype(F32) + across.astype(F32)).astype(BF16)
    partial_value = lax.dot_general(mixed_heads, out_weight, NT, preferred_element_type=F32)
    return lax.psum_scatter(
        partial_value.astype(BF16), ("head", "rep"), scatter_dimension=1, tiled=True
    )


def per_device(queries, keys, values, out_weight, level_mask, cotangent):
    rows, columns = queries.shape
    features = out_weight.shape[0]
    heads = columns // HEAD_DIM
    heads_up = -(-heads // 8) * 8
    blocks = rows // BLOCK
    peers = lax.axis_size("seq")
    place = lax.axis_index("seq")
    tiles = seen_tiles(blocks, peers)
    distances = sorted({d for mine in tiles for d, _, _ in mine})
    count = len(distances)
    slot = {d: i for i, d in enumerate(distances)}
    tiles = [[(slot[d], b, level) for d, b, level in mine] for mine in tiles]
    pairs = sum(len(mine) for mine in tiles)
    attention_flops = 2 * heads * pairs * BLOCK * BLOCK * HEAD_DIM
    array_bytes = 2 * rows * columns
    exps = heads * pairs * BLOCK * BLOCK
    like_queries = jax.ShapeDtypeStruct((rows, columns), BF16)

    def further(got, sign, *others):
        near, far = distances[len(got) - 1], distances[len(got)]
        return got + [shift(after(got[-1], *others), sign * (far - near))]

    block_ids = place * blocks + jnp.arange(blocks, dtype=jnp.int32)
    offsets = 2 ** jnp.arange(LEVELS, dtype=jnp.int32)
    use = ((block_ids[:, None] >= offsets[None]) & (level_mask == 1)).astype(jnp.int32)
    use = use.reshape(-1)

    key_all, value_all, query_all = [keys], [values], [queries]
    key_all = further(key_all, 1)
    value_all = further(value_all, 1)
    query_all = further(query_all, -1)
    c_blocks, c_places = features_here(cotangent)
    group_count = len(c_blocks)
    part_cols = cotangent.shape[1]
    key_all = further(key_all, 1)
    value_all = further(value_all, 1, key_all[-1])
    query_all = further(query_all, -1)

    mixed_grad = kernel_call(
        functools.partial(mixed_grad_kernel, group_count),
        "mixed_grad",
        [c_places],
        c_blocks,
        like_queries,
        cost(2 * rows * columns * features, 2 * columns * features),
        [out_weight],
        weight_scratch(group_count, part_cols, columns),
    )
    grad_all = further([mixed_grad], -1)

    h, r = lax.axis_index("head"), lax.axis_index("rep")
    n_head, n_rep = lax.axis_size("head"), lax.axis_size("rep")
    step_of = lambda i: (i // n_rep) + n_head * (i % n_rep)
    wanted = (place + step_of(h * n_rep + r)) % peers
    out_block = c_blocks[0]
    for i in range(1, group_count):
        out_block = jnp.where(c_places[i] == wanted, c_blocks[i], out_block)
    links = []
    for s in range(peers):
        for q in range(group_count):
            links.append((s * group_count + q, ((s + step_of(q)) % peers) * group_count + q))
    arrived = lax.ppermute(out_block, ("seq", "head", "rep"), links)

    while len(key_all) < count:
        key_all = further(key_all, 1)
        value_all = further(value_all, 1, key_all[-1])
        query_all = further(query_all, -1)
    held_queries = after(queries, query_all[-1], grad_all[1], arrived)
    mixed_heads, lse = kernel_call(
        functools.partial(forward_kernel, tiles, count, heads),
        "attention_forward",
        [use],
        [held_queries, *key_all, *value_all],
        [like_queries, jax.ShapeDtypeStruct((heads_up, rows), F32)],
        cost(2 * attention_flops, (2 * count + 2) * array_bytes, exps),
    )
    while len(grad_all) < count:
        grad_all = further(grad_all, -1)

    if peers <= 4:
        mixed_all = [mixed_heads] + [cyclic(mixed_heads, k) for k in range(1, peers)]
    else:
        gathered = lax.all_gather(mixed_heads, "seq", axis=0)
        mixed_all = [
            lax.dynamic_index_in_dim(gathered, (place - k) % peers, 0, False)
            for k in range(peers)
        ]

    estimate = cost(2 * rows * columns * features, 2 * rows * features)
    attended = attended_share(mixed_heads, out_weight, c_places, estimate, grad_all[-1])
    ct_blocks, ct_places = features_here(arrived, mixed_heads, serial=True)

    stats_shape = jax.ShapeDtypeStruct((2 * heads_up + 8, rows), F32)
    q_grad, stats = kernel_call(
        functools.partial(query_kernel, tiles, count, heads, heads_up),
        "attention_query_grad",
        [use],
        [queries, mixed_grad, lse, *key_all, *value_all],
        [like_queries, stats_shape],
        cost(3 * attention_flops, (2 * count + 3) * array_bytes, exps),
    )
    stats_all = [after(stats, ct_blocks[-1])]
    while len(stats_all) < count:
        stats_all = further(stats_all, -1)
    k_grad, v_grad = kernel_call(
        functools.partial(key_kernel, tiles, count, heads, heads_up),
        "attention_key_grad",
        [],
        [keys, values, *query_all, *grad_all, *stats_all],
        [like_queries] * 2,
        cost(4 * attention_flops, (2 * count + 4) * array_bytes, exps),
    )

    steps = step_of(ct_places)
    ct_at = jnp.sum(
        jnp.where(steps[None] == jnp.arange(peers)[:, None], jnp.arange(group_count)[None], 0), 1
    ).astype(jnp.int32)
    weight_grad = kernel_call(
        functools.partial(weight_grad_kernel, peers),
        "weight_grad",
        [ct_at],
        [jnp.stack(ct_blocks), after(mixed_all[0], attended, k_grad), *mixed_all[1:]],
        jax.ShapeDtypeStruct((part_cols, columns), BF16),
        cost(2 * part_cols * columns * rows * peers, 2 * array_bytes * peers),
    )
    return (attended, q_grad, k_grad, v_grad, weight_grad)


def solution(mesh):
    shared = P(("groups", "seq"), ("head", "rep"))
    return jax.shard_map(
        per_device,
        mesh=mesh,
        in_specs=(shared, shared, shared, P(None, ("head", "rep")), P(("groups", "seq"), None), shared),
        out_specs=(shared,) * 5,
        check_vma=False,
    )
```

```python
import functools
import math

import jax
import jax.numpy as jnp
from jax import lax
from jax.experimental import pallas as pl
from jax.experimental.pallas import tpu as pltpu
from jax.sharding import PartitionSpec as P

HEAD_DIM = 128
BLOCK = 128
LEVELS = 5
SCALE = HEAD_DIM ** (-0.5)
LOG2_SCALE = SCALE * math.log2(math.e)
MASKED = -1e30

F32 = jnp.float32
BF16 = jnp.bfloat16
NT = (((1,), (1,)), ((), ()))
TN = (((0,), (0,)), ((), ()))


def shift(value, by):
    peers = lax.axis_size("seq")
    return lax.ppermute(
        value, "seq", [(i, i + by) for i in range(peers) if 0 <= i + by < peers]
    )


def cyclic(value, by):
    peers = lax.axis_size("seq")
    return lax.ppermute(value, "seq", [(i, (i + by) % peers) for i in range(peers)])


def swap(value, axis):
    return lax.ppermute(value, axis, [(0, 1), (1, 0)])


def dot(a, b):
    return jnp.dot(a, b, preferred_element_type=F32)


def dot_nt(a, b):
    return lax.dot_general(a, b, NT, preferred_element_type=F32)


def dot_tn(a, b):
    return lax.dot_general(a, b, TN, preferred_element_type=F32)


def after(value, *others):
    return lax.optimization_barrier((value, others))[0]


def seen_tiles(blocks, peers):
    tiles = []
    for n in range(blocks):
        mine = [(0, n, None)]
        for level in range(LEVELS):
            target = n - 2**level
            distance = -(target // blocks)
            if distance < peers:
                mine.append((distance, target % blocks, level))
        tiles.append(mine)
    return tiles


def block_rows(n):
    return pl.ds(n * BLOCK, BLOCK)


def head_cols(j):
    return slice(j * HEAD_DIM, (j + 1) * HEAD_DIM)


def cat(parts, axis=0):
    return parts[0] if len(parts) == 1 else jnp.concatenate(parts, axis)


def causal_tile():
    rows = lax.broadcasted_iota(jnp.int32, (BLOCK, BLOCK), 0)
    cols = lax.broadcasted_iota(jnp.int32, (BLOCK, BLOCK), 1)
    return rows <= cols


def forward_kernel(tiles, count, heads, use_ref, q_ref, *refs):
    k_refs, v_refs = refs[:count], refs[count : 2 * count]
    mixed_ref, lse_ref = refs[2 * count :]
    causal = causal_tile()
    for n, mine in enumerate(tiles):
        rows = block_rows(n)
        for j in range(heads):
            cols = head_cols(j)
            keys = cat([k_refs[d][block_rows(b), cols] for d, b, _ in mine])
            vals = cat([v_refs[d][block_rows(b), cols] for d, b, _ in mine])
            raw = dot_nt(keys, q_ref[rows, cols])
            parts = []
            for i, (_, _, level) in enumerate(mine):
                part = raw[i * BLOCK : (i + 1) * BLOCK]
                if level is None:
                    part = jnp.where(causal, part, MASKED)
                else:
                    part = part + jnp.where(use_ref[n * LEVELS + level] == 1, 0.0, MASKED)
                parts.append(part)
            top = jnp.max(functools.reduce(jnp.maximum, parts), 0, keepdims=True) * LOG2_SCALE
            grown = [jnp.exp2(part * LOG2_SCALE - top) for part in parts]
            total = jnp.sum(functools.reduce(jnp.add, grown), 0, keepdims=True)
            share = 1.0 / total
            prob = cat([(part * share).astype(BF16) for part in grown])
            mixed_ref[rows, cols] = dot_tn(prob, vals).astype(BF16)
            lse_ref[j : j + 1, rows] = top + jnp.log2(total)


def query_kernel(tiles, count, heads, heads_up, use_ref, q_ref, g_ref, lse_ref, *refs):
    k_refs, v_refs = refs[:count], refs[count : 2 * count]
    dq_ref, stats_ref = refs[2 * count :]
    causal = causal_tile()
    for n, mine in enumerate(tiles):
        rows = block_rows(n)
        for j in range(heads):
            cols = head_cols(j)
            keys = cat([k_refs[d][block_rows(b), cols] for d, b, _ in mine])
            vals = cat([v_refs[d][block_rows(b), cols] for d, b, _ in mine])
            lse = lse_ref[j : j + 1, rows]
            raw = dot_nt(keys, q_ref[rows, cols])
            prob_grad = dot_nt(vals, g_ref[rows, cols])
            probs, weighted = [], None
            for i, (_, _, level) in enumerate(mine):
                here = slice(i * BLOCK, (i + 1) * BLOCK)
                if level is None:
                    logits = jnp.where(causal, raw[here] * LOG2_SCALE - lse, MASKED)
                else:
                    off = lse + jnp.where(use_ref[n * LEVELS + level] == 1, 0.0, -MASKED)
                    logits = raw[here] * LOG2_SCALE - off
                prob = jnp.exp2(logits)
                probs.append(prob)
                part = prob * prob_grad[here]
                weighted = part if weighted is None else weighted + part
            delta = jnp.sum(weighted, 0, keepdims=True)
            score_grad = [
                (prob * SCALE * (prob_grad[i * BLOCK : (i + 1) * BLOCK] - delta)).astype(BF16)
                for i, prob in enumerate(probs)
            ]
            dq_ref[rows, cols] = dot_tn(cat(score_grad), keys).astype(BF16)
            stats_ref[j : j + 1, rows] = lse
            stats_ref[heads_up + j : heads_up + j + 1, rows] = delta
        flags = jnp.zeros((8, BLOCK), F32)
        level_row = lax.broadcasted_iota(jnp.int32, (8, BLOCK), 0)
        for level in range(LEVELS):
            flag = jnp.where(use_ref[n * LEVELS + level] == 1, 1.0, 0.0)
            flags = jnp.where(level_row == level, flag, flags)
        stats_ref[2 * heads_up :, rows] = flags
    for row in range(heads, heads_up):
        for first in (0, heads_up):
            stats_ref[first + row : first + row + 1, :] = jnp.zeros((1, stats_ref.shape[1]), F32)


def key_kernel(tiles, count, heads, heads_up, k_ref, v_ref, *refs):
    q_refs, g_refs, s_refs = refs[:count], refs[count : 2 * count], refs[2 * count : 3 * count]
    dk_ref, dv_ref = refs[3 * count :]
    causal = causal_tile()
    for b in range(len(tiles)):
        rows = block_rows(b)
        seers = [
            (d, n, level)
            for n, mine in enumerate(tiles)
            for d, block, level in mine
            if block == b
        ]
        for j in range(heads):
            cols = head_cols(j)
            ques = cat([q_refs[d][block_rows(n), cols] for d, n, _ in seers])
            grads = cat([g_refs[d][block_rows(n), cols] for d, n, _ in seers])
            raw = dot_nt(k_ref[rows, cols], ques)
            prob_grad = dot_nt(v_ref[rows, cols], grads)
            probs, score_grads = [], []
            for i, (d, n, level) in enumerate(seers):
                here = slice(i * BLOCK, (i + 1) * BLOCK)
                lse = s_refs[d][j : j + 1, block_rows(n)]
                delta = s_refs[d][heads_up + j : heads_up + j + 1, block_rows(n)]
                if level is None:
                    logits = jnp.where(causal, raw[:, here] * LOG2_SCALE - lse, MASKED)
                else:
                    row = 2 * heads_up + level
                    off = lse + (1.0 - s_refs[d][row : row + 1, block_rows(n)]) * (-MASKED)
                    logits = raw[:, here] * LOG2_SCALE - off
                prob = jnp.exp2(logits)
                probs.append(prob.astype(BF16))
                score_grads.append((prob * SCALE * (prob_grad[:, here] - delta)).astype(BF16))
            dv_ref[rows, cols] = dot(cat(probs, 1), grads).astype(BF16)
            dk_ref[rows, cols] = dot(cat(score_grads, 1), ques).astype(BF16)


class Stream:
    def __init__(self, w_ref, held, sems, firsts, height):
        self.held = held
        self.height = height
        self.copies = [
            pltpu.make_async_copy(
                w_ref.at[pl.ds(pl.multiple_of(first, height), height), :],
                held.at[i],
                sems.at[i],
            )
            for i, first in enumerate(firsts)
        ]
        for copy in self.copies[:2]:
            copy.start()

    def piece(self, i):
        self.copies[i].wait()
        if i + 2 < len(self.copies):
            self.copies[i + 2].start()
        return self.held[i]


def mixed_grad_kernel(count, split, place_ref, *refs):
    c_refs, w_ref, out_ref, held, sems = refs[:count], refs[count], *refs[count + 1 :]
    depth = c_refs[0].shape[1]
    height = depth // split
    firsts = [place_ref[i] * depth + part * height for i in range(count) for part in range(split)]
    stream = Stream(w_ref, held, sems, firsts, height)
    total = None
    for i in range(count):
        for part in range(split):
            piece = stream.piece(i * split + part)
            step = dot(c_refs[i][:, part * height : (part + 1) * height], piece)
            total = step if total is None else total + step
    out_ref[...] = total.astype(BF16)


def partial_kernel(split, place_ref, m_ref, w_ref, keep_ref, give_ref, held, sems):
    depth = keep_ref.shape[2]
    height = depth // split
    firsts = [place_ref[i] * depth + part * height for i in range(4) for part in range(split)]
    stream = Stream(w_ref, held, sems, firsts, height)
    outs = [(give_ref, 0), (give_ref, 1), (keep_ref, 0), (keep_ref, 1)]
    for i, (out_ref, at) in enumerate(outs):
        for part in range(split):
            piece = stream.piece(i * split + part)
            cols = slice(part * height, (part + 1) * height)
            out_ref[at, :, cols] = dot_nt(m_ref[...], piece).astype(BF16)


def weight_grad_kernel(count, place_ref, c_ref, *refs):
    m_refs, out_ref = refs[:count], refs[count]
    features = out_ref.shape[0]
    height = min(512, features)
    for first in range(0, features, height):
        total = None
        for p in range(count):
            part = dot_tn(c_ref[place_ref[p], :, first : first + height], m_refs[p][...])
            total = part if total is None else total + part
        out_ref[first : first + height, :] = total.astype(BF16)


def cost(flops, bytes_accessed, exps=0, weight=1.0):
    return pl.CostEstimate(
        flops=int(flops * weight),
        bytes_accessed=int(bytes_accessed * weight),
        transcendentals=int(exps * weight),
    )


def kernel_call(body, name, scalars, arrays, out_shape, estimate, outside=(), scratch=()):
    smem = pl.BlockSpec(memory_space=pltpu.SMEM)
    vmem = pl.BlockSpec(memory_space=pltpu.VMEM)
    return pl.pallas_call(
        body,
        in_specs=[smem] * len(scalars)
        + [vmem] * len(arrays)
        + [pl.BlockSpec(memory_space=pltpu.HBM)] * len(outside),
        out_specs=jax.tree.map(lambda _: vmem, out_shape),
        out_shape=out_shape,
        scratch_shapes=list(scratch),
        compiler_params=pltpu.CompilerParams(
            vmem_limit_bytes=STREAM_LIMIT if outside else VMEM_LIMIT
        ),
        cost_estimate=estimate,
        name=name,
    )(*scalars, *arrays, *outside)


def weight_scratch(count, depth, columns):
    return [pltpu.VMEM((count, depth, columns), BF16), pltpu.SemaphoreType.DMA((count,))]


VMEM_LIMIT = 20 * 1024 * 1024
WEIGHTS = dict(mixed_grad=100.0, forward=100.0, partial=0.0, query=100.0, key=0.0)
STREAM_LIMIT = 54 * 1024 * 1024


def features_here(value, *others, serial=False):
    heads, reps = lax.axis_size("head"), lax.axis_size("rep")
    if heads == 2 and reps == 2:
        h, r = lax.axis_index("head"), lax.axis_index("rep")
        across = swap(after(value, *others), "head")
        beside = swap(after(value, across) if serial else value, "rep")
        corner = swap(after(across, beside) if serial else across, "rep")
        blocks = [value, beside, across, corner]
        places = [2 * h + r, 2 * h + 1 - r, 2 * (1 - h) + r, 2 * (1 - h) + 1 - r]
        return blocks, jnp.stack(places).astype(jnp.int32)
    gathered = lax.all_gather(value, ("head", "rep"), axis=0)
    count = heads * reps
    return [gathered[i] for i in range(count)], jnp.arange(count, dtype=jnp.int32)


def attended_partial(mixed_heads, out_weight, places, estimate):
    heads, reps = lax.axis_size("head"), lax.axis_size("rep")
    if heads == 2 and reps == 2:
        rows = mixed_heads.shape[0]
        share = out_weight.shape[0] // 4
        order = jnp.stack([places[1], places[3], places[0], places[2]])
        return kernel_call(
            functools.partial(partial_kernel, 2),
            "attended_partial",
            [order],
            [mixed_heads],
            [jax.ShapeDtypeStruct((2, rows, share), BF16)] * 2,
            estimate,
            [out_weight],
            weight_scratch(8, share // 2, mixed_heads.shape[1]),
        )
    partial_value = lax.dot_general(mixed_heads, out_weight, NT, preferred_element_type=F32)
    return [partial_value.astype(BF16)]


def attended_share(partial_products, *others):
    if len(partial_products) == 1:
        return lax.psum_scatter(
            partial_products[0], ("head", "rep"), scatter_dimension=1, tiled=True
        )
    keep, give = partial_products
    got = swap(after(give, *others), "rep")
    across = (keep[1].astype(F32) + got[1].astype(F32)).astype(BF16)
    across = swap(across, "head")
    return (keep[0].astype(F32) + got[0].astype(F32) + across.astype(F32)).astype(BF16)


def per_device(queries, keys, values, out_weight, level_mask, cotangent):
    rows, columns = queries.shape
    features = out_weight.shape[0]
    heads = columns // HEAD_DIM
    heads_up = -(-heads // 8) * 8
    blocks = rows // BLOCK
    peers = lax.axis_size("seq")
    place = lax.axis_index("seq")
    tiles = seen_tiles(blocks, peers)
    distances = sorted({d for mine in tiles for d, _, _ in mine})
    count = len(distances)
    slot = {d: i for i, d in enumerate(distances)}
    tiles = [[(slot[d], b, level) for d, b, level in mine] for mine in tiles]
    pairs = sum(len(mine) for mine in tiles)
    attention_flops = 2 * heads * pairs * BLOCK * BLOCK * HEAD_DIM
    array_bytes = 2 * rows * columns
    exps = heads * pairs * BLOCK * BLOCK
    like_queries = jax.ShapeDtypeStruct((rows, columns), BF16)

    def further(got, sign, *others):
        near, far = distances[len(got) - 1], distances[len(got)]
        return got + [shift(after(got[-1], *others), sign * (far - near))]

    block_ids = place * blocks + jnp.arange(blocks, dtype=jnp.int32)
    offsets = 2 ** jnp.arange(LEVELS, dtype=jnp.int32)
    use = ((block_ids[:, None] >= offsets[None]) & (level_mask == 1)).astype(jnp.int32)
    use = use.reshape(-1)

    key_all = further([keys], 1)
    value_all = further([values], 1)
    query_all = further([queries], -1)
    first_ones = (key_all[-1], value_all[-1], query_all[-1])
    c_blocks, c_places = features_here(cotangent)
    group_count = len(c_blocks)
    part_cols = cotangent.shape[1]
    while len(query_all) < count:
        query_all = further(query_all, -1)
    mixed_grad = kernel_call(
        functools.partial(mixed_grad_kernel, group_count, 2),
        "mixed_grad",
        [c_places],
        c_blocks,
        like_queries,
        cost(2 * rows * columns * features, 2 * columns * features, 0, WEIGHTS["mixed_grad"]),
        [out_weight],
        weight_scratch(2 * group_count, part_cols // 2, columns),
    )
    key_all = further(key_all, 1, *first_ones)
    grad_all = further([mixed_grad], -1, query_all[-1])
    while len(key_all) < count:
        key_all = further(key_all, 1)
    relayed = (key_all[-1], grad_all[-1])
    while len(value_all) < count:
        value_all = further(value_all, 1, *relayed)
    while len(grad_all) < count:
        grad_all = further(grad_all, -1, *relayed)

    h, r = lax.axis_index("head"), lax.axis_index("rep")
    n_head, n_rep = lax.axis_size("head"), lax.axis_size("rep")
    step_of = lambda i: (i // n_rep) + n_head * (i % n_rep)
    wanted = (place + step_of(h * n_rep + r)) % peers
    out_block = c_blocks[0]
    for i in range(1, group_count):
        out_block = jnp.where(c_places[i] == wanted, c_blocks[i], out_block)
    links = []
    for s in range(peers):
        for q in range(group_count):
            links.append((s * group_count + q, ((s + step_of(q)) % peers) * group_count + q))
    arrived = lax.ppermute(after(out_block, *relayed), ("seq", "head", "rep"), links)

    mixed_heads, lse = kernel_call(
        functools.partial(forward_kernel, tiles, count, heads),
        "attention_forward",
        [use],
        [after(queries, query_all[-1]), *key_all, *value_all],
        [like_queries, jax.ShapeDtypeStruct((heads_up, rows), F32)],
        cost(2 * attention_flops, (2 * count + 2) * array_bytes, exps, WEIGHTS["forward"]),
    )
    mixed_heads = after(mixed_heads, arrived, grad_all[-1])

    near = {}
    if peers <= 4:
        near = {k: cyclic(mixed_heads, k) for k in sorted({1, peers - 1}) if 0 < k < peers}
    stats_shape = jax.ShapeDtypeStruct((2 * heads_up + 8, rows), F32)
    q_grad, stats = kernel_call(
        functools.partial(query_kernel, tiles, count, heads, heads_up),
        "attention_query_grad",
        [use],
        [after(queries, mixed_heads), mixed_grad, lse, *key_all, *value_all],
        [like_queries, stats_shape],
        cost(3 * attention_flops, (2 * count + 3) * array_bytes, exps, WEIGHTS["query"]),
    )
    stats_all = [stats] + [shift(stats, -d) for d in distances[1:]]
    partial_products = attended_partial(
        mixed_heads, out_weight, c_places, cost(2 * rows * columns * features, 2 * rows * features, 0, WEIGHTS["partial"])
    )
    ct_across = swap(after(arrived, mixed_heads), "head") if n_head == 2 and n_rep == 2 else arrived
    held = after(mixed_heads, ct_across, *near.values(), *stats_all[1:], *partial_products)
    if peers <= 4:
        mixed_all = [mixed_heads] + [
            near[k] if k in near else cyclic(held, k) for k in range(1, peers)
        ]
    else:
        gathered = lax.all_gather(mixed_heads, "seq", axis=0)
        mixed_all = [
            lax.dynamic_index_in_dim(gathered, (place - k) % peers, 0, False)
            for k in range(peers)
        ]
    attended = attended_share(partial_products, held)
    if n_head == 2 and n_rep == 2:
        ct_blocks = [arrived, swap(after(arrived, held), "rep"), ct_across, swap(after(ct_across, held), "rep")]
        ct_places = c_places
    else:
        ct_blocks, ct_places = features_here(arrived)
    ct = jnp.stack(ct_blocks)
    k_grad, v_grad = kernel_call(
        functools.partial(key_kernel, tiles, count, heads, heads_up),
        "attention_key_grad",
        [],
        [after(keys, held), values, *query_all, *grad_all, *stats_all],
        [like_queries] * 2,
        cost(4 * attention_flops, (2 * count + 4) * array_bytes, exps, WEIGHTS["key"]),
    )

    steps = step_of(ct_places)
    ct_at = jnp.sum(
        jnp.where(steps[None] == jnp.arange(peers)[:, None], jnp.arange(group_count)[None], 0), 1
    ).astype(jnp.int32)
    weight_grad = kernel_call(
        functools.partial(weight_grad_kernel, peers),
        "weight_grad",
        [ct_at],
        [ct, after(mixed_all[0], attended, k_grad), *mixed_all[1:]],
        jax.ShapeDtypeStruct((part_cols, columns), BF16),
        cost(2 * part_cols * columns * rows * peers, 2 * array_bytes * peers),
    )
    return (attended, q_grad, k_grad, v_grad, weight_grad)


def solution(mesh):
    shared = P(("groups", "seq"), ("head", "rep"))
    return jax.shard_map(
        per_device,
        mesh=mesh,
        in_specs=(shared, shared, shared, P(None, ("head", "rep")), P(("groups", "seq"), None), shared),
        out_specs=(shared,) * 5,
        check_vma=False,
    )
```

```python
import functools
import math

import jax
import jax.numpy as jnp
from jax import lax
from jax.experimental import pallas as pl
from jax.experimental.pallas import tpu as pltpu
from jax.sharding import PartitionSpec as P

HEAD_DIM = 128
BLOCK = 128
LEVELS = 5
SCALE = HEAD_DIM ** (-0.5)
LOG2_SCALE = SCALE * math.log2(math.e)
MASKED = -1e30

F32 = jnp.float32
BF16 = jnp.bfloat16
NT = (((1,), (1,)), ((), ()))
TN = (((0,), (0,)), ((), ()))


def shift(value, by):
    peers = lax.axis_size("seq")
    return lax.ppermute(
        value, "seq", [(i, i + by) for i in range(peers) if 0 <= i + by < peers]
    )


def cyclic(value, by):
    peers = lax.axis_size("seq")
    return lax.ppermute(value, "seq", [(i, (i + by) % peers) for i in range(peers)])


def swap(value, axis):
    return lax.ppermute(value, axis, [(0, 1), (1, 0)])


def dot(a, b):
    return jnp.dot(a, b, preferred_element_type=F32)


def dot_nt(a, b):
    return lax.dot_general(a, b, NT, preferred_element_type=F32)


def dot_tn(a, b):
    return lax.dot_general(a, b, TN, preferred_element_type=F32)


def after(value, *others):
    return lax.optimization_barrier((value, others))[0]


def seen_tiles(blocks, peers):
    tiles = []
    for n in range(blocks):
        mine = [(0, n, None)]
        for level in range(LEVELS):
            target = n - 2**level
            distance = -(target // blocks)
            if distance < peers:
                mine.append((distance, target % blocks, level))
        tiles.append(mine)
    return tiles


def block_rows(n):
    return pl.ds(n * BLOCK, BLOCK)


def head_cols(j):
    return slice(j * HEAD_DIM, (j + 1) * HEAD_DIM)


def cat(parts, axis=0):
    return parts[0] if len(parts) == 1 else jnp.concatenate(parts, axis)


def causal_tile():
    rows = lax.broadcasted_iota(jnp.int32, (BLOCK, BLOCK), 0)
    cols = lax.broadcasted_iota(jnp.int32, (BLOCK, BLOCK), 1)
    return rows <= cols


def forward_kernel(tiles, count, heads, use_ref, q_ref, *refs):
    kv_refs = refs[:count]
    mixed_ref, lse_ref = refs[count:]
    blocks = len(tiles)
    causal = causal_tile()
    for n, mine in enumerate(tiles):
        rows = block_rows(n)
        for j in range(heads):
            cols = head_cols(j)
            keys = cat([kv_refs[d][block_rows(b), cols] for d, b, _ in mine])
            vals = cat([kv_refs[d][block_rows(blocks + b), cols] for d, b, _ in mine])
            raw = dot_nt(keys, q_ref[rows, cols])
            parts = []
            for i, (_, _, level) in enumerate(mine):
                part = raw[i * BLOCK : (i + 1) * BLOCK]
                if level is None:
                    part = jnp.where(causal, part, MASKED)
                else:
                    part = part + jnp.where(use_ref[n * LEVELS + level] == 1, 0.0, MASKED)
                parts.append(part)
            top = jnp.max(functools.reduce(jnp.maximum, parts), 0, keepdims=True) * LOG2_SCALE
            grown = [jnp.exp2(part * LOG2_SCALE - top) for part in parts]
            total = jnp.sum(functools.reduce(jnp.add, grown), 0, keepdims=True)
            share = 1.0 / total
            prob = cat([(part * share).astype(BF16) for part in grown])
            mixed_ref[rows, cols] = dot_tn(prob, vals).astype(BF16)
            lse_ref[j : j + 1, rows] = top + jnp.log2(total)


def query_kernel(tiles, count, heads, heads_up, use_ref, q_ref, g_ref, lse_ref, *refs):
    kv_refs = refs[:count]
    dq_ref, stats_ref = refs[count:]
    blocks = len(tiles)
    causal = causal_tile()
    for n, mine in enumerate(tiles):
        rows = block_rows(n)
        for j in range(heads):
            cols = head_cols(j)
            keys = cat([kv_refs[d][block_rows(b), cols] for d, b, _ in mine])
            vals = cat([kv_refs[d][block_rows(blocks + b), cols] for d, b, _ in mine])
            lse = lse_ref[j : j + 1, rows]
            raw = dot_nt(keys, q_ref[rows, cols])
            prob_grad = dot_nt(vals, g_ref[rows, cols])
            probs, weighted = [], None
            for i, (_, _, level) in enumerate(mine):
                here = slice(i * BLOCK, (i + 1) * BLOCK)
                if level is None:
                    logits = jnp.where(causal, raw[here] * LOG2_SCALE - lse, MASKED)
                else:
                    off = lse + jnp.where(use_ref[n * LEVELS + level] == 1, 0.0, -MASKED)
                    logits = raw[here] * LOG2_SCALE - off
                prob = jnp.exp2(logits)
                probs.append(prob)
                part = prob * prob_grad[here]
                weighted = part if weighted is None else weighted + part
            delta = jnp.sum(weighted, 0, keepdims=True)
            score_grad = [
                (prob * SCALE * (prob_grad[i * BLOCK : (i + 1) * BLOCK] - delta)).astype(BF16)
                for i, prob in enumerate(probs)
            ]
            dq_ref[rows, cols] = dot_tn(cat(score_grad), keys).astype(BF16)
            stats_ref[j : j + 1, rows] = lse
            stats_ref[heads_up + j : heads_up + j + 1, rows] = delta
        flags = jnp.zeros((8, BLOCK), F32)
        level_row = lax.broadcasted_iota(jnp.int32, (8, BLOCK), 0)
        for level in range(LEVELS):
            flag = jnp.where(use_ref[n * LEVELS + level] == 1, 1.0, 0.0)
            flags = jnp.where(level_row == level, flag, flags)
        stats_ref[2 * heads_up :, rows] = flags
    for row in range(heads, heads_up):
        for first in (0, heads_up):
            stats_ref[first + row : first + row + 1, :] = jnp.zeros((1, stats_ref.shape[1]), F32)


def key_kernel(tiles, count, heads, heads_up, k_ref, v_ref, *refs):
    q_refs, g_refs, s_refs = refs[:count], refs[count : 2 * count], refs[2 * count : 3 * count]
    dk_ref, dv_ref = refs[3 * count :]
    causal = causal_tile()
    for b in range(len(tiles)):
        rows = block_rows(b)
        seers = [
            (d, n, level)
            for n, mine in enumerate(tiles)
            for d, block, level in mine
            if block == b
        ]
        for j in range(heads):
            cols = head_cols(j)
            ques = cat([q_refs[d][block_rows(n), cols] for d, n, _ in seers])
            grads = cat([g_refs[d][block_rows(n), cols] for d, n, _ in seers])
            raw = dot_nt(k_ref[rows, cols], ques)
            prob_grad = dot_nt(v_ref[rows, cols], grads)
            probs, score_grads = [], []
            for i, (d, n, level) in enumerate(seers):
                here = slice(i * BLOCK, (i + 1) * BLOCK)
                lse = s_refs[d][j : j + 1, block_rows(n)]
                delta = s_refs[d][heads_up + j : heads_up + j + 1, block_rows(n)]
                if level is None:
                    logits = jnp.where(causal, raw[:, here] * LOG2_SCALE - lse, MASKED)
                else:
                    row = 2 * heads_up + level
                    off = lse + (1.0 - s_refs[d][row : row + 1, block_rows(n)]) * (-MASKED)
                    logits = raw[:, here] * LOG2_SCALE - off
                prob = jnp.exp2(logits)
                probs.append(prob.astype(BF16))
                score_grads.append((prob * SCALE * (prob_grad[:, here] - delta)).astype(BF16))
            dv_ref[rows, cols] = dot(cat(probs, 1), grads).astype(BF16)
            dk_ref[rows, cols] = dot(cat(score_grads, 1), ques).astype(BF16)


class Stream:
    def __init__(self, pieces, held, sems):
        self.held = held
        self.copies = [
            pltpu.make_async_copy(piece, held.at[i], sems.at[i]) for i, piece in enumerate(pieces)
        ]
        for copy in self.copies[:2]:
            copy.start()

    def piece(self, i):
        self.copies[i].wait()
        if i + 2 < len(self.copies):
            self.copies[i + 2].start()
        return self.held.at[i]


def mixed_grad_kernel(count, split, place_ref, *refs):
    c_refs, w_ref, out_ref, held, sems = refs[:count], refs[count], *refs[count + 1 :]
    depth = c_refs[0].shape[1]
    width = out_ref.shape[1] // split
    stream = Stream(
        [w_ref.at[:, part * width : (part + 1) * width] for part in range(split)], held, sems
    )
    for part in range(split):
        piece = stream.piece(part)
        total = None
        for i in range(count):
            rows = pl.ds(pl.multiple_of(place_ref[i] * depth, depth), depth)
            step = dot(c_refs[i][...], piece[rows, :])
            total = step if total is None else total + step
        out_ref[:, part * width : (part + 1) * width] = total.astype(BF16)


def partial_kernel(split, place_ref, m_ref, w_ref, keep_ref, give_ref, held, sems):
    depth = keep_ref.shape[2]
    height = depth // split
    firsts = [place_ref[i] * depth + part * height for i in range(4) for part in range(split)]
    pieces = [w_ref.at[pl.ds(pl.multiple_of(first, height), height), :] for first in firsts]
    stream = Stream(pieces, held, sems)
    outs = [(give_ref, 0), (give_ref, 1), (keep_ref, 0), (keep_ref, 1)]
    for i, (out_ref, at) in enumerate(outs):
        for part in range(split):
            piece = stream.piece(i * split + part)
            cols = slice(part * height, (part + 1) * height)
            out_ref[at, :, cols] = dot_nt(m_ref[...], piece[...]).astype(BF16)


def weight_grad_kernel(count, place_ref, c_ref, *refs):
    m_refs, out_ref = refs[:count], refs[count]
    features = out_ref.shape[0]
    height = min(512, features)
    for first in range(0, features, height):
        total = None
        for p in range(count):
            part = dot_tn(c_ref[place_ref[p], :, first : first + height], m_refs[p][...])
            total = part if total is None else total + part
        out_ref[first : first + height, :] = total.astype(BF16)


def cost(flops, bytes_accessed, exps=0, weight=1.0):
    return pl.CostEstimate(
        flops=int(flops * weight),
        bytes_accessed=int(bytes_accessed * weight),
        transcendentals=int(exps * weight),
    )


def kernel_call(body, name, scalars, arrays, out_shape, estimate, outside=(), scratch=()):
    smem = pl.BlockSpec(memory_space=pltpu.SMEM)
    vmem = pl.BlockSpec(memory_space=pltpu.VMEM)
    return pl.pallas_call(
        body,
        in_specs=[smem] * len(scalars)
        + [vmem] * len(arrays)
        + [pl.BlockSpec(memory_space=pltpu.HBM)] * len(outside),
        out_specs=jax.tree.map(lambda _: vmem, out_shape),
        out_shape=out_shape,
        scratch_shapes=list(scratch),
        compiler_params=pltpu.CompilerParams(
            vmem_limit_bytes=STREAM_LIMIT if outside else VMEM_LIMIT
        ),
        cost_estimate=estimate,
        name=name,
    )(*scalars, *arrays, *outside)


def weight_scratch(count, depth, columns):
    return [pltpu.VMEM((count, depth, columns), BF16), pltpu.SemaphoreType.DMA((count,))]


VMEM_LIMIT = 20 * 1024 * 1024
WEIGHTS = dict(mixed_grad=0.0, forward=100.0, partial=0.0, query=100.0, key=0.0)
STREAM_LIMIT = 54 * 1024 * 1024


def features_here(value, *others, serial=False):
    heads, reps = lax.axis_size("head"), lax.axis_size("rep")
    if heads == 2 and reps == 2:
        h, r = lax.axis_index("head"), lax.axis_index("rep")
        across = swap(after(value, *others), "head")
        beside = swap(after(value, across) if serial else value, "rep")
        corner = swap(after(across, beside) if serial else across, "rep")
        blocks = [value, beside, across, corner]
        places = [2 * h + r, 2 * h + 1 - r, 2 * (1 - h) + r, 2 * (1 - h) + 1 - r]
        return blocks, jnp.stack(places).astype(jnp.int32)
    gathered = lax.all_gather(value, ("head", "rep"), axis=0)
    count = heads * reps
    return [gathered[i] for i in range(count)], jnp.arange(count, dtype=jnp.int32)


def attended_partial(mixed_heads, out_weight, places, estimate):
    heads, reps = lax.axis_size("head"), lax.axis_size("rep")
    if heads == 2 and reps == 2:
        rows = mixed_heads.shape[0]
        share = out_weight.shape[0] // 4
        order = jnp.stack([places[1], places[3], places[0], places[2]])
        return kernel_call(
            functools.partial(partial_kernel, 1),
            "attended_partial",
            [order],
            [mixed_heads],
            [jax.ShapeDtypeStruct((2, rows, share), BF16)] * 2,
            estimate,
            [out_weight],
            weight_scratch(4, share, mixed_heads.shape[1]),
        )
    partial_value = lax.dot_general(mixed_heads, out_weight, NT, preferred_element_type=F32)
    return [partial_value.astype(BF16)]


def attended_share(partial_products, *others):
    if len(partial_products) == 1:
        return lax.psum_scatter(
            partial_products[0], ("head", "rep"), scatter_dimension=1, tiled=True
        )
    keep, give = partial_products
    got = swap(after(give, *others), "rep")
    across = (keep[1].astype(F32) + got[1].astype(F32)).astype(BF16)
    across = swap(across, "head")
    return (keep[0].astype(F32) + got[0].astype(F32) + across.astype(F32)).astype(BF16)


def per_device(queries, keys, values, out_weight, level_mask, cotangent):
    rows, columns = queries.shape
    features = out_weight.shape[0]
    heads = columns // HEAD_DIM
    heads_up = -(-heads // 8) * 8
    blocks = rows // BLOCK
    peers = lax.axis_size("seq")
    place = lax.axis_index("seq")
    tiles = seen_tiles(blocks, peers)
    distances = sorted({d for mine in tiles for d, _, _ in mine})
    count = len(distances)
    slot = {d: i for i, d in enumerate(distances)}
    tiles = [[(slot[d], b, level) for d, b, level in mine] for mine in tiles]
    pairs = sum(len(mine) for mine in tiles)
    attention_flops = 2 * heads * pairs * BLOCK * BLOCK * HEAD_DIM
    array_bytes = 2 * rows * columns
    exps = heads * pairs * BLOCK * BLOCK
    like_queries = jax.ShapeDtypeStruct((rows, columns), BF16)

    def further(got, sign, *others):
        near, far = distances[len(got) - 1], distances[len(got)]
        return got + [shift(after(got[-1], *others), sign * (far - near))]

    block_ids = place * blocks + jnp.arange(blocks, dtype=jnp.int32)
    offsets = 2 ** jnp.arange(LEVELS, dtype=jnp.int32)
    use = ((block_ids[:, None] >= offsets[None]) & (level_mask == 1)).astype(jnp.int32)
    use = use.reshape(-1)

    kv_all = further([jnp.concatenate([keys, values])], 1)
    query_all = further([queries], -1)
    c_blocks, c_places = features_here(cotangent)
    group_count = len(c_blocks)
    part_cols = cotangent.shape[1]
    while len(query_all) < count:
        query_all = further(query_all, -1)
    split = max(1, columns // 256)
    mixed_grad = kernel_call(
        functools.partial(mixed_grad_kernel, group_count, split),
        "mixed_grad",
        [c_places],
        c_blocks,
        like_queries,
        cost(2 * rows * columns * features, 2 * columns * features, 0, WEIGHTS["mixed_grad"]),
        [out_weight],
        weight_scratch(split, features, columns // split),
    )
    while len(kv_all) < count:
        kv_all = further(kv_all, 1, mixed_grad)
    grad_all = further([mixed_grad], -1, query_all[-1])
    first_grad = grad_all[-1]
    while len(grad_all) < count:
        grad_all = further(grad_all, -1)

    h, r = lax.axis_index("head"), lax.axis_index("rep")
    n_head, n_rep = lax.axis_size("head"), lax.axis_size("rep")
    step_of = lambda i: (i // n_rep) + n_head * (i % n_rep)
    wanted = (place + step_of(h * n_rep + r)) % peers
    out_block = c_blocks[0]
    for i in range(1, group_count):
        out_block = jnp.where(c_places[i] == wanted, c_blocks[i], out_block)
    links = []
    for s in range(peers):
        for q in range(group_count):
            links.append((s * group_count + q, ((s + step_of(q)) % peers) * group_count + q))
    arrived = lax.ppermute(after(out_block, first_grad), ("seq", "head", "rep"), links)

    mixed_heads, lse = kernel_call(
        functools.partial(forward_kernel, tiles, count, heads),
        "attention_forward",
        [use],
        [after(queries, query_all[-1], grad_all[-1]), *kv_all],
        [like_queries, jax.ShapeDtypeStruct((heads_up, rows), F32)],
        cost(2 * attention_flops, (2 * count + 2) * array_bytes, exps, WEIGHTS["forward"]),
    )

    near = {}
    if peers <= 4:
        near = {k: cyclic(mixed_heads, k) for k in sorted({1, peers - 1}) if 0 < k < peers}
    stats_shape = jax.ShapeDtypeStruct((2 * heads_up + 8, rows), F32)
    q_grad, stats = kernel_call(
        functools.partial(query_kernel, tiles, count, heads, heads_up),
        "attention_query_grad",
        [use],
        [after(queries, mixed_heads), mixed_grad, lse, *kv_all],
        [like_queries, stats_shape],
        cost(3 * attention_flops, (2 * count + 3) * array_bytes, exps, WEIGHTS["query"]),
    )
    stats_all = [stats] + [shift(stats, -d) for d in distances[1:]]
    partial_products = attended_partial(
        mixed_heads, out_weight, c_places, cost(2 * rows * columns * features, 2 * rows * features, 0, WEIGHTS["partial"])
    )
    ct_across = swap(after(arrived, mixed_heads), "head") if n_head == 2 and n_rep == 2 else arrived
    held = after(mixed_heads, ct_across, *near.values(), *stats_all[1:], *partial_products)
    if peers <= 4:
        mixed_all = [mixed_heads] + [
            near[k] if k in near else cyclic(held, k) for k in range(1, peers)
        ]
    else:
        gathered = lax.all_gather(mixed_heads, "seq", axis=0)
        mixed_all = [
            lax.dynamic_index_in_dim(gathered, (place - k) % peers, 0, False)
            for k in range(peers)
        ]
    attended = attended_share(partial_products, held)
    if n_head == 2 and n_rep == 2:
        ct_blocks = [arrived, swap(after(arrived, held), "rep"), ct_across, swap(after(ct_across, held), "rep")]
        ct_places = c_places
    else:
        ct_blocks, ct_places = features_here(arrived)
    ct = jnp.stack(ct_blocks)
    k_grad, v_grad = kernel_call(
        functools.partial(key_kernel, tiles, count, heads, heads_up),
        "attention_key_grad",
        [],
        [after(keys, held), values, *query_all, *grad_all, *stats_all],
        [like_queries] * 2,
        cost(4 * attention_flops, (2 * count + 4) * array_bytes, exps, WEIGHTS["key"]),
    )

    steps = step_of(ct_places)
    ct_at = jnp.sum(
        jnp.where(steps[None] == jnp.arange(peers)[:, None], jnp.arange(group_count)[None], 0), 1
    ).astype(jnp.int32)
    weight_grad = kernel_call(
        functools.partial(weight_grad_kernel, peers),
        "weight_grad",
        [ct_at],
        [ct, after(mixed_all[0], attended, k_grad), *mixed_all[1:]],
        jax.ShapeDtypeStruct((part_cols, columns), BF16),
        cost(2 * part_cols * columns * rows * peers, 2 * array_bytes * peers),
    )
    return (attended, q_grad, k_grad, v_grad, weight_grad)


def solution(mesh):
    shared = P(("groups", "seq"), ("head", "rep"))
    return jax.shard_map(
        per_device,
        mesh=mesh,
        in_specs=(shared, shared, shared, P(None, ("head", "rep")), P(("groups", "seq"), None), shared),
        out_specs=(shared,) * 5,
        check_vma=False,
    )
```

```python
import functools
import math

import jax
import jax.numpy as jnp
from jax import lax
from jax.experimental import pallas as pl
from jax.experimental.pallas import tpu as pltpu
from jax.sharding import PartitionSpec as P

HEAD_DIM = 128
BLOCK = 128
LEVELS = 5
SCALE = HEAD_DIM ** (-0.5)
LOG2_SCALE = SCALE * math.log2(math.e)
MASKED = -1e30

F32 = jnp.float32
BF16 = jnp.bfloat16
NT = (((1,), (1,)), ((), ()))
TN = (((0,), (0,)), ((), ()))


def shift(value, by):
    peers = lax.axis_size("seq")
    return lax.ppermute(
        value, "seq", [(i, i + by) for i in range(peers) if 0 <= i + by < peers]
    )


def cyclic(value, by):
    peers = lax.axis_size("seq")
    return lax.ppermute(value, "seq", [(i, (i + by) % peers) for i in range(peers)])


def swap(value, axis):
    return lax.ppermute(value, axis, [(0, 1), (1, 0)])


def dot(a, b):
    return jnp.dot(a, b, preferred_element_type=F32)


def dot_nt(a, b):
    return lax.dot_general(a, b, NT, preferred_element_type=F32)


def dot_tn(a, b):
    return lax.dot_general(a, b, TN, preferred_element_type=F32)


def after(value, *others):
    return lax.optimization_barrier((value, others))[0]


def seen_tiles(blocks, peers):
    tiles = []
    for n in range(blocks):
        mine = [(0, n, None)]
        for level in range(LEVELS):
            target = n - 2**level
            distance = -(target // blocks)
            if distance < peers:
                mine.append((distance, target % blocks, level))
        tiles.append(mine)
    return tiles


def block_rows(n):
    return pl.ds(n * BLOCK, BLOCK)


def head_cols(j):
    return slice(j * HEAD_DIM, (j + 1) * HEAD_DIM)


def cat(parts, axis=0):
    return parts[0] if len(parts) == 1 else jnp.concatenate(parts, axis)


def causal_tile():
    rows = lax.broadcasted_iota(jnp.int32, (BLOCK, BLOCK), 0)
    cols = lax.broadcasted_iota(jnp.int32, (BLOCK, BLOCK), 1)
    return rows <= cols


def forward_kernel(tiles, count, heads, use_ref, q_ref, *refs):
    kv_refs = refs[:count]
    mixed_ref, lse_ref = refs[count:]
    blocks = len(tiles)
    causal = causal_tile()
    for n, mine in enumerate(tiles):
        rows = block_rows(n)
        for j in range(heads):
            cols = head_cols(j)
            keys = cat([kv_refs[d][block_rows(b), cols] for d, b, _ in mine])
            vals = cat([kv_refs[d][block_rows(blocks + b), cols] for d, b, _ in mine])
            raw = dot_nt(keys, q_ref[rows, cols])
            parts = []
            for i, (_, _, level) in enumerate(mine):
                part = raw[i * BLOCK : (i + 1) * BLOCK]
                if level is None:
                    part = jnp.where(causal, part, MASKED)
                else:
                    part = part + jnp.where(use_ref[n * LEVELS + level] == 1, 0.0, MASKED)
                parts.append(part)
            top = jnp.max(functools.reduce(jnp.maximum, parts), 0, keepdims=True) * LOG2_SCALE
            grown = [jnp.exp2(part * LOG2_SCALE - top) for part in parts]
            total = jnp.sum(functools.reduce(jnp.add, grown), 0, keepdims=True)
            share = 1.0 / total
            prob = cat([(part * share).astype(BF16) for part in grown])
            mixed_ref[rows, cols] = dot_tn(prob, vals).astype(BF16)
            lse_ref[j : j + 1, rows] = top + jnp.log2(total)


def query_kernel(tiles, count, heads, heads_up, use_ref, q_ref, g_ref, lse_ref, *refs):
    kv_refs = refs[:count]
    dq_ref, stats_ref = refs[count:]
    blocks = len(tiles)
    causal = causal_tile()
    for n, mine in enumerate(tiles):
        rows = block_rows(n)
        for j in range(heads):
            cols = head_cols(j)
            keys = cat([kv_refs[d][block_rows(b), cols] for d, b, _ in mine])
            vals = cat([kv_refs[d][block_rows(blocks + b), cols] for d, b, _ in mine])
            lse = lse_ref[j : j + 1, rows]
            raw = dot_nt(keys, q_ref[rows, cols])
            prob_grad = dot_nt(vals, g_ref[rows, cols])
            probs, weighted = [], None
            for i, (_, _, level) in enumerate(mine):
                here = slice(i * BLOCK, (i + 1) * BLOCK)
                if level is None:
                    logits = jnp.where(causal, raw[here] * LOG2_SCALE - lse, MASKED)
                else:
                    off = lse + jnp.where(use_ref[n * LEVELS + level] == 1, 0.0, -MASKED)
                    logits = raw[here] * LOG2_SCALE - off
                prob = jnp.exp2(logits)
                probs.append(prob)
                part = prob * prob_grad[here]
                weighted = part if weighted is None else weighted + part
            delta = jnp.sum(weighted, 0, keepdims=True)
            score_grad = [
                (prob * SCALE * (prob_grad[i * BLOCK : (i + 1) * BLOCK] - delta)).astype(BF16)
                for i, prob in enumerate(probs)
            ]
            dq_ref[rows, cols] = dot_tn(cat(score_grad), keys).astype(BF16)
            stats_ref[j : j + 1, rows] = lse
            stats_ref[heads_up + j : heads_up + j + 1, rows] = delta
        flags = jnp.zeros((8, BLOCK), F32)
        level_row = lax.broadcasted_iota(jnp.int32, (8, BLOCK), 0)
        for level in range(LEVELS):
            flag = jnp.where(use_ref[n * LEVELS + level] == 1, 1.0, 0.0)
            flags = jnp.where(level_row == level, flag, flags)
        stats_ref[2 * heads_up :, rows] = flags
    for row in range(heads, heads_up):
        for first in (0, heads_up):
            stats_ref[first + row : first + row + 1, :] = jnp.zeros((1, stats_ref.shape[1]), F32)


def key_kernel(tiles, count, heads, heads_up, k_ref, v_ref, *refs):
    q_refs, g_refs, s_refs = refs[:count], refs[count : 2 * count], refs[2 * count : 3 * count]
    dk_ref, dv_ref = refs[3 * count :]
    causal = causal_tile()
    for b in range(len(tiles)):
        rows = block_rows(b)
        seers = [
            (d, n, level)
            for n, mine in enumerate(tiles)
            for d, block, level in mine
            if block == b
        ]
        for j in range(heads):
            cols = head_cols(j)
            ques = cat([q_refs[d][block_rows(n), cols] for d, n, _ in seers])
            grads = cat([g_refs[d][block_rows(n), cols] for d, n, _ in seers])
            raw = dot_nt(k_ref[rows, cols], ques)
            prob_grad = dot_nt(v_ref[rows, cols], grads)
            probs, score_grads = [], []
            for i, (d, n, level) in enumerate(seers):
                here = slice(i * BLOCK, (i + 1) * BLOCK)
                lse = s_refs[d][j : j + 1, block_rows(n)]
                delta = s_refs[d][heads_up + j : heads_up + j + 1, block_rows(n)]
                if level is None:
                    logits = jnp.where(causal, raw[:, here] * LOG2_SCALE - lse, MASKED)
                else:
                    row = 2 * heads_up + level
                    off = lse + (1.0 - s_refs[d][row : row + 1, block_rows(n)]) * (-MASKED)
                    logits = raw[:, here] * LOG2_SCALE - off
                prob = jnp.exp2(logits)
                probs.append(prob.astype(BF16))
                score_grads.append((prob * SCALE * (prob_grad[:, here] - delta)).astype(BF16))
            dv_ref[rows, cols] = dot(cat(probs, 1), grads).astype(BF16)
            dk_ref[rows, cols] = dot(cat(score_grads, 1), ques).astype(BF16)


class Stream:
    def __init__(self, pieces, held, sems):
        self.held = held
        self.copies = [
            pltpu.make_async_copy(piece, held.at[i], sems.at[i]) for i, piece in enumerate(pieces)
        ]
        for copy in self.copies[:2]:
            copy.start()

    def piece(self, i):
        self.copies[i].wait()
        if i + 2 < len(self.copies):
            self.copies[i + 2].start()
        return self.held.at[i]


def mixed_grad_kernel(count, given, place_ref, *refs):
    total = refs[0][...] if given else None
    c_refs, w_ref, out_ref, held, sems = refs[given : given + count], *refs[given + count :]
    depth = c_refs[0].shape[1]
    firsts = [pl.multiple_of(place_ref[i] * depth, depth) for i in range(count)]
    stream = Stream([w_ref.at[pl.ds(first, depth), :] for first in firsts], held, sems)
    for i in range(count):
        step = dot(c_refs[i][...], stream.piece(i)[...])
        total = step if total is None else total + step
    out_ref[...] = total.astype(out_ref.dtype)


def partial_kernel(split, place_ref, m_ref, w_ref, keep_ref, give_ref, held, sems):
    depth = keep_ref.shape[2]
    height = depth // split
    firsts = [place_ref[i] * depth + part * height for i in range(4) for part in range(split)]
    pieces = [w_ref.at[pl.ds(pl.multiple_of(first, height), height), :] for first in firsts]
    stream = Stream(pieces, held, sems)
    outs = [(give_ref, 0), (give_ref, 1), (keep_ref, 0), (keep_ref, 1)]
    for i, (out_ref, at) in enumerate(outs):
        for part in range(split):
            piece = stream.piece(i * split + part)
            cols = slice(part * height, (part + 1) * height)
            out_ref[at, :, cols] = dot_nt(m_ref[...], piece[...]).astype(BF16)


def weight_grad_kernel(which, given, place_ref, *refs):
    c_ref, m_refs, out_ref = refs[given], refs[given + 1 : -1], refs[-1]
    features = out_ref.shape[0]
    height = min(512, features)
    for first in range(0, features, height):
        rows = slice(first, first + height)
        total = refs[0][rows, :] if given else None
        for p, m_ref in zip(which, m_refs):
            part = dot_tn(c_ref[place_ref[p], :, rows], m_ref[...])
            total = part if total is None else total + part
        out_ref[rows, :] = total.astype(out_ref.dtype)


def cost(flops, bytes_accessed, exps=0, weight=1.0):
    return pl.CostEstimate(
        flops=int(flops * weight),
        bytes_accessed=int(bytes_accessed * weight),
        transcendentals=int(exps * weight),
    )


def kernel_call(body, name, scalars, arrays, out_shape, estimate, outside=(), scratch=()):
    smem = pl.BlockSpec(memory_space=pltpu.SMEM)
    vmem = pl.BlockSpec(memory_space=pltpu.VMEM)
    return pl.pallas_call(
        body,
        in_specs=[smem] * len(scalars)
        + [vmem] * len(arrays)
        + [pl.BlockSpec(memory_space=pltpu.HBM)] * len(outside),
        out_specs=jax.tree.map(lambda _: vmem, out_shape),
        out_shape=out_shape,
        scratch_shapes=list(scratch),
        compiler_params=pltpu.CompilerParams(
            vmem_limit_bytes=STREAM_LIMIT if outside else VMEM_LIMIT
        ),
        cost_estimate=estimate,
        name=name,
    )(*scalars, *arrays, *outside)


def weight_scratch(count, depth, columns):
    return [pltpu.VMEM((count, depth, columns), BF16), pltpu.SemaphoreType.DMA((count,))]


VMEM_LIMIT = 20 * 1024 * 1024
WEIGHTS = dict(mixed_grad=0.0, forward=100.0, partial=0.0, query=100.0, key=0.0, weight=0.0)
STREAM_LIMIT = 54 * 1024 * 1024


def two_by_two():
    return lax.axis_size("head") == 2 and lax.axis_size("rep") == 2


def features_here(value):
    heads, reps = lax.axis_size("head"), lax.axis_size("rep")
    if two_by_two():
        h, r = lax.axis_index("head"), lax.axis_index("rep")
        places = [2 * h + r, 2 * h + 1 - r, 2 * (1 - h) + r, 2 * (1 - h) + 1 - r]
        rest = swap(value, "head")
        return [value, swap(value, "rep")], rest, jnp.stack(places).astype(jnp.int32)
    count = heads * reps
    gathered = lax.all_gather(value, ("head", "rep"), axis=0)
    blocks = [gathered[i] for i in range(count)]
    return blocks[: count // 2], blocks[count // 2 :], jnp.arange(count, dtype=jnp.int32)


def other_features(rest, *others):
    if two_by_two():
        return [rest, swap(after(rest, *others), "rep")]
    return rest


def attended_partial(mixed_heads, out_weight, places, estimate):
    if two_by_two():
        rows = mixed_heads.shape[0]
        share = out_weight.shape[0] // 4
        order = jnp.stack([places[1], places[3], places[0], places[2]])
        return kernel_call(
            functools.partial(partial_kernel, 1),
            "attended_partial",
            [order],
            [mixed_heads],
            [jax.ShapeDtypeStruct((2, rows, share), BF16)] * 2,
            estimate,
            [out_weight],
            weight_scratch(4, share, mixed_heads.shape[1]),
        )
    partial_value = lax.dot_general(mixed_heads, out_weight, NT, preferred_element_type=F32)
    return [partial_value.astype(BF16)]


def attended_share(partial_products, *others):
    if len(partial_products) == 1:
        return lax.psum_scatter(
            partial_products[0], ("head", "rep"), scatter_dimension=1, tiled=True
        )
    keep, give = partial_products
    got = swap(after(give, *others), "rep")
    across = (keep[1].astype(F32) + got[1].astype(F32)).astype(BF16)
    across = swap(across, "head")
    return (keep[0].astype(F32) + got[0].astype(F32) + across.astype(F32)).astype(BF16)


def per_device(queries, keys, values, out_weight, level_mask, cotangent):
    rows, columns = queries.shape
    features = out_weight.shape[0]
    heads = columns // HEAD_DIM
    heads_up = -(-heads // 8) * 8
    blocks = rows // BLOCK
    peers = lax.axis_size("seq")
    place = lax.axis_index("seq")
    tiles = seen_tiles(blocks, peers)
    distances = sorted({d for mine in tiles for d, _, _ in mine})
    count = len(distances)
    slot = {d: i for i, d in enumerate(distances)}
    tiles = [[(slot[d], b, level) for d, b, level in mine] for mine in tiles]
    pairs = sum(len(mine) for mine in tiles)
    attention_flops = 2 * heads * pairs * BLOCK * BLOCK * HEAD_DIM
    array_bytes = 2 * rows * columns
    exps = heads * pairs * BLOCK * BLOCK
    like_queries = jax.ShapeDtypeStruct((rows, columns), BF16)

    def further(got, sign, *others):
        near, far = distances[len(got) - 1], distances[len(got)]
        return got + [shift(after(got[-1], *others), sign * (far - near))]

    block_ids = place * blocks + jnp.arange(blocks, dtype=jnp.int32)
    offsets = 2 ** jnp.arange(LEVELS, dtype=jnp.int32)
    use = ((block_ids[:, None] >= offsets[None]) & (level_mask == 1)).astype(jnp.int32)
    use = use.reshape(-1)

    kv_all = further([jnp.concatenate([keys, values])], 1)
    query_all = further([queries], -1)
    c_blocks, c_rest, c_places = features_here(cotangent)
    half = len(c_blocks)
    part_cols = cotangent.shape[1]
    while len(query_all) < count:
        query_all = further(query_all, -1)
    mixed_sum = []
    for part in range(2):
        if part:
            c_blocks = c_blocks + other_features(c_rest, *mixed_sum)
        mine = slice(part * half, (part + 1) * half)
        mixed_sum = [
            kernel_call(
                functools.partial(mixed_grad_kernel, half, part),
                "mixed_grad",
                [c_places[mine]],
                [*mixed_sum, *c_blocks[mine]],
                jax.ShapeDtypeStruct((rows, columns), BF16 if part else F32),
                cost(rows * columns * features, columns * features, 0, WEIGHTS["mixed_grad"] * (1 - part)),
                [out_weight],
                weight_scratch(half, part_cols, columns),
            )
        ]
    mixed_grad = mixed_sum[0]
    group_count = len(c_blocks)
    while len(kv_all) < count:
        kv_all = further(kv_all, 1, mixed_grad)
    grad_all = further([mixed_grad], -1, query_all[-1])
    while len(grad_all) < count:
        grad_all = further(grad_all, -1)

    h, r = lax.axis_index("head"), lax.axis_index("rep")
    n_head, n_rep = lax.axis_size("head"), lax.axis_size("rep")
    step_of = lambda i: (i // n_rep) + n_head * (i % n_rep)
    wanted = (place + step_of(h * n_rep + r)) % peers
    out_block = c_blocks[0]
    for i in range(1, group_count):
        out_block = jnp.where(c_places[i] == wanted, c_blocks[i], out_block)
    links = []
    for s in range(peers):
        for q in range(group_count):
            links.append((s * group_count + q, ((s + step_of(q)) % peers) * group_count + q))
    arrived = lax.ppermute(after(out_block, grad_all[-1], kv_all[-1]), ("seq", "head", "rep"), links)

    mixed_heads, lse = kernel_call(
        functools.partial(forward_kernel, tiles, count, heads),
        "attention_forward",
        [use],
        [after(queries, query_all[-1], grad_all[-1]), *kv_all],
        [like_queries, jax.ShapeDtypeStruct((heads_up, rows), F32)],
        cost(2 * attention_flops, (2 * count + 2) * array_bytes, exps, WEIGHTS["forward"]),
    )

    near = {}
    if peers <= 4:
        near = {k: cyclic(mixed_heads, k) for k in sorted({1, peers - 1}) if 0 < k < peers}
    stats_shape = jax.ShapeDtypeStruct((2 * heads_up + 8, rows), F32)
    q_grad, stats = kernel_call(
        functools.partial(query_kernel, tiles, count, heads, heads_up),
        "attention_query_grad",
        [use],
        [after(queries, mixed_heads), mixed_grad, lse, *kv_all],
        [like_queries, stats_shape],
        cost(3 * attention_flops, (2 * count + 3) * array_bytes, exps, WEIGHTS["query"]),
    )
    stats_all = [stats] + [shift(stats, -d) for d in distances[1:]]
    partial_products = attended_partial(
        mixed_heads, out_weight, c_places, cost(2 * rows * columns * features, 2 * rows * features, 0, WEIGHTS["partial"])
    )
    ct_across = swap(after(arrived, mixed_heads), "head") if two_by_two() else arrived
    held = after(mixed_heads, ct_across, *near.values(), *stats_all[1:], *partial_products)
    if peers <= 4:
        mixed_all = [mixed_heads] + [
            near[k] if k in near else cyclic(held, k) for k in range(1, peers)
        ]
    else:
        gathered = lax.all_gather(mixed_heads, "seq", axis=0)
        mixed_all = [
            lax.dynamic_index_in_dim(gathered, (place - k) % peers, 0, False)
            for k in range(peers)
        ]
    attended = attended_share(partial_products, held)
    if two_by_two():
        ct_blocks = [arrived, swap(after(arrived, held), "rep"), *other_features(ct_across, held)]
    else:
        ct_blocks, ct_rest, _ = features_here(arrived)
        ct_blocks = ct_blocks + ct_rest
    ct = jnp.stack(ct_blocks)
    k_grad, v_grad = kernel_call(
        functools.partial(key_kernel, tiles, count, heads, heads_up),
        "attention_key_grad",
        [],
        [after(keys, held), values, *query_all, *grad_all, *stats_all],
        [like_queries] * 2,
        cost(4 * attention_flops, (2 * count + 4) * array_bytes, exps, WEIGHTS["key"]),
    )

    steps = step_of(c_places)
    ct_at = jnp.sum(
        jnp.where(steps[None] == jnp.arange(peers)[:, None], jnp.arange(group_count)[None], 0), 1
    ).astype(jnp.int32)
    early = sorted({0, 1, peers - 1}) if 2 < peers <= 4 else [0]
    late = [k for k in range(peers) if k not in early]
    weight_sum = []
    for part, which in enumerate((early, late)):
        if not which:
            weight_sum = [weight_sum[0].astype(BF16)]
            break
        ranges = [mixed_all[k] for k in which]
        if part:
            ranges[0] = after(ranges[0], attended, k_grad)
        weight_sum = [
            kernel_call(
                functools.partial(weight_grad_kernel, which, part),
                "weight_grad",
                [ct_at],
                [*weight_sum, ct, *ranges],
                jax.ShapeDtypeStruct((part_cols, columns), BF16 if part else F32),
                cost(2 * part_cols * columns * rows * len(which), array_bytes * len(which), 0, WEIGHTS["weight"]),
            )
        ]
    weight_grad = weight_sum[0]
    return (attended, q_grad, k_grad, v_grad, weight_grad)


def solution(mesh):
    shared = P(("groups", "seq"), ("head", "rep"))
    return jax.shard_map(
        per_device,
        mesh=mesh,
        in_specs=(shared, shared, shared, P(None, ("head", "rep")), P(("groups", "seq"), None), shared),
        out_specs=(shared,) * 5,
        check_vma=False,
    )
```

```python
import functools
import math

import jax
import jax.numpy as jnp
from jax import lax
from jax.experimental import pallas as pl
from jax.experimental.pallas import tpu as pltpu
from jax.sharding import PartitionSpec as P

HEAD_DIM = 128
BLOCK = 128
LEVELS = 5
SCALE = HEAD_DIM ** (-0.5)
LOG2_SCALE = SCALE * math.log2(math.e)
MASKED = -1e30

F32 = jnp.float32
BF16 = jnp.bfloat16
NT = (((1,), (1,)), ((), ()))
TN = (((0,), (0,)), ((), ()))


def shift(value, by):
    peers = lax.axis_size("seq")
    return lax.ppermute(
        value, "seq", [(i, i + by) for i in range(peers) if 0 <= i + by < peers]
    )


def cyclic(value, by):
    peers = lax.axis_size("seq")
    return lax.ppermute(value, "seq", [(i, (i + by) % peers) for i in range(peers)])


def swap(value, axis):
    return lax.ppermute(value, axis, [(0, 1), (1, 0)])


def dot(a, b):
    return jnp.dot(a, b, preferred_element_type=F32)


def dot_nt(a, b):
    return lax.dot_general(a, b, NT, preferred_element_type=F32)


def dot_tn(a, b):
    return lax.dot_general(a, b, TN, preferred_element_type=F32)


def after(value, *others):
    return lax.optimization_barrier((value, others))[0]


def seen_tiles(blocks, peers):
    tiles = []
    for n in range(blocks):
        mine = [(0, n, None)]
        for level in range(LEVELS):
            target = n - 2**level
            distance = -(target // blocks)
            if distance < peers:
                mine.append((distance, target % blocks, level))
        tiles.append(mine)
    return tiles


def block_rows(n):
    return pl.ds(n * BLOCK, BLOCK)


def head_cols(j):
    return slice(j * HEAD_DIM, (j + 1) * HEAD_DIM)


def cat(parts, axis=0):
    return parts[0] if len(parts) == 1 else jnp.concatenate(parts, axis)


def causal_tile():
    rows = lax.broadcasted_iota(jnp.int32, (BLOCK, BLOCK), 0)
    cols = lax.broadcasted_iota(jnp.int32, (BLOCK, BLOCK), 1)
    return rows <= cols


def forward_kernel(tiles, count, heads, use_ref, q_ref, *refs):
    kv_refs = refs[:count]
    mixed_ref, lse_ref = refs[count:]
    blocks = len(tiles)
    causal = causal_tile()
    for n, mine in enumerate(tiles):
        rows = block_rows(n)
        for j in range(heads):
            cols = head_cols(j)
            keys = cat([kv_refs[d][block_rows(b), cols] for d, b, _ in mine])
            vals = cat([kv_refs[d][block_rows(blocks + b), cols] for d, b, _ in mine])
            raw = dot_nt(keys, q_ref[rows, cols])
            parts = []
            for i, (_, _, level) in enumerate(mine):
                part = raw[i * BLOCK : (i + 1) * BLOCK]
                if level is None:
                    part = jnp.where(causal, part, MASKED)
                else:
                    part = part + jnp.where(use_ref[n * LEVELS + level] == 1, 0.0, MASKED)
                parts.append(part)
            top = jnp.max(functools.reduce(jnp.maximum, parts), 0, keepdims=True) * LOG2_SCALE
            grown = [jnp.exp2(part * LOG2_SCALE - top) for part in parts]
            total = jnp.sum(functools.reduce(jnp.add, grown), 0, keepdims=True)
            share = 1.0 / total
            prob = cat([(part * share).astype(BF16) for part in grown])
            mixed_ref[rows, cols] = dot_tn(prob, vals).astype(BF16)
            lse_ref[j : j + 1, rows] = top + jnp.log2(total)


def query_kernel(tiles, count, heads, heads_up, use_ref, q_ref, g_ref, lse_ref, *refs):
    kv_refs = refs[:count]
    dq_ref, stats_ref = refs[count:]
    blocks = len(tiles)
    causal = causal_tile()
    for n, mine in enumerate(tiles):
        rows = block_rows(n)
        for j in range(heads):
            cols = head_cols(j)
            keys = cat([kv_refs[d][block_rows(b), cols] for d, b, _ in mine])
            vals = cat([kv_refs[d][block_rows(blocks + b), cols] for d, b, _ in mine])
            lse = lse_ref[j : j + 1, rows]
            raw = dot_nt(keys, q_ref[rows, cols])
            prob_grad = dot_nt(vals, g_ref[rows, cols])
            probs, weighted = [], None
            for i, (_, _, level) in enumerate(mine):
                here = slice(i * BLOCK, (i + 1) * BLOCK)
                if level is None:
                    logits = jnp.where(causal, raw[here] * LOG2_SCALE - lse, MASKED)
                else:
                    off = lse + jnp.where(use_ref[n * LEVELS + level] == 1, 0.0, -MASKED)
                    logits = raw[here] * LOG2_SCALE - off
                prob = jnp.exp2(logits)
                probs.append(prob)
                part = prob * prob_grad[here]
                weighted = part if weighted is None else weighted + part
            delta = jnp.sum(weighted, 0, keepdims=True)
            score_grad = [
                (prob * SCALE * (prob_grad[i * BLOCK : (i + 1) * BLOCK] - delta)).astype(BF16)
                for i, prob in enumerate(probs)
            ]
            dq_ref[rows, cols] = dot_tn(cat(score_grad), keys).astype(BF16)
            stats_ref[j : j + 1, rows] = lse
            stats_ref[heads_up + j : heads_up + j + 1, rows] = delta
        flags = jnp.zeros((8, BLOCK), F32)
        level_row = lax.broadcasted_iota(jnp.int32, (8, BLOCK), 0)
        for level in range(LEVELS):
            flag = jnp.where(use_ref[n * LEVELS + level] == 1, 1.0, 0.0)
            flags = jnp.where(level_row == level, flag, flags)
        stats_ref[2 * heads_up :, rows] = flags
    for row in range(heads, heads_up):
        for first in (0, heads_up):
            stats_ref[first + row : first + row + 1, :] = jnp.zeros((1, stats_ref.shape[1]), F32)


def key_kernel(tiles, count, heads, heads_up, k_ref, v_ref, *refs):
    q_refs, g_refs, s_refs = refs[:count], refs[count : 2 * count], refs[2 * count : 3 * count]
    dk_ref, dv_ref = refs[3 * count :]
    causal = causal_tile()
    for b in range(len(tiles)):
        rows = block_rows(b)
        seers = [
            (d, n, level)
            for n, mine in enumerate(tiles)
            for d, block, level in mine
            if block == b
        ]
        for j in range(heads):
            cols = head_cols(j)
            ques = cat([q_refs[d][block_rows(n), cols] for d, n, _ in seers])
            grads = cat([g_refs[d][block_rows(n), cols] for d, n, _ in seers])
            raw = dot_nt(k_ref[rows, cols], ques)
            prob_grad = dot_nt(v_ref[rows, cols], grads)
            probs, score_grads = [], []
            for i, (d, n, level) in enumerate(seers):
                here = slice(i * BLOCK, (i + 1) * BLOCK)
                lse = s_refs[d][j : j + 1, block_rows(n)]
                delta = s_refs[d][heads_up + j : heads_up + j + 1, block_rows(n)]
                if level is None:
                    logits = jnp.where(causal, raw[:, here] * LOG2_SCALE - lse, MASKED)
                else:
                    row = 2 * heads_up + level
                    off = lse + (1.0 - s_refs[d][row : row + 1, block_rows(n)]) * (-MASKED)
                    logits = raw[:, here] * LOG2_SCALE - off
                prob = jnp.exp2(logits)
                probs.append(prob.astype(BF16))
                score_grads.append((prob * SCALE * (prob_grad[:, here] - delta)).astype(BF16))
            dv_ref[rows, cols] = dot(cat(probs, 1), grads).astype(BF16)
            dk_ref[rows, cols] = dot(cat(score_grads, 1), ques).astype(BF16)


class Stream:
    def __init__(self, pieces, held, sems):
        self.held = held
        self.copies = [
            pltpu.make_async_copy(piece, held.at[i], sems.at[i]) for i, piece in enumerate(pieces)
        ]
        for copy in self.copies[:2]:
            copy.start()

    def piece(self, i):
        self.copies[i].wait()
        if i + 2 < len(self.copies):
            self.copies[i + 2].start()
        return self.held.at[i]


def mixed_grad_kernel(count, given, place_ref, *refs):
    total = refs[0][...] if given else None
    c_refs, w_ref, out_ref, held, sems = refs[given : given + count], *refs[given + count :]
    depth = c_refs[0].shape[1]
    firsts = [pl.multiple_of(place_ref[i] * depth, depth) for i in range(count)]
    stream = Stream([w_ref.at[pl.ds(first, depth), :] for first in firsts], held, sems)
    for i in range(count):
        step = dot(c_refs[i][...], stream.piece(i)[...])
        total = step if total is None else total + step
    out_ref[...] = total.astype(out_ref.dtype)


def partial_kernel(split, place_ref, m_ref, w_ref, keep_ref, give_ref, held, sems):
    depth = keep_ref.shape[2]
    height = depth // split
    firsts = [place_ref[i] * depth + part * height for i in range(4) for part in range(split)]
    pieces = [w_ref.at[pl.ds(pl.multiple_of(first, height), height), :] for first in firsts]
    stream = Stream(pieces, held, sems)
    outs = [(give_ref, 0), (give_ref, 1), (keep_ref, 0), (keep_ref, 1)]
    for i, (out_ref, at) in enumerate(outs):
        for part in range(split):
            piece = stream.piece(i * split + part)
            cols = slice(part * height, (part + 1) * height)
            out_ref[at, :, cols] = dot_nt(m_ref[...], piece[...]).astype(BF16)


def weight_grad_kernel(which, given, place_ref, *refs):
    c_ref, m_refs, out_ref = refs[given], refs[given + 1 : -1], refs[-1]
    features = out_ref.shape[0]
    height = min(512, features)
    for first in range(0, features, height):
        rows = slice(first, first + height)
        total = refs[0][rows, :] if given else None
        for p, m_ref in zip(which, m_refs):
            part = dot_tn(c_ref[place_ref[p], :, rows], m_ref[...])
            total = part if total is None else total + part
        out_ref[rows, :] = total.astype(out_ref.dtype)


def cost(flops, bytes_accessed, exps=0, weight=1.0):
    return pl.CostEstimate(
        flops=int(flops * weight),
        bytes_accessed=int(bytes_accessed * weight),
        transcendentals=int(exps * weight),
    )


def kernel_call(body, name, scalars, arrays, out_shape, estimate, outside=(), scratch=()):
    smem = pl.BlockSpec(memory_space=pltpu.SMEM)
    vmem = pl.BlockSpec(memory_space=pltpu.VMEM)
    return pl.pallas_call(
        body,
        in_specs=[smem] * len(scalars)
        + [vmem] * len(arrays)
        + [pl.BlockSpec(memory_space=pltpu.HBM)] * len(outside),
        out_specs=jax.tree.map(lambda _: vmem, out_shape),
        out_shape=out_shape,
        scratch_shapes=list(scratch),
        compiler_params=pltpu.CompilerParams(
            vmem_limit_bytes=STREAM_LIMIT if outside else VMEM_LIMIT
        ),
        cost_estimate=estimate,
        name=name,
    )(*scalars, *arrays, *outside)


def weight_scratch(count, depth, columns):
    return [pltpu.VMEM((count, depth, columns), BF16), pltpu.SemaphoreType.DMA((count,))]


VMEM_LIMIT = 20 * 1024 * 1024
WEIGHTS = dict(mixed_grad=0.0, forward=100.0, partial=0.0, query=100.0, key=100.0, weight=0.0)
STREAM_LIMIT = 54 * 1024 * 1024


def two_by_two():
    return lax.axis_size("head") == 2 and lax.axis_size("rep") == 2


def features_here(value):
    heads, reps = lax.axis_size("head"), lax.axis_size("rep")
    if two_by_two():
        h, r = lax.axis_index("head"), lax.axis_index("rep")
        places = [2 * h + r, 2 * h + 1 - r, 2 * (1 - h) + r, 2 * (1 - h) + 1 - r]
        rest = swap(value, "head")
        return [value, swap(value, "rep")], rest, jnp.stack(places).astype(jnp.int32)
    count = heads * reps
    gathered = lax.all_gather(value, ("head", "rep"), axis=0)
    blocks = [gathered[i] for i in range(count)]
    return blocks[: count // 2], blocks[count // 2 :], jnp.arange(count, dtype=jnp.int32)


def other_features(rest, *others):
    if two_by_two():
        return [rest, swap(after(rest, *others), "rep")]
    return rest


def attended_partial(mixed_heads, out_weight, places, estimate):
    if two_by_two():
        rows = mixed_heads.shape[0]
        share = out_weight.shape[0] // 4
        order = jnp.stack([places[1], places[3], places[0], places[2]])
        return kernel_call(
            functools.partial(partial_kernel, 1),
            "attended_partial",
            [order],
            [mixed_heads],
            [jax.ShapeDtypeStruct((2, rows, share), BF16)] * 2,
            estimate,
            [out_weight],
            weight_scratch(4, share, mixed_heads.shape[1]),
        )
    partial_value = lax.dot_general(mixed_heads, out_weight, NT, preferred_element_type=F32)
    return [partial_value.astype(BF16)]


def core_sum(partial_products):
    if len(partial_products) == 1:
        return partial_products
    keep, give = partial_products
    got = swap(give, "rep")
    return [
        keep[0].astype(F32) + got[0].astype(F32),
        (keep[1].astype(F32) + got[1].astype(F32)).astype(BF16),
    ]


def chip_sum(shares, *others):
    if len(shares) == 1:
        return lax.psum_scatter(shares[0], ("head", "rep"), scatter_dimension=1, tiled=True)
    return (shares[0] + swap(after(shares[1], *others), "head").astype(F32)).astype(BF16)


def per_device(queries, keys, values, out_weight, level_mask, cotangent):
    rows, columns = queries.shape
    features = out_weight.shape[0]
    heads = columns // HEAD_DIM
    heads_up = -(-heads // 8) * 8
    blocks = rows // BLOCK
    peers = lax.axis_size("seq")
    place = lax.axis_index("seq")
    tiles = seen_tiles(blocks, peers)
    distances = sorted({d for mine in tiles for d, _, _ in mine})
    count = len(distances)
    slot = {d: i for i, d in enumerate(distances)}
    tiles = [[(slot[d], b, level) for d, b, level in mine] for mine in tiles]
    pairs = sum(len(mine) for mine in tiles)
    attention_flops = 2 * heads * pairs * BLOCK * BLOCK * HEAD_DIM
    array_bytes = 2 * rows * columns
    exps = heads * pairs * BLOCK * BLOCK
    like_queries = jax.ShapeDtypeStruct((rows, columns), BF16)

    def further(got, sign, *others):
        near, far = distances[len(got) - 1], distances[len(got)]
        return got + [shift(after(got[-1], *others), sign * (far - near))]

    block_ids = place * blocks + jnp.arange(blocks, dtype=jnp.int32)
    offsets = 2 ** jnp.arange(LEVELS, dtype=jnp.int32)
    use = ((block_ids[:, None] >= offsets[None]) & (level_mask == 1)).astype(jnp.int32)
    use = use.reshape(-1)

    kv_all = further([jnp.concatenate([keys, values])], 1)
    query_all = further([queries], -1)
    c_blocks, c_rest, c_places = features_here(cotangent)
    half = len(c_blocks)
    part_cols = cotangent.shape[1]
    while len(query_all) < count:
        query_all = further(query_all, -1)
    mixed_sum = []
    for part in range(2):
        if part:
            c_blocks = c_blocks + other_features(c_rest, *mixed_sum)
        mine = slice(part * half, (part + 1) * half)
        mixed_sum = [
            kernel_call(
                functools.partial(mixed_grad_kernel, half, part),
                "mixed_grad",
                [c_places[mine]],
                [*mixed_sum, *c_blocks[mine]],
                jax.ShapeDtypeStruct((rows, columns), BF16 if part else F32),
                cost(rows * columns * features, columns * features, 0, WEIGHTS["mixed_grad"] * (1 - part)),
                [out_weight],
                weight_scratch(half, part_cols, columns),
            )
        ]
    mixed_grad = mixed_sum[0]
    group_count = len(c_blocks)
    while len(kv_all) < count:
        kv_all = further(kv_all, 1, mixed_grad)
    grad_all = further([mixed_grad], -1, query_all[-1])
    while len(grad_all) < count:
        grad_all = further(grad_all, -1)

    h, r = lax.axis_index("head"), lax.axis_index("rep")
    n_head, n_rep = lax.axis_size("head"), lax.axis_size("rep")
    step_of = lambda i: (i // n_rep) + n_head * (i % n_rep)
    wanted = (place + step_of(h * n_rep + r)) % peers
    out_block = c_blocks[0]
    for i in range(1, group_count):
        out_block = jnp.where(c_places[i] == wanted, c_blocks[i], out_block)
    links = []
    for s in range(peers):
        for q in range(group_count):
            links.append((s * group_count + q, ((s + step_of(q)) % peers) * group_count + q))
    arrived = lax.ppermute(after(out_block, grad_all[-1], kv_all[-1]), ("seq", "head", "rep"), links)

    mixed_heads, lse = kernel_call(
        functools.partial(forward_kernel, tiles, count, heads),
        "attention_forward",
        [use],
        [after(queries, query_all[-1], grad_all[-1]), *kv_all],
        [like_queries, jax.ShapeDtypeStruct((heads_up, rows), F32)],
        cost(2 * attention_flops, (2 * count + 2) * array_bytes, exps, WEIGHTS["forward"]),
    )

    near = {}
    if peers <= 4:
        near = {k: cyclic(mixed_heads, k) for k in sorted({1, peers - 1}) if 0 < k < peers}
    stats_shape = jax.ShapeDtypeStruct((2 * heads_up + 8, rows), F32)
    q_grad, stats = kernel_call(
        functools.partial(query_kernel, tiles, count, heads, heads_up),
        "attention_query_grad",
        [use],
        [after(queries, mixed_heads), mixed_grad, lse, *kv_all],
        [like_queries, stats_shape],
        cost(3 * attention_flops, (2 * count + 3) * array_bytes, exps, WEIGHTS["query"]),
    )
    stats_all = [stats] + [shift(stats, -d) for d in distances[1:]]
    partial_products = attended_partial(
        mixed_heads, out_weight, c_places, cost(2 * rows * columns * features, 2 * rows * features, 0, WEIGHTS["partial"])
    )
    shares = core_sum(partial_products)
    held = after(mixed_heads, arrived, *near.values(), *stats_all[1:], *shares)
    if peers <= 4:
        mixed_all = [mixed_heads] + [
            near[k] if k in near else cyclic(held, k) for k in range(1, peers)
        ]
    else:
        gathered = lax.all_gather(mixed_heads, "seq", axis=0)
        mixed_all = [
            lax.dynamic_index_in_dim(gathered, (place - k) % peers, 0, False)
            for k in range(peers)
        ]
    attended = chip_sum(shares, held)
    k_grad, v_grad = kernel_call(
        functools.partial(key_kernel, tiles, count, heads, heads_up),
        "attention_key_grad",
        [],
        [after(keys, held), values, *query_all, *grad_all, *stats_all],
        [like_queries] * 2,
        cost(4 * attention_flops, (2 * count + 4) * array_bytes, exps, WEIGHTS["key"]),
    )

    ct_blocks, ct_rest, _ = features_here(after(arrived, held))
    ct = jnp.stack(ct_blocks + other_features(ct_rest, k_grad))
    steps = step_of(c_places)
    ct_at = jnp.sum(
        jnp.where(steps[None] == jnp.arange(peers)[:, None], jnp.arange(group_count)[None], 0), 1
    ).astype(jnp.int32)
    early = sorted({0, 1, peers - 1}) if 2 < peers <= 4 else [0]
    late = [k for k in range(peers) if k not in early]
    weight_sum = []
    for part, which in enumerate((early, late)):
        if not which:
            weight_sum = [weight_sum[0].astype(BF16)]
            break
        ranges = [mixed_all[k] for k in which]
        if part:
            ranges[0] = after(ranges[0], attended, k_grad)
        weight_sum = [
            kernel_call(
                functools.partial(weight_grad_kernel, which, part),
                "weight_grad",
                [ct_at],
                [*weight_sum, ct, *ranges],
                jax.ShapeDtypeStruct((part_cols, columns), BF16 if part else F32),
                cost(2 * part_cols * columns * rows * len(which), array_bytes * len(which), 0, WEIGHTS["weight"]),
            )
        ]
    weight_grad = weight_sum[0]
    return (attended, q_grad, k_grad, v_grad, weight_grad)


def solution(mesh):
    shared = P(("groups", "seq"), ("head", "rep"))
    return jax.shard_map(
        per_device,
        mesh=mesh,
        in_specs=(shared, shared, shared, P(None, ("head", "rep")), P(("groups", "seq"), None), shared),
        out_specs=(shared,) * 5,
        check_vma=False,
    )
```

```python
import functools
import math

import jax
import jax.numpy as jnp
from jax import lax
from jax.experimental import pallas as pl
from jax.experimental.pallas import tpu as pltpu
from jax.sharding import PartitionSpec as P

HEAD_DIM = 128
BLOCK = 128
LEVELS = 5
SCALE = HEAD_DIM ** (-0.5)
LOG2_SCALE = SCALE * math.log2(math.e)
MASKED = -1e30

F32 = jnp.float32
BF16 = jnp.bfloat16
NT = (((1,), (1,)), ((), ()))
TN = (((0,), (0,)), ((), ()))


def shift(value, by):
    peers = lax.axis_size("seq")
    return lax.ppermute(
        value, "seq", [(i, i + by) for i in range(peers) if 0 <= i + by < peers]
    )


def cyclic(value, by):
    peers = lax.axis_size("seq")
    return lax.ppermute(value, "seq", [(i, (i + by) % peers) for i in range(peers)])


def swap(value, axis):
    return lax.ppermute(value, axis, [(0, 1), (1, 0)])


def dot(a, b):
    return jnp.dot(a, b, preferred_element_type=F32)


def dot_nt(a, b):
    return lax.dot_general(a, b, NT, preferred_element_type=F32)


def dot_tn(a, b):
    return lax.dot_general(a, b, TN, preferred_element_type=F32)


def after(value, *others):
    return lax.optimization_barrier((value, others))[0]


def seen_tiles(blocks, peers):
    tiles = []
    for n in range(blocks):
        mine = [(0, n, None)]
        for level in range(LEVELS):
            target = n - 2**level
            distance = -(target // blocks)
            if distance < peers:
                mine.append((distance, target % blocks, level))
        tiles.append(mine)
    return tiles


def block_rows(n):
    return pl.ds(n * BLOCK, BLOCK)


def head_cols(j):
    return slice(j * HEAD_DIM, (j + 1) * HEAD_DIM)


def cat(parts, axis=0):
    return parts[0] if len(parts) == 1 else jnp.concatenate(parts, axis)


def causal_tile():
    rows = lax.broadcasted_iota(jnp.int32, (BLOCK, BLOCK), 0)
    cols = lax.broadcasted_iota(jnp.int32, (BLOCK, BLOCK), 1)
    return rows <= cols


def forward_kernel(tiles, count, heads, use_ref, q_ref, *refs):
    kv_refs = refs[:count]
    mixed_ref, lse_ref = refs[count:]
    blocks = len(tiles)
    causal = causal_tile()
    for n, mine in enumerate(tiles):
        rows = block_rows(n)
        for j in range(heads):
            cols = head_cols(j)
            keys = cat([kv_refs[d][block_rows(b), cols] for d, b, _ in mine])
            vals = cat([kv_refs[d][block_rows(blocks + b), cols] for d, b, _ in mine])
            raw = dot_nt(keys, q_ref[rows, cols])
            parts = []
            for i, (_, _, level) in enumerate(mine):
                part = raw[i * BLOCK : (i + 1) * BLOCK]
                if level is None:
                    part = jnp.where(causal, part, MASKED)
                else:
                    part = part + jnp.where(use_ref[n * LEVELS + level] == 1, 0.0, MASKED)
                parts.append(part)
            top = jnp.max(functools.reduce(jnp.maximum, parts), 0, keepdims=True) * LOG2_SCALE
            grown = [jnp.exp2(part * LOG2_SCALE - top) for part in parts]
            total = jnp.sum(functools.reduce(jnp.add, grown), 0, keepdims=True)
            share = 1.0 / total
            prob = cat([(part * share).astype(BF16) for part in grown])
            mixed_ref[rows, cols] = dot_tn(prob, vals).astype(BF16)
            lse_ref[j : j + 1, rows] = top + jnp.log2(total)


def query_kernel(tiles, count, heads, heads_up, use_ref, q_ref, g_ref, lse_ref, *refs):
    kv_refs = refs[:count]
    dq_ref, stats_ref = refs[count:]
    blocks = len(tiles)
    causal = causal_tile()
    for n, mine in enumerate(tiles):
        rows = block_rows(n)
        for j in range(heads):
            cols = head_cols(j)
            keys = cat([kv_refs[d][block_rows(b), cols] for d, b, _ in mine])
            vals = cat([kv_refs[d][block_rows(blocks + b), cols] for d, b, _ in mine])
            lse = lse_ref[j : j + 1, rows]
            raw = dot_nt(keys, q_ref[rows, cols])
            prob_grad = dot_nt(vals, g_ref[rows, cols])
            probs, weighted = [], None
            for i, (_, _, level) in enumerate(mine):
                here = slice(i * BLOCK, (i + 1) * BLOCK)
                if level is None:
                    logits = jnp.where(causal, raw[here] * LOG2_SCALE - lse, MASKED)
                else:
                    off = lse + jnp.where(use_ref[n * LEVELS + level] == 1, 0.0, -MASKED)
                    logits = raw[here] * LOG2_SCALE - off
                prob = jnp.exp2(logits)
                probs.append(prob)
                part = prob * prob_grad[here]
                weighted = part if weighted is None else weighted + part
            delta = jnp.sum(weighted, 0, keepdims=True)
            score_grad = [
                (prob * SCALE * (prob_grad[i * BLOCK : (i + 1) * BLOCK] - delta)).astype(BF16)
                for i, prob in enumerate(probs)
            ]
            dq_ref[rows, cols] = dot_tn(cat(score_grad), keys).astype(BF16)
            stats_ref[j : j + 1, rows] = lse
            stats_ref[heads_up + j : heads_up + j + 1, rows] = delta
        flags = jnp.zeros((8, BLOCK), F32)
        level_row = lax.broadcasted_iota(jnp.int32, (8, BLOCK), 0)
        for level in range(LEVELS):
            flag = jnp.where(use_ref[n * LEVELS + level] == 1, 1.0, 0.0)
            flags = jnp.where(level_row == level, flag, flags)
        stats_ref[2 * heads_up :, rows] = flags
    for row in range(heads, heads_up):
        for first in (0, heads_up):
            stats_ref[first + row : first + row + 1, :] = jnp.zeros((1, stats_ref.shape[1]), F32)


def key_kernel(tiles, count, heads, heads_up, k_ref, v_ref, *refs):
    q_refs, g_refs, s_refs = refs[:count], refs[count : 2 * count], refs[2 * count : 3 * count]
    dk_ref, dv_ref = refs[3 * count :]
    causal = causal_tile()
    for b in range(len(tiles)):
        rows = block_rows(b)
        seers = [
            (d, n, level)
            for n, mine in enumerate(tiles)
            for d, block, level in mine
            if block == b
        ]
        for j in range(heads):
            cols = head_cols(j)
            ques = cat([q_refs[d][block_rows(n), cols] for d, n, _ in seers])
            grads = cat([g_refs[d][block_rows(n), cols] for d, n, _ in seers])
            raw = dot_nt(k_ref[rows, cols], ques)
            prob_grad = dot_nt(v_ref[rows, cols], grads)
            probs, score_grads = [], []
            for i, (d, n, level) in enumerate(seers):
                here = slice(i * BLOCK, (i + 1) * BLOCK)
                lse = s_refs[d][j : j + 1, block_rows(n)]
                delta = s_refs[d][heads_up + j : heads_up + j + 1, block_rows(n)]
                if level is None:
                    logits = jnp.where(causal, raw[:, here] * LOG2_SCALE - lse, MASKED)
                else:
                    row = 2 * heads_up + level
                    off = lse + (1.0 - s_refs[d][row : row + 1, block_rows(n)]) * (-MASKED)
                    logits = raw[:, here] * LOG2_SCALE - off
                prob = jnp.exp2(logits)
                probs.append(prob.astype(BF16))
                score_grads.append((prob * SCALE * (prob_grad[:, here] - delta)).astype(BF16))
            dv_ref[rows, cols] = dot(cat(probs, 1), grads).astype(BF16)
            dk_ref[rows, cols] = dot(cat(score_grads, 1), ques).astype(BF16)


class Stream:
    def __init__(self, pieces, held, sems):
        self.held = held
        self.copies = [
            pltpu.make_async_copy(piece, held.at[i], sems.at[i]) for i, piece in enumerate(pieces)
        ]
        for copy in self.copies[:2]:
            copy.start()

    def piece(self, i):
        self.copies[i].wait()
        if i + 2 < len(self.copies):
            self.copies[i + 2].start()
        return self.held.at[i]


def mixed_grad_kernel(count, given, place_ref, *refs):
    total = refs[0][...] if given else None
    c_refs, w_ref, out_ref, held, sems = refs[given : given + count], *refs[given + count :]
    depth = c_refs[0].shape[1]
    firsts = [pl.multiple_of(place_ref[i] * depth, depth) for i in range(count)]
    stream = Stream([w_ref.at[pl.ds(first, depth), :] for first in firsts], held, sems)
    for i in range(count):
        step = dot(c_refs[i][...], stream.piece(i)[...])
        total = step if total is None else total + step
    out_ref[...] = total.astype(out_ref.dtype)


def partial_kernel(split, place_ref, m_ref, w_ref, keep_ref, give_ref, held, sems):
    depth = keep_ref.shape[2]
    height = depth // split
    firsts = [place_ref[i] * depth + part * height for i in range(4) for part in range(split)]
    pieces = [w_ref.at[pl.ds(pl.multiple_of(first, height), height), :] for first in firsts]
    stream = Stream(pieces, held, sems)
    outs = [(give_ref, 0), (give_ref, 1), (keep_ref, 0), (keep_ref, 1)]
    for i, (out_ref, at) in enumerate(outs):
        for part in range(split):
            piece = stream.piece(i * split + part)
            cols = slice(part * height, (part + 1) * height)
            out_ref[at, :, cols] = dot_nt(m_ref[...], piece[...]).astype(BF16)


def weight_grad_kernel(which, given, place_ref, *refs):
    c_ref, m_refs, out_ref = refs[given], refs[given + 1 : -1], refs[-1]
    features = out_ref.shape[0]
    height = min(512, features)
    for first in range(0, features, height):
        rows = slice(first, first + height)
        total = refs[0][rows, :] if given else None
        for p, m_ref in zip(which, m_refs):
            part = dot_tn(c_ref[place_ref[p], :, rows], m_ref[...])
            total = part if total is None else total + part
        out_ref[rows, :] = total.astype(out_ref.dtype)


def cost(flops, bytes_accessed, exps=0, weight=1.0):
    return pl.CostEstimate(
        flops=int(flops * weight),
        bytes_accessed=int(bytes_accessed * weight),
        transcendentals=int(exps * weight),
    )


def kernel_call(body, name, scalars, arrays, out_shape, estimate, outside=(), scratch=()):
    smem = pl.BlockSpec(memory_space=pltpu.SMEM)
    vmem = pl.BlockSpec(memory_space=pltpu.VMEM)
    return pl.pallas_call(
        body,
        in_specs=[smem] * len(scalars)
        + [vmem] * len(arrays)
        + [pl.BlockSpec(memory_space=pltpu.HBM)] * len(outside),
        out_specs=jax.tree.map(lambda _: vmem, out_shape),
        out_shape=out_shape,
        scratch_shapes=list(scratch),
        compiler_params=pltpu.CompilerParams(
            vmem_limit_bytes=STREAM_LIMIT if outside else VMEM_LIMIT
        ),
        cost_estimate=estimate,
        name=name,
    )(*scalars, *arrays, *outside)


def weight_scratch(count, depth, columns):
    return [pltpu.VMEM((count, depth, columns), BF16), pltpu.SemaphoreType.DMA((count,))]


VMEM_LIMIT = 20 * 1024 * 1024
WEIGHTS = dict(mixed_grad=0.0, forward=100.0, partial=0.0, query=100.0, key=100.0, weight=0.0)
STREAM_LIMIT = 54 * 1024 * 1024


def two_by_two():
    return lax.axis_size("head") == 2 and lax.axis_size("rep") == 2


def features_here(value):
    heads, reps = lax.axis_size("head"), lax.axis_size("rep")
    if two_by_two():
        h, r = lax.axis_index("head"), lax.axis_index("rep")
        places = [2 * h + r, 2 * h + 1 - r, 2 * (1 - h) + r, 2 * (1 - h) + 1 - r]
        rest = swap(value, "head")
        return [value, swap(value, "rep")], rest, jnp.stack(places).astype(jnp.int32)
    count = heads * reps
    gathered = lax.all_gather(value, ("head", "rep"), axis=0)
    blocks = [gathered[i] for i in range(count)]
    return blocks[: count // 2], blocks[count // 2 :], jnp.arange(count, dtype=jnp.int32)


def other_features(rest, *others):
    if two_by_two():
        return [rest, swap(after(rest, *others), "rep")]
    return rest


def attended_partial(mixed_heads, out_weight, places, estimate):
    if two_by_two():
        rows = mixed_heads.shape[0]
        share = out_weight.shape[0] // 4
        order = jnp.stack([places[1], places[3], places[0], places[2]])
        return kernel_call(
            functools.partial(partial_kernel, 1),
            "attended_partial",
            [order],
            [mixed_heads],
            [jax.ShapeDtypeStruct((2, rows, share), BF16)] * 2,
            estimate,
            [out_weight],
            weight_scratch(4, share, mixed_heads.shape[1]),
        )
    partial_value = lax.dot_general(mixed_heads, out_weight, NT, preferred_element_type=F32)
    return [partial_value.astype(BF16)]


def core_sum(partial_products):
    if len(partial_products) == 1:
        return partial_products
    keep, give = partial_products
    got = swap(give, "rep")
    return [
        keep[0].astype(F32) + got[0].astype(F32),
        (keep[1].astype(F32) + got[1].astype(F32)).astype(BF16),
    ]


def chip_sum(shares, *others):
    if len(shares) == 1:
        return lax.psum_scatter(shares[0], ("head", "rep"), scatter_dimension=1, tiled=True)
    return (shares[0] + swap(after(shares[1], *others), "head").astype(F32)).astype(BF16)


def per_device(queries, keys, values, out_weight, level_mask, cotangent):
    rows, columns = queries.shape
    features = out_weight.shape[0]
    heads = columns // HEAD_DIM
    heads_up = -(-heads // 8) * 8
    blocks = rows // BLOCK
    peers = lax.axis_size("seq")
    place = lax.axis_index("seq")
    tiles = seen_tiles(blocks, peers)
    distances = sorted({d for mine in tiles for d, _, _ in mine})
    count = len(distances)
    slot = {d: i for i, d in enumerate(distances)}
    tiles = [[(slot[d], b, level) for d, b, level in mine] for mine in tiles]
    pairs = sum(len(mine) for mine in tiles)
    attention_flops = 2 * heads * pairs * BLOCK * BLOCK * HEAD_DIM
    array_bytes = 2 * rows * columns
    exps = heads * pairs * BLOCK * BLOCK
    like_queries = jax.ShapeDtypeStruct((rows, columns), BF16)

    def further(got, sign, *others):
        near, far = distances[len(got) - 1], distances[len(got)]
        return got + [shift(after(got[-1], *others), sign * (far - near))]

    block_ids = place * blocks + jnp.arange(blocks, dtype=jnp.int32)
    offsets = 2 ** jnp.arange(LEVELS, dtype=jnp.int32)
    use = ((block_ids[:, None] >= offsets[None]) & (level_mask == 1)).astype(jnp.int32)
    use = use.reshape(-1)

    kv_all = further([jnp.concatenate([keys, values])], 1)
    query_all = further([queries], -1)
    c_blocks, c_rest, c_places = features_here(cotangent)
    half = len(c_blocks)
    part_cols = cotangent.shape[1]
    while len(query_all) < count:
        query_all = further(query_all, -1)
    mixed_sum = []
    for part in range(2):
        if part:
            c_blocks = c_blocks + other_features(c_rest, *mixed_sum)
        mine = slice(part * half, (part + 1) * half)
        mixed_sum = [
            kernel_call(
                functools.partial(mixed_grad_kernel, half, part),
                "mixed_grad",
                [c_places[mine]],
                [*mixed_sum, *c_blocks[mine]],
                jax.ShapeDtypeStruct((rows, columns), BF16 if part else F32),
                cost(rows * columns * features, columns * features, 0, WEIGHTS["mixed_grad"] * (1 - part)),
                [out_weight],
                weight_scratch(half, part_cols, columns),
            )
        ]
    mixed_grad = mixed_sum[0]
    group_count = len(c_blocks)
    while len(kv_all) < count:
        kv_all = further(kv_all, 1, mixed_grad)
    grad_all = further([mixed_grad], -1)
    while len(grad_all) < count:
        grad_all = further(grad_all, -1, query_all[-1])

    h, r = lax.axis_index("head"), lax.axis_index("rep")
    n_head, n_rep = lax.axis_size("head"), lax.axis_size("rep")
    step_of = lambda i: (i // n_rep) + n_head * (i % n_rep)
    wanted = (place + step_of(h * n_rep + r)) % peers
    out_block = c_blocks[0]
    for i in range(1, group_count):
        out_block = jnp.where(c_places[i] == wanted, c_blocks[i], out_block)
    links = []
    for s in range(peers):
        for q in range(group_count):
            links.append((s * group_count + q, ((s + step_of(q)) % peers) * group_count + q))
    arrived = lax.ppermute(after(out_block, grad_all[-1], kv_all[-1]), ("seq", "head", "rep"), links)

    mixed_heads, lse = kernel_call(
        functools.partial(forward_kernel, tiles, count, heads),
        "attention_forward",
        [use],
        [after(queries, query_all[-1], grad_all[-1]), *kv_all],
        [like_queries, jax.ShapeDtypeStruct((heads_up, rows), F32)],
        cost(2 * attention_flops, (2 * count + 2) * array_bytes, exps, WEIGHTS["forward"]),
    )

    near = {}
    if peers <= 4:
        near = {k: cyclic(mixed_heads, k) for k in sorted({1, peers - 1}) if 0 < k < peers}
    stats_shape = jax.ShapeDtypeStruct((2 * heads_up + 8, rows), F32)
    q_grad, stats = kernel_call(
        functools.partial(query_kernel, tiles, count, heads, heads_up),
        "attention_query_grad",
        [use],
        [after(queries, mixed_heads), mixed_grad, lse, *kv_all],
        [like_queries, stats_shape],
        cost(3 * attention_flops, (2 * count + 3) * array_bytes, exps, WEIGHTS["query"]),
    )
    stats_all = [stats] + [shift(stats, -d) for d in distances[1:]]
    partial_products = attended_partial(
        mixed_heads, out_weight, c_places, cost(2 * rows * columns * features, 2 * rows * features, 0, WEIGHTS["partial"])
    )
    shares = core_sum(partial_products)
    held = after(mixed_heads, arrived, *near.values(), *stats_all[1:], *shares)
    if peers <= 4:
        mixed_all = [mixed_heads] + [
            near[k] if k in near else cyclic(held, k) for k in range(1, peers)
        ]
    else:
        gathered = lax.all_gather(mixed_heads, "seq", axis=0)
        mixed_all = [
            lax.dynamic_index_in_dim(gathered, (place - k) % peers, 0, False)
            for k in range(peers)
        ]
    attended = chip_sum(shares, held)
    k_grad, v_grad = kernel_call(
        functools.partial(key_kernel, tiles, count, heads, heads_up),
        "attention_key_grad",
        [],
        [after(keys, held), values, *query_all, *grad_all, *stats_all],
        [like_queries] * 2,
        cost(4 * attention_flops, (2 * count + 4) * array_bytes, exps, WEIGHTS["key"]),
    )

    ct_blocks, ct_rest, _ = features_here(after(arrived, held))
    ct = jnp.stack(ct_blocks + other_features(ct_rest, k_grad))
    steps = step_of(c_places)
    ct_at = jnp.sum(
        jnp.where(steps[None] == jnp.arange(peers)[:, None], jnp.arange(group_count)[None], 0), 1
    ).astype(jnp.int32)
    early = sorted({0, 1, peers - 1}) if 2 < peers <= 4 else [0]
    late = [k for k in range(peers) if k not in early]
    weight_sum = []
    for part, which in enumerate((early, late)):
        if not which:
            weight_sum = [weight_sum[0].astype(BF16)]
            break
        ranges = [mixed_all[k] for k in which]
        if part:
            ranges[0] = after(ranges[0], attended, k_grad)
        weight_sum = [
            kernel_call(
                functools.partial(weight_grad_kernel, which, part),
                "weight_grad",
                [ct_at],
                [*weight_sum, ct, *ranges],
                jax.ShapeDtypeStruct((part_cols, columns), BF16 if part else F32),
                cost(2 * part_cols * columns * rows * len(which), array_bytes * len(which), 0, WEIGHTS["weight"]),
            )
        ]
    weight_grad = weight_sum[0]
    return (attended, q_grad, k_grad, v_grad, weight_grad)


def solution(mesh):
    shared = P(("groups", "seq"), ("head", "rep"))
    return jax.shard_map(
        per_device,
        mesh=mesh,
        in_specs=(shared, shared, shared, P(None, ("head", "rep")), P(("groups", "seq"), None), shared),
        out_specs=(shared,) * 5,
        check_vma=False,
    )
```

```python
import functools
import math

import jax
import jax.numpy as jnp
from jax import lax
from jax.experimental import pallas as pl
from jax.experimental.pallas import tpu as pltpu
from jax.sharding import PartitionSpec as P

HEAD_DIM = 128
BLOCK = 128
LEVELS = 5
SCALE = HEAD_DIM ** (-0.5)
LOG2_SCALE = SCALE * math.log2(math.e)
MASKED = -1e30

F32 = jnp.float32
BF16 = jnp.bfloat16
NT = (((1,), (1,)), ((), ()))
TN = (((0,), (0,)), ((), ()))


def shift(value, by):
    peers = lax.axis_size("seq")
    return lax.ppermute(
        value, "seq", [(i, i + by) for i in range(peers) if 0 <= i + by < peers]
    )


def cyclic(value, by):
    peers = lax.axis_size("seq")
    return lax.ppermute(value, "seq", [(i, (i + by) % peers) for i in range(peers)])


def swap(value, axis):
    return lax.ppermute(value, axis, [(0, 1), (1, 0)])


def dot(a, b):
    return jnp.dot(a, b, preferred_element_type=F32)


def dot_nt(a, b):
    return lax.dot_general(a, b, NT, preferred_element_type=F32)


def dot_tn(a, b):
    return lax.dot_general(a, b, TN, preferred_element_type=F32)


def after(value, *others):
    return lax.optimization_barrier((value, others))[0]


def seen_tiles(blocks, peers):
    tiles = []
    for n in range(blocks):
        mine = [(0, n, None)]
        for level in range(LEVELS):
            target = n - 2**level
            distance = -(target // blocks)
            if distance < peers:
                mine.append((distance, target % blocks, level))
        tiles.append(mine)
    return tiles


def block_rows(n):
    return pl.ds(n * BLOCK, BLOCK)


def head_cols(j):
    return slice(j * HEAD_DIM, (j + 1) * HEAD_DIM)


def cat(parts, axis=0):
    return parts[0] if len(parts) == 1 else jnp.concatenate(parts, axis)


def causal_tile():
    rows = lax.broadcasted_iota(jnp.int32, (BLOCK, BLOCK), 0)
    cols = lax.broadcasted_iota(jnp.int32, (BLOCK, BLOCK), 1)
    return rows <= cols


def forward_kernel(tiles, count, heads, use_ref, q_ref, *refs):
    kv_refs = refs[:count]
    mixed_ref, lse_ref = refs[count:]
    blocks = len(tiles)
    causal = causal_tile()
    for n, mine in enumerate(tiles):
        rows = block_rows(n)
        for j in range(heads):
            cols = head_cols(j)
            keys = cat([kv_refs[d][block_rows(b), cols] for d, b, _ in mine])
            vals = cat([kv_refs[d][block_rows(blocks + b), cols] for d, b, _ in mine])
            raw = dot_nt(keys, q_ref[rows, cols])
            parts = []
            for i, (_, _, level) in enumerate(mine):
                part = raw[i * BLOCK : (i + 1) * BLOCK]
                if level is None:
                    part = jnp.where(causal, part, MASKED)
                else:
                    part = part + jnp.where(use_ref[n * LEVELS + level] == 1, 0.0, MASKED)
                parts.append(part)
            top = jnp.max(functools.reduce(jnp.maximum, parts), 0, keepdims=True) * LOG2_SCALE
            grown = [jnp.exp2(part * LOG2_SCALE - top) for part in parts]
            total = jnp.sum(functools.reduce(jnp.add, grown), 0, keepdims=True)
            share = 1.0 / total
            prob = cat([(part * share).astype(BF16) for part in grown])
            mixed_ref[rows, cols] = dot_tn(prob, vals).astype(BF16)
            lse_ref[j : j + 1, rows] = top + jnp.log2(total)


def query_kernel(tiles, count, heads, heads_up, use_ref, q_ref, g_ref, lse_ref, *refs):
    kv_refs = refs[:count]
    dq_ref, stats_ref = refs[count:]
    blocks = len(tiles)
    causal = causal_tile()
    for n, mine in enumerate(tiles):
        rows = block_rows(n)
        for j in range(heads):
            cols = head_cols(j)
            keys = cat([kv_refs[d][block_rows(b), cols] for d, b, _ in mine])
            vals = cat([kv_refs[d][block_rows(blocks + b), cols] for d, b, _ in mine])
            lse = lse_ref[j : j + 1, rows]
            raw = dot_nt(keys, q_ref[rows, cols])
            prob_grad = dot_nt(vals, g_ref[rows, cols])
            probs, weighted = [], None
            for i, (_, _, level) in enumerate(mine):
                here = slice(i * BLOCK, (i + 1) * BLOCK)
                if level is None:
                    logits = jnp.where(causal, raw[here] * LOG2_SCALE - lse, MASKED)
                else:
                    off = lse + jnp.where(use_ref[n * LEVELS + level] == 1, 0.0, -MASKED)
                    logits = raw[here] * LOG2_SCALE - off
                prob = jnp.exp2(logits)
                probs.append(prob)
                part = prob * prob_grad[here]
                weighted = part if weighted is None else weighted + part
            delta = jnp.sum(weighted, 0, keepdims=True)
            score_grad = [
                (prob * SCALE * (prob_grad[i * BLOCK : (i + 1) * BLOCK] - delta)).astype(BF16)
                for i, prob in enumerate(probs)
            ]
            dq_ref[rows, cols] = dot_tn(cat(score_grad), keys).astype(BF16)
            stats_ref[j : j + 1, rows] = lse
            stats_ref[heads_up + j : heads_up + j + 1, rows] = delta
        flags = jnp.zeros((8, BLOCK), F32)
        level_row = lax.broadcasted_iota(jnp.int32, (8, BLOCK), 0)
        for level in range(LEVELS):
            flag = jnp.where(use_ref[n * LEVELS + level] == 1, 1.0, 0.0)
            flags = jnp.where(level_row == level, flag, flags)
        stats_ref[2 * heads_up :, rows] = flags
    for row in range(heads, heads_up):
        for first in (0, heads_up):
            stats_ref[first + row : first + row + 1, :] = jnp.zeros((1, stats_ref.shape[1]), F32)


def key_kernel(tiles, count, heads, heads_up, k_ref, v_ref, *refs):
    q_refs, g_refs, s_refs = refs[:count], refs[count : 2 * count], refs[2 * count : 3 * count]
    dk_ref, dv_ref = refs[3 * count :]
    causal = causal_tile()
    for b in range(len(tiles)):
        rows = block_rows(b)
        seers = [
            (d, n, level)
            for n, mine in enumerate(tiles)
            for d, block, level in mine
            if block == b
        ]
        for j in range(heads):
            cols = head_cols(j)
            ques = cat([q_refs[d][block_rows(n), cols] for d, n, _ in seers])
            grads = cat([g_refs[d][block_rows(n), cols] for d, n, _ in seers])
            raw = dot_nt(k_ref[rows, cols], ques)
            prob_grad = dot_nt(v_ref[rows, cols], grads)
            probs, score_grads = [], []
            for i, (d, n, level) in enumerate(seers):
                here = slice(i * BLOCK, (i + 1) * BLOCK)
                lse = s_refs[d][j : j + 1, block_rows(n)]
                delta = s_refs[d][heads_up + j : heads_up + j + 1, block_rows(n)]
                if level is None:
                    logits = jnp.where(causal, raw[:, here] * LOG2_SCALE - lse, MASKED)
                else:
                    row = 2 * heads_up + level
                    off = lse + (1.0 - s_refs[d][row : row + 1, block_rows(n)]) * (-MASKED)
                    logits = raw[:, here] * LOG2_SCALE - off
                prob = jnp.exp2(logits)
                probs.append(prob.astype(BF16))
                score_grads.append((prob * SCALE * (prob_grad[:, here] - delta)).astype(BF16))
            dv_ref[rows, cols] = dot(cat(probs, 1), grads).astype(BF16)
            dk_ref[rows, cols] = dot(cat(score_grads, 1), ques).astype(BF16)


class Stream:
    def __init__(self, pieces, held, sems):
        self.held = held
        self.copies = [
            pltpu.make_async_copy(piece, held.at[i], sems.at[i]) for i, piece in enumerate(pieces)
        ]
        for copy in self.copies[:2]:
            copy.start()

    def piece(self, i):
        self.copies[i].wait()
        if i + 2 < len(self.copies):
            self.copies[i + 2].start()
        return self.held.at[i]


def mixed_grad_kernel(count, given, place_ref, *refs):
    total = refs[0][...] if given else None
    c_refs, w_ref, out_ref, held, sems = refs[given : given + count], *refs[given + count :]
    depth = c_refs[0].shape[1]
    firsts = [pl.multiple_of(place_ref[i] * depth, depth) for i in range(count)]
    stream = Stream([w_ref.at[pl.ds(first, depth), :] for first in firsts], held, sems)
    for i in range(count):
        step = dot(c_refs[i][...], stream.piece(i)[...])
        total = step if total is None else total + step
    out_ref[...] = total.astype(out_ref.dtype)


def partial_kernel(split, place_ref, m_ref, w_ref, keep_ref, give_ref, held, sems):
    depth = keep_ref.shape[2]
    height = depth // split
    firsts = [place_ref[i] * depth + part * height for i in range(4) for part in range(split)]
    pieces = [w_ref.at[pl.ds(pl.multiple_of(first, height), height), :] for first in firsts]
    stream = Stream(pieces, held, sems)
    outs = [(give_ref, 0), (give_ref, 1), (keep_ref, 0), (keep_ref, 1)]
    for i, (out_ref, at) in enumerate(outs):
        for part in range(split):
            piece = stream.piece(i * split + part)
            cols = slice(part * height, (part + 1) * height)
            out_ref[at, :, cols] = dot_nt(m_ref[...], piece[...]).astype(BF16)


def weight_grad_kernel(which, given, place_ref, *refs):
    c_ref, m_refs, out_ref = refs[given], refs[given + 1 : -1], refs[-1]
    features = out_ref.shape[0]
    height = min(512, features)
    for first in range(0, features, height):
        rows = slice(first, first + height)
        total = refs[0][rows, :] if given else None
        for p, m_ref in zip(which, m_refs):
            part = dot_tn(c_ref[place_ref[p], :, rows], m_ref[...])
            total = part if total is None else total + part
        out_ref[rows, :] = total.astype(out_ref.dtype)


def cost(flops, bytes_accessed, exps=0, weight=1.0):
    return pl.CostEstimate(
        flops=int(flops * weight),
        bytes_accessed=int(bytes_accessed * weight),
        transcendentals=int(exps * weight),
    )


def kernel_call(body, name, scalars, arrays, out_shape, estimate, outside=(), scratch=()):
    smem = pl.BlockSpec(memory_space=pltpu.SMEM)
    vmem = pl.BlockSpec(memory_space=pltpu.VMEM)
    return pl.pallas_call(
        body,
        in_specs=[smem] * len(scalars)
        + [vmem] * len(arrays)
        + [pl.BlockSpec(memory_space=pltpu.HBM)] * len(outside),
        out_specs=jax.tree.map(lambda _: vmem, out_shape),
        out_shape=out_shape,
        scratch_shapes=list(scratch),
        compiler_params=pltpu.CompilerParams(
            vmem_limit_bytes=STREAM_LIMIT if outside else VMEM_LIMIT
        ),
        cost_estimate=estimate,
        name=name,
    )(*scalars, *arrays, *outside)


def weight_scratch(count, depth, columns):
    return [pltpu.VMEM((count, depth, columns), BF16), pltpu.SemaphoreType.DMA((count,))]


VMEM_LIMIT = 20 * 1024 * 1024
WEIGHTS = dict(mixed_grad=0.0, forward=0.0, partial=0.0, query=100.0, key=100.0, weight=0.0)
STREAM_LIMIT = 54 * 1024 * 1024


def two_by_two():
    return lax.axis_size("head") == 2 and lax.axis_size("rep") == 2


def features_here(value):
    heads, reps = lax.axis_size("head"), lax.axis_size("rep")
    if two_by_two():
        h, r = lax.axis_index("head"), lax.axis_index("rep")
        places = [2 * h + r, 2 * h + 1 - r, 2 * (1 - h) + r, 2 * (1 - h) + 1 - r]
        rest = swap(value, "head")
        return [value, swap(value, "rep")], rest, jnp.stack(places).astype(jnp.int32)
    count = heads * reps
    gathered = lax.all_gather(value, ("head", "rep"), axis=0)
    blocks = [gathered[i] for i in range(count)]
    return blocks[: count // 2], blocks[count // 2 :], jnp.arange(count, dtype=jnp.int32)


def other_features(rest, *others):
    if two_by_two():
        return [rest, swap(after(rest, *others), "rep")]
    return rest


def attended_partial(mixed_heads, out_weight, places, estimate):
    if two_by_two():
        rows = mixed_heads.shape[0]
        share = out_weight.shape[0] // 4
        order = jnp.stack([places[1], places[3], places[0], places[2]])
        return kernel_call(
            functools.partial(partial_kernel, 1),
            "attended_partial",
            [order],
            [mixed_heads],
            [jax.ShapeDtypeStruct((2, rows, share), BF16)] * 2,
            estimate,
            [out_weight],
            weight_scratch(4, share, mixed_heads.shape[1]),
        )
    partial_value = lax.dot_general(mixed_heads, out_weight, NT, preferred_element_type=F32)
    return [partial_value.astype(BF16)]


def core_sum(partial_products):
    if len(partial_products) == 1:
        return partial_products
    keep, give = partial_products
    got = swap(give, "rep")
    return [
        keep[0].astype(F32) + got[0].astype(F32),
        (keep[1].astype(F32) + got[1].astype(F32)).astype(BF16),
    ]


def chip_sum(shares, *others):
    if len(shares) == 1:
        return lax.psum_scatter(shares[0], ("head", "rep"), scatter_dimension=1, tiled=True)
    return (shares[0] + swap(after(shares[1], *others), "head").astype(F32)).astype(BF16)


def per_device(queries, keys, values, out_weight, level_mask, cotangent):
    rows, columns = queries.shape
    features = out_weight.shape[0]
    heads = columns // HEAD_DIM
    heads_up = -(-heads // 8) * 8
    blocks = rows // BLOCK
    peers = lax.axis_size("seq")
    place = lax.axis_index("seq")
    tiles = seen_tiles(blocks, peers)
    distances = sorted({d for mine in tiles for d, _, _ in mine})
    count = len(distances)
    slot = {d: i for i, d in enumerate(distances)}
    tiles = [[(slot[d], b, level) for d, b, level in mine] for mine in tiles]
    pairs = sum(len(mine) for mine in tiles)
    attention_flops = 2 * heads * pairs * BLOCK * BLOCK * HEAD_DIM
    array_bytes = 2 * rows * columns
    exps = heads * pairs * BLOCK * BLOCK
    like_queries = jax.ShapeDtypeStruct((rows, columns), BF16)

    def further(got, sign, *others):
        near, far = distances[len(got) - 1], distances[len(got)]
        return got + [shift(after(got[-1], *others), sign * (far - near))]

    block_ids = place * blocks + jnp.arange(blocks, dtype=jnp.int32)
    offsets = 2 ** jnp.arange(LEVELS, dtype=jnp.int32)
    use = ((block_ids[:, None] >= offsets[None]) & (level_mask == 1)).astype(jnp.int32)
    use = use.reshape(-1)

    kv_all = further([jnp.concatenate([keys, values])], 1)
    query_all = further([queries], -1)
    c_blocks, c_rest, c_places = features_here(cotangent)
    half = len(c_blocks)
    part_cols = cotangent.shape[1]
    mixed_sum = []
    for part in range(2):
        if part:
            c_blocks = c_blocks + other_features(c_rest, *mixed_sum, query_all[1])
        mine = slice(part * half, (part + 1) * half)
        mixed_sum = [
            kernel_call(
                functools.partial(mixed_grad_kernel, half, part),
                "mixed_grad",
                [c_places[mine]],
                [*mixed_sum, *c_blocks[mine]],
                jax.ShapeDtypeStruct((rows, columns), BF16 if part else F32),
                cost(rows * columns * features, columns * features, 0, WEIGHTS["mixed_grad"] * (1 - part)),
                [out_weight],
                weight_scratch(half, part_cols, columns),
            )
        ]
    mixed_grad = mixed_sum[0]
    group_count = len(c_blocks)
    while len(kv_all) < count:
        kv_all = further(kv_all, 1, mixed_grad)
    grad_all = further([mixed_grad], -1)
    while len(query_all) < count:
        query_all = further(query_all, -1, mixed_grad)
    while len(grad_all) < count:
        grad_all = further(grad_all, -1)

    h, r = lax.axis_index("head"), lax.axis_index("rep")
    n_head, n_rep = lax.axis_size("head"), lax.axis_size("rep")
    step_of = lambda i: (i // n_rep) + n_head * (i % n_rep)
    wanted = (place + step_of(h * n_rep + r)) % peers
    out_block = c_blocks[0]
    for i in range(1, group_count):
        out_block = jnp.where(c_places[i] == wanted, c_blocks[i], out_block)
    links = []
    for s in range(peers):
        for q in range(group_count):
            links.append((s * group_count + q, ((s + step_of(q)) % peers) * group_count + q))
    arrived = lax.ppermute(after(out_block, grad_all[1], kv_all[-1]), ("seq", "head", "rep"), links)

    mixed_heads, lse = kernel_call(
        functools.partial(forward_kernel, tiles, count, heads),
        "attention_forward",
        [use],
        [queries, *kv_all],
        [like_queries, jax.ShapeDtypeStruct((heads_up, rows), F32)],
        cost(2 * attention_flops, (2 * count + 2) * array_bytes, exps, WEIGHTS["forward"]),
    )

    near = {}
    if peers <= 4:
        near = {k: cyclic(mixed_heads, k) for k in sorted({1, peers - 1}) if 0 < k < peers}
    stats_shape = jax.ShapeDtypeStruct((2 * heads_up + 8, rows), F32)
    q_grad, stats = kernel_call(
        functools.partial(query_kernel, tiles, count, heads, heads_up),
        "attention_query_grad",
        [use],
        [after(queries, mixed_heads), mixed_grad, lse, *kv_all],
        [like_queries, stats_shape],
        cost(3 * attention_flops, (2 * count + 3) * array_bytes, exps, WEIGHTS["query"]),
    )
    stats_all = [stats] + [shift(stats, -d) for d in distances[1:]]
    partial_products = attended_partial(
        after(mixed_heads, query_all[-1], grad_all[-1]), out_weight, c_places, cost(2 * rows * columns * features, 2 * rows * features, 0, WEIGHTS["partial"])
    )
    shares = core_sum(partial_products)
    held = after(mixed_heads, arrived, *near.values(), *stats_all[1:], *shares)
    if peers <= 4:
        mixed_all = [mixed_heads] + [
            near[k] if k in near else cyclic(held, k) for k in range(1, peers)
        ]
    else:
        gathered = lax.all_gather(mixed_heads, "seq", axis=0)
        mixed_all = [
            lax.dynamic_index_in_dim(gathered, (place - k) % peers, 0, False)
            for k in range(peers)
        ]
    attended = chip_sum(shares, held)
    k_grad, v_grad = kernel_call(
        functools.partial(key_kernel, tiles, count, heads, heads_up),
        "attention_key_grad",
        [],
        [after(keys, held), values, *query_all, *grad_all, *stats_all],
        [like_queries] * 2,
        cost(4 * attention_flops, (2 * count + 4) * array_bytes, exps, WEIGHTS["key"]),
    )

    ct_blocks, ct_rest, _ = features_here(after(arrived, held))
    ct = jnp.stack(ct_blocks + other_features(ct_rest, k_grad))
    steps = step_of(c_places)
    ct_at = jnp.sum(
        jnp.where(steps[None] == jnp.arange(peers)[:, None], jnp.arange(group_count)[None], 0), 1
    ).astype(jnp.int32)
    early = sorted({0, 1, peers - 1}) if 2 < peers <= 4 else [0]
    late = [k for k in range(peers) if k not in early]
    weight_sum = []
    for part, which in enumerate((early, late)):
        if not which:
            weight_sum = [weight_sum[0].astype(BF16)]
            break
        ranges = [mixed_all[k] for k in which]
        if part:
            ranges[0] = after(ranges[0], attended, k_grad)
        weight_sum = [
            kernel_call(
                functools.partial(weight_grad_kernel, which, part),
                "weight_grad",
                [ct_at],
                [*weight_sum, ct, *ranges],
                jax.ShapeDtypeStruct((part_cols, columns), BF16 if part else F32),
                cost(2 * part_cols * columns * rows * len(which), array_bytes * len(which), 0, WEIGHTS["weight"]),
            )
        ]
    weight_grad = weight_sum[0]
    return (attended, q_grad, k_grad, v_grad, weight_grad)


def solution(mesh):
    shared = P(("groups", "seq"), ("head", "rep"))
    return jax.shard_map(
        per_device,
        mesh=mesh,
        in_specs=(shared, shared, shared, P(None, ("head", "rep")), P(("groups", "seq"), None), shared),
        out_specs=(shared,) * 5,
        check_vma=False,
    )
```

```python
import functools
import math

import jax
import jax.numpy as jnp
from jax import lax
from jax.experimental import pallas as pl
from jax.experimental.pallas import tpu as pltpu
from jax.sharding import PartitionSpec as P

HEAD_DIM = 128
BLOCK = 128
LEVELS = 5
SCALE = HEAD_DIM ** (-0.5)
LOG2_SCALE = SCALE * math.log2(math.e)
MASKED = -1e30

F32 = jnp.float32
BF16 = jnp.bfloat16
NT = (((1,), (1,)), ((), ()))
TN = (((0,), (0,)), ((), ()))


def shift(value, by):
    peers = lax.axis_size("seq")
    return lax.ppermute(
        value, "seq", [(i, i + by) for i in range(peers) if 0 <= i + by < peers]
    )


def cyclic(value, by):
    peers = lax.axis_size("seq")
    return lax.ppermute(value, "seq", [(i, (i + by) % peers) for i in range(peers)])


def swap(value, axis):
    return lax.ppermute(value, axis, [(0, 1), (1, 0)])


def dot(a, b):
    return jnp.dot(a, b, preferred_element_type=F32)


def dot_nt(a, b):
    return lax.dot_general(a, b, NT, preferred_element_type=F32)


def dot_tn(a, b):
    return lax.dot_general(a, b, TN, preferred_element_type=F32)


def after(value, *others):
    return lax.optimization_barrier((value, others))[0]


def seen_tiles(blocks, peers):
    tiles = []
    for n in range(blocks):
        mine = [(0, n, None)]
        for level in range(LEVELS):
            target = n - 2**level
            distance = -(target // blocks)
            if distance < peers:
                mine.append((distance, target % blocks, level))
        tiles.append(mine)
    return tiles


def block_rows(n):
    return pl.ds(n * BLOCK, BLOCK)


def head_cols(j):
    return slice(j * HEAD_DIM, (j + 1) * HEAD_DIM)


def cat(parts, axis=0):
    return parts[0] if len(parts) == 1 else jnp.concatenate(parts, axis)


def causal_tile():
    rows = lax.broadcasted_iota(jnp.int32, (BLOCK, BLOCK), 0)
    cols = lax.broadcasted_iota(jnp.int32, (BLOCK, BLOCK), 1)
    return rows <= cols


def forward_kernel(tiles, count, heads, use_ref, q_ref, *refs):
    kv_refs = refs[:count]
    mixed_ref, lse_ref = refs[count:]
    blocks = len(tiles)
    causal = causal_tile()
    for n, mine in enumerate(tiles):
        rows = block_rows(n)
        for j in range(heads):
            cols = head_cols(j)
            keys = cat([kv_refs[d][block_rows(b), cols] for d, b, _ in mine])
            vals = cat([kv_refs[d][block_rows(blocks + b), cols] for d, b, _ in mine])
            raw = dot_nt(keys, q_ref[rows, cols])
            parts = []
            for i, (_, _, level) in enumerate(mine):
                part = raw[i * BLOCK : (i + 1) * BLOCK]
                if level is None:
                    part = jnp.where(causal, part, MASKED)
                else:
                    part = part + jnp.where(use_ref[n * LEVELS + level] == 1, 0.0, MASKED)
                parts.append(part)
            top = jnp.max(functools.reduce(jnp.maximum, parts), 0, keepdims=True) * LOG2_SCALE
            grown = [jnp.exp2(part * LOG2_SCALE - top) for part in parts]
            total = jnp.sum(functools.reduce(jnp.add, grown), 0, keepdims=True)
            share = 1.0 / total
            prob = cat([(part * share).astype(BF16) for part in grown])
            mixed_ref[rows, cols] = dot_tn(prob, vals).astype(BF16)
            lse_ref[j : j + 1, rows] = top + jnp.log2(total)


def query_kernel(tiles, count, heads, heads_up, use_ref, q_ref, g_ref, lse_ref, *refs):
    kv_refs = refs[:count]
    dq_ref, stats_ref = refs[count:]
    blocks = len(tiles)
    causal = causal_tile()
    for n, mine in enumerate(tiles):
        rows = block_rows(n)
        for j in range(heads):
            cols = head_cols(j)
            keys = cat([kv_refs[d][block_rows(b), cols] for d, b, _ in mine])
            vals = cat([kv_refs[d][block_rows(blocks + b), cols] for d, b, _ in mine])
            lse = lse_ref[j : j + 1, rows]
            raw = dot_nt(keys, q_ref[rows, cols])
            prob_grad = dot_nt(vals, g_ref[rows, cols])
            probs, weighted = [], None
            for i, (_, _, level) in enumerate(mine):
                here = slice(i * BLOCK, (i + 1) * BLOCK)
                if level is None:
                    logits = jnp.where(causal, raw[here] * LOG2_SCALE - lse, MASKED)
                else:
                    off = lse + jnp.where(use_ref[n * LEVELS + level] == 1, 0.0, -MASKED)
                    logits = raw[here] * LOG2_SCALE - off
                prob = jnp.exp2(logits)
                probs.append(prob)
                part = prob * prob_grad[here]
                weighted = part if weighted is None else weighted + part
            delta = jnp.sum(weighted, 0, keepdims=True)
            score_grad = [
                (prob * SCALE * (prob_grad[i * BLOCK : (i + 1) * BLOCK] - delta)).astype(BF16)
                for i, prob in enumerate(probs)
            ]
            dq_ref[rows, cols] = dot_tn(cat(score_grad), keys).astype(BF16)
            stats_ref[j : j + 1, rows] = lse
            stats_ref[heads_up + j : heads_up + j + 1, rows] = delta
        flags = jnp.zeros((8, BLOCK), F32)
        level_row = lax.broadcasted_iota(jnp.int32, (8, BLOCK), 0)
        for level in range(LEVELS):
            flag = jnp.where(use_ref[n * LEVELS + level] == 1, 1.0, 0.0)
            flags = jnp.where(level_row == level, flag, flags)
        stats_ref[2 * heads_up :, rows] = flags
    for row in range(heads, heads_up):
        for first in (0, heads_up):
            stats_ref[first + row : first + row + 1, :] = jnp.zeros((1, stats_ref.shape[1]), F32)


def key_kernel(tiles, count, heads, heads_up, k_ref, v_ref, *refs):
    q_refs, g_refs, s_refs = refs[:count], refs[count : 2 * count], refs[2 * count : 3 * count]
    dk_ref, dv_ref = refs[3 * count :]
    causal = causal_tile()
    for b in range(len(tiles)):
        rows = block_rows(b)
        seers = [
            (d, n, level)
            for n, mine in enumerate(tiles)
            for d, block, level in mine
            if block == b
        ]
        for j in range(heads):
            cols = head_cols(j)
            ques = cat([q_refs[d][block_rows(n), cols] for d, n, _ in seers])
            grads = cat([g_refs[d][block_rows(n), cols] for d, n, _ in seers])
            raw = dot_nt(k_ref[rows, cols], ques)
            prob_grad = dot_nt(v_ref[rows, cols], grads)
            probs, score_grads = [], []
            for i, (d, n, level) in enumerate(seers):
                here = slice(i * BLOCK, (i + 1) * BLOCK)
                lse = s_refs[d][j : j + 1, block_rows(n)]
                delta = s_refs[d][heads_up + j : heads_up + j + 1, block_rows(n)]
                if level is None:
                    logits = jnp.where(causal, raw[:, here] * LOG2_SCALE - lse, MASKED)
                else:
                    row = 2 * heads_up + level
                    off = lse + (1.0 - s_refs[d][row : row + 1, block_rows(n)]) * (-MASKED)
                    logits = raw[:, here] * LOG2_SCALE - off
                prob = jnp.exp2(logits)
                probs.append(prob.astype(BF16))
                score_grads.append((prob * SCALE * (prob_grad[:, here] - delta)).astype(BF16))
            dv_ref[rows, cols] = dot(cat(probs, 1), grads).astype(BF16)
            dk_ref[rows, cols] = dot(cat(score_grads, 1), ques).astype(BF16)


class Stream:
    def __init__(self, pieces, held, sems):
        self.held = held
        self.copies = [
            pltpu.make_async_copy(piece, held.at[i], sems.at[i]) for i, piece in enumerate(pieces)
        ]
        for copy in self.copies[:2]:
            copy.start()

    def piece(self, i):
        self.copies[i].wait()
        if i + 2 < len(self.copies):
            self.copies[i + 2].start()
        return self.held.at[i]


def mixed_grad_kernel(count, given, place_ref, *refs):
    total = refs[0][...] if given else None
    c_refs, w_ref, out_ref, held, sems = refs[given : given + count], *refs[given + count :]
    depth = c_refs[0].shape[1]
    firsts = [pl.multiple_of(place_ref[i] * depth, depth) for i in range(count)]
    stream = Stream([w_ref.at[pl.ds(first, depth), :] for first in firsts], held, sems)
    for i in range(count):
        step = dot(c_refs[i][...], stream.piece(i)[...])
        total = step if total is None else total + step
    out_ref[...] = total.astype(out_ref.dtype)


def partial_kernel(split, place_ref, m_ref, w_ref, keep_ref, give_ref, held, sems):
    depth = keep_ref.shape[2]
    height = depth // split
    firsts = [place_ref[i] * depth + part * height for i in range(4) for part in range(split)]
    pieces = [w_ref.at[pl.ds(pl.multiple_of(first, height), height), :] for first in firsts]
    stream = Stream(pieces, held, sems)
    outs = [(give_ref, 0), (give_ref, 1), (keep_ref, 0), (keep_ref, 1)]
    for i, (out_ref, at) in enumerate(outs):
        for part in range(split):
            piece = stream.piece(i * split + part)
            cols = slice(part * height, (part + 1) * height)
            out_ref[at, :, cols] = dot_nt(m_ref[...], piece[...]).astype(BF16)


def weight_grad_kernel(which, given, place_ref, *refs):
    c_ref, m_refs, out_ref = refs[given], refs[given + 1 : -1], refs[-1]
    features = out_ref.shape[0]
    height = min(512, features)
    for first in range(0, features, height):
        rows = slice(first, first + height)
        total = refs[0][rows, :] if given else None
        fold = len(m_refs) // len(which)
        for i, p in enumerate(which):
            mixed = functools.reduce(jnp.add, [m[...] for m in m_refs[i * fold : (i + 1) * fold]])
            part = dot_tn(c_ref[place_ref[p], :, rows], mixed)
            total = part if total is None else total + part
        out_ref[rows, :] = total.astype(out_ref.dtype)


def cost(flops, bytes_accessed, exps=0, weight=1.0):
    return pl.CostEstimate(
        flops=int(flops * weight),
        bytes_accessed=int(bytes_accessed * weight),
        transcendentals=int(exps * weight),
    )


def kernel_call(body, name, scalars, arrays, out_shape, estimate, outside=(), scratch=()):
    smem = pl.BlockSpec(memory_space=pltpu.SMEM)
    vmem = pl.BlockSpec(memory_space=pltpu.VMEM)
    return pl.pallas_call(
        body,
        in_specs=[smem] * len(scalars)
        + [vmem] * len(arrays)
        + [pl.BlockSpec(memory_space=pltpu.HBM)] * len(outside),
        out_specs=jax.tree.map(lambda _: vmem, out_shape),
        out_shape=out_shape,
        scratch_shapes=list(scratch),
        compiler_params=pltpu.CompilerParams(
            vmem_limit_bytes=STREAM_LIMIT if outside else VMEM_LIMIT
        ),
        cost_estimate=estimate,
        name=name,
    )(*scalars, *arrays, *outside)


def weight_scratch(count, depth, columns):
    return [pltpu.VMEM((count, depth, columns), BF16), pltpu.SemaphoreType.DMA((count,))]


VMEM_LIMIT = 20 * 1024 * 1024
WEIGHTS = dict(mixed_grad=0.0, forward=0.0, partial=100.0, query=100.0, key=100.0, weight=0.0)
STREAM_LIMIT = 54 * 1024 * 1024


def two_by_two():
    return lax.axis_size("head") == 2 and lax.axis_size("rep") == 2


def features_here(value):
    heads, reps = lax.axis_size("head"), lax.axis_size("rep")
    if two_by_two():
        h, r = lax.axis_index("head"), lax.axis_index("rep")
        places = [2 * h + r, 2 * h + 1 - r, 2 * (1 - h) + r, 2 * (1 - h) + 1 - r]
        rest = swap(value, "head")
        return [value, swap(value, "rep")], rest, jnp.stack(places).astype(jnp.int32)
    count = heads * reps
    gathered = lax.all_gather(value, ("head", "rep"), axis=0)
    blocks = [gathered[i] for i in range(count)]
    return blocks[: count // 2], blocks[count // 2 :], jnp.arange(count, dtype=jnp.int32)


def other_features(rest, *others):
    if two_by_two():
        return [rest, swap(after(rest, *others), "rep")]
    return rest


def attended_partial(mixed_heads, out_weight, places, estimate):
    if two_by_two():
        rows = mixed_heads.shape[0]
        share = out_weight.shape[0] // 4
        order = jnp.stack([places[1], places[3], places[0], places[2]])
        return kernel_call(
            functools.partial(partial_kernel, 1),
            "attended_partial",
            [order],
            [mixed_heads],
            [jax.ShapeDtypeStruct((2, rows, share), BF16)] * 2,
            estimate,
            [out_weight],
            weight_scratch(4, share, mixed_heads.shape[1]),
        )
    partial_value = lax.dot_general(mixed_heads, out_weight, NT, preferred_element_type=F32)
    return [partial_value.astype(BF16)]


def core_sum(partial_products):
    if len(partial_products) == 1:
        return partial_products
    keep, give = partial_products
    got = swap(give, "rep")
    return [
        keep[0].astype(F32) + got[0].astype(F32),
        (keep[1].astype(F32) + got[1].astype(F32)).astype(BF16),
    ]


def chip_sum(shares):
    if len(shares) == 1:
        return lax.psum_scatter(shares[0], ("head", "rep"), scatter_dimension=1, tiled=True)
    return (shares[0] + swap(shares[1], "head").astype(F32)).astype(BF16)


def per_device(queries, keys, values, out_weight, level_mask, cotangent):
    rows, columns = queries.shape
    features = out_weight.shape[0]
    heads = columns // HEAD_DIM
    heads_up = -(-heads // 8) * 8
    blocks = rows // BLOCK
    peers = lax.axis_size("seq")
    place = lax.axis_index("seq")
    tiles = seen_tiles(blocks, peers)
    distances = sorted({d for mine in tiles for d, _, _ in mine})
    count = len(distances)
    slot = {d: i for i, d in enumerate(distances)}
    tiles = [[(slot[d], b, level) for d, b, level in mine] for mine in tiles]
    pairs = sum(len(mine) for mine in tiles)
    attention_flops = 2 * heads * pairs * BLOCK * BLOCK * HEAD_DIM
    array_bytes = 2 * rows * columns
    exps = heads * pairs * BLOCK * BLOCK
    like_queries = jax.ShapeDtypeStruct((rows, columns), BF16)

    def further(got, sign, *others):
        near, far = distances[len(got) - 1], distances[len(got)]
        return got + [shift(after(got[-1], *others), sign * (far - near))]

    block_ids = place * blocks + jnp.arange(blocks, dtype=jnp.int32)
    offsets = 2 ** jnp.arange(LEVELS, dtype=jnp.int32)
    use = ((block_ids[:, None] >= offsets[None]) & (level_mask == 1)).astype(jnp.int32)
    use = use.reshape(-1)

    kv_all = further([jnp.concatenate([keys, values])], 1)
    query_all = further([queries], -1)
    c_blocks, c_rest, c_places = features_here(cotangent)
    half = len(c_blocks)
    part_cols = cotangent.shape[1]
    mixed_sum = []
    for part in range(2):
        if part:
            c_blocks = c_blocks + other_features(c_rest, *mixed_sum, query_all[1])
        mine = slice(part * half, (part + 1) * half)
        mixed_sum = [
            kernel_call(
                functools.partial(mixed_grad_kernel, half, part),
                "mixed_grad",
                [c_places[mine]],
                [*mixed_sum, *c_blocks[mine]],
                jax.ShapeDtypeStruct((rows, columns), BF16 if part else F32),
                cost(rows * columns * features, columns * features, 0, WEIGHTS["mixed_grad"] * (1 - part)),
                [out_weight],
                weight_scratch(half, part_cols, columns),
            )
        ]
    mixed_grad = mixed_sum[0]
    group_count = len(c_blocks)
    while len(kv_all) < count:
        kv_all = further(kv_all, 1, mixed_grad)
    grad_all = further([mixed_grad], -1)
    while len(query_all) < count:
        query_all = further(query_all, -1, mixed_grad)
    while len(grad_all) < count:
        grad_all = further(grad_all, -1)

    h, r = lax.axis_index("head"), lax.axis_index("rep")
    n_head, n_rep = lax.axis_size("head"), lax.axis_size("rep")
    step_of = lambda i: (i // n_rep) + n_head * (i % n_rep)
    wanted = (place + step_of(h * n_rep + r)) % peers
    out_block = c_blocks[0]
    for i in range(1, group_count):
        out_block = jnp.where(c_places[i] == wanted, c_blocks[i], out_block)
    links = []
    for s in range(peers):
        for q in range(group_count):
            links.append((s * group_count + q, ((s + step_of(q)) % peers) * group_count + q))
    arrived = lax.ppermute(after(out_block, grad_all[1], kv_all[-1]), ("seq", "head", "rep"), links)

    mixed_heads, lse = kernel_call(
        functools.partial(forward_kernel, tiles, count, heads),
        "attention_forward",
        [use],
        [queries, *kv_all],
        [like_queries, jax.ShapeDtypeStruct((heads_up, rows), F32)],
        cost(2 * attention_flops, (2 * count + 2) * array_bytes, exps, WEIGHTS["forward"]),
    )

    near = {}
    if peers <= 4:
        near = {k: cyclic(mixed_heads, k) for k in sorted({1, peers - 1}) if 0 < k < peers}
    stats_shape = jax.ShapeDtypeStruct((2 * heads_up + 8, rows), F32)
    q_grad, stats = kernel_call(
        functools.partial(query_kernel, tiles, count, heads, heads_up),
        "attention_query_grad",
        [use],
        [after(queries, mixed_heads, query_all[-1], grad_all[-1]), mixed_grad, lse, *kv_all],
        [like_queries, stats_shape],
        cost(3 * attention_flops, (2 * count + 3) * array_bytes, exps, WEIGHTS["query"]),
    )
    stats_all = further([stats], -1)
    partial_products = attended_partial(
        after(mixed_heads, query_all[-1], grad_all[-1]), out_weight, c_places, cost(2 * rows * columns * features, 2 * rows * features, 0, WEIGHTS["partial"])
    )
    shares = core_sum(partial_products)
    attended = chip_sum(shares)
    held = after(mixed_heads, arrived, *near.values(), *stats_all[1:], attended)
    while len(stats_all) < count:
        stats_all = further(stats_all, -1, held)
    if peers <= 4:
        mixed_all = [[mixed_heads]] + [[near[k]] if k in near else [] for k in range(1, peers)]
        if peers == 4:
            up = lax.ppermute(after(near[1], held), "seq", [(1, 2), (2, 3)])
            down = lax.ppermute(after(near[3], held), "seq", [(1, 0), (2, 1)])
            mixed_all[2] = [up, down]
    else:
        gathered = lax.all_gather(mixed_heads, "seq", axis=0)
        mixed_all = [
            [lax.dynamic_index_in_dim(gathered, (place - k) % peers, 0, False)]
            for k in range(peers)
        ]
    k_grad, v_grad = kernel_call(
        functools.partial(key_kernel, tiles, count, heads, heads_up),
        "attention_key_grad",
        [],
        [after(keys, held), values, *query_all, *grad_all, *stats_all],
        [like_queries] * 2,
        cost(4 * attention_flops, (2 * count + 4) * array_bytes, exps, WEIGHTS["key"]),
    )

    if two_by_two():
        ct_across = swap(after(arrived, held), "head")
        far = [value for values in mixed_all for value in values]
        beside = swap(after(arrived, ct_across, *far), "rep")
        ct_blocks = [arrived, beside, *other_features(ct_across, *far, k_grad)]
    else:
        ct_blocks, ct_rest, _ = features_here(arrived)
        ct_blocks = ct_blocks + ct_rest
    ct = jnp.stack(ct_blocks)
    steps = step_of(c_places)
    ct_at = jnp.sum(
        jnp.where(steps[None] == jnp.arange(peers)[:, None], jnp.arange(group_count)[None], 0), 1
    ).astype(jnp.int32)
    early = sorted({0, 1, peers - 1}) if 2 < peers <= 4 else [0]
    late = [k for k in range(peers) if k not in early]
    weight_sum = []
    for part, which in enumerate((early, late)):
        if not which:
            weight_sum = [weight_sum[0].astype(BF16)]
            break
        ranges = [value for k in which for value in mixed_all[k]]
        if part:
            ranges[0] = after(ranges[0], k_grad)
        weight_sum = [
            kernel_call(
                functools.partial(weight_grad_kernel, which, part),
                "weight_grad",
                [ct_at],
                [*weight_sum, ct, *ranges],
                jax.ShapeDtypeStruct((part_cols, columns), BF16 if part else F32),
                cost(2 * part_cols * columns * rows * len(which), array_bytes * len(which), 0, WEIGHTS["weight"]),
            )
        ]
    weight_grad = weight_sum[0]
    return (attended, q_grad, k_grad, v_grad, weight_grad)


def solution(mesh):
    shared = P(("groups", "seq"), ("head", "rep"))
    return jax.shard_map(
        per_device,
        mesh=mesh,
        in_specs=(shared, shared, shared, P(None, ("head", "rep")), P(("groups", "seq"), None), shared),
        out_specs=(shared,) * 5,
        check_vma=False,
    )
```

```python
import functools
import math

import jax
import jax.numpy as jnp
from jax import lax
from jax.experimental import pallas as pl
from jax.experimental.pallas import tpu as pltpu
from jax.sharding import PartitionSpec as P

HEAD_DIM = 128
BLOCK = 128
LEVELS = 5
SCALE = HEAD_DIM ** (-0.5)
LOG2_SCALE = SCALE * math.log2(math.e)
MASKED = -1e30

F32 = jnp.float32
BF16 = jnp.bfloat16
NT = (((1,), (1,)), ((), ()))
TN = (((0,), (0,)), ((), ()))


def shift(value, by):
    peers = lax.axis_size("seq")
    return lax.ppermute(
        value, "seq", [(i, i + by) for i in range(peers) if 0 <= i + by < peers]
    )


def cyclic(value, by):
    peers = lax.axis_size("seq")
    return lax.ppermute(value, "seq", [(i, (i + by) % peers) for i in range(peers)])


def swap(value, axis):
    return lax.ppermute(value, axis, [(0, 1), (1, 0)])


def dot(a, b):
    return jnp.dot(a, b, preferred_element_type=F32)


def dot_nt(a, b):
    return lax.dot_general(a, b, NT, preferred_element_type=F32)


def dot_tn(a, b):
    return lax.dot_general(a, b, TN, preferred_element_type=F32)


def after(value, *others):
    return lax.optimization_barrier((value, others))[0]


def seen_tiles(blocks, peers):
    tiles = []
    for n in range(blocks):
        mine = [(0, n, None)]
        for level in range(LEVELS):
            target = n - 2**level
            distance = -(target // blocks)
            if distance < peers:
                mine.append((distance, target % blocks, level))
        tiles.append(mine)
    return tiles


def block_rows(n):
    return pl.ds(n * BLOCK, BLOCK)


def head_cols(j):
    return slice(j * HEAD_DIM, (j + 1) * HEAD_DIM)


def cat(parts, axis=0):
    return parts[0] if len(parts) == 1 else jnp.concatenate(parts, axis)


def causal_tile():
    rows = lax.broadcasted_iota(jnp.int32, (BLOCK, BLOCK), 0)
    cols = lax.broadcasted_iota(jnp.int32, (BLOCK, BLOCK), 1)
    return rows <= cols


def forward_kernel(tiles, count, heads, use_ref, q_ref, *refs):
    kv_refs = refs[:count]
    mixed_ref, lse_ref = refs[count:]
    blocks = len(tiles)
    causal = causal_tile()
    for n, mine in enumerate(tiles):
        rows = block_rows(n)
        for j in range(heads):
            cols = head_cols(j)
            keys = cat([kv_refs[d][block_rows(b), cols] for d, b, _ in mine])
            vals = cat([kv_refs[d][block_rows(blocks + b), cols] for d, b, _ in mine])
            raw = dot_nt(keys, q_ref[rows, cols])
            parts = []
            for i, (_, _, level) in enumerate(mine):
                part = raw[i * BLOCK : (i + 1) * BLOCK]
                if level is None:
                    part = jnp.where(causal, part, MASKED)
                else:
                    part = part + jnp.where(use_ref[n * LEVELS + level] == 1, 0.0, MASKED)
                parts.append(part)
            top = jnp.max(functools.reduce(jnp.maximum, parts), 0, keepdims=True) * LOG2_SCALE
            grown = [jnp.exp2(part * LOG2_SCALE - top) for part in parts]
            total = jnp.sum(functools.reduce(jnp.add, grown), 0, keepdims=True)
            share = 1.0 / total
            prob = cat([(part * share).astype(BF16) for part in grown])
            mixed_ref[rows, cols] = dot_tn(prob, vals).astype(BF16)
            lse_ref[j : j + 1, rows] = top + jnp.log2(total)


def query_kernel(tiles, count, heads, heads_up, use_ref, q_ref, g_ref, lse_ref, *refs):
    kv_refs = refs[:count]
    dq_ref, stats_ref = refs[count:]
    blocks = len(tiles)
    causal = causal_tile()
    for n, mine in enumerate(tiles):
        rows = block_rows(n)
        for j in range(heads):
            cols = head_cols(j)
            keys = cat([kv_refs[d][block_rows(b), cols] for d, b, _ in mine])
            vals = cat([kv_refs[d][block_rows(blocks + b), cols] for d, b, _ in mine])
            lse = lse_ref[j : j + 1, rows]
            raw = dot_nt(keys, q_ref[rows, cols])
            prob_grad = dot_nt(vals, g_ref[rows, cols])
            probs, weighted = [], None
            for i, (_, _, level) in enumerate(mine):
                here = slice(i * BLOCK, (i + 1) * BLOCK)
                if level is None:
                    logits = jnp.where(causal, raw[here] * LOG2_SCALE - lse, MASKED)
                else:
                    off = lse + jnp.where(use_ref[n * LEVELS + level] == 1, 0.0, -MASKED)
                    logits = raw[here] * LOG2_SCALE - off
                prob = jnp.exp2(logits)
                probs.append(prob)
                part = prob * prob_grad[here]
                weighted = part if weighted is None else weighted + part
            delta = jnp.sum(weighted, 0, keepdims=True)
            score_grad = [
                (prob * SCALE * (prob_grad[i * BLOCK : (i + 1) * BLOCK] - delta)).astype(BF16)
                for i, prob in enumerate(probs)
            ]
            dq_ref[rows, cols] = dot_tn(cat(score_grad), keys).astype(BF16)
            stats_ref[j : j + 1, rows] = lse
            stats_ref[heads_up + j : heads_up + j + 1, rows] = delta
        flags = jnp.zeros((8, BLOCK), F32)
        level_row = lax.broadcasted_iota(jnp.int32, (8, BLOCK), 0)
        for level in range(LEVELS):
            flag = jnp.where(use_ref[n * LEVELS + level] == 1, 1.0, 0.0)
            flags = jnp.where(level_row == level, flag, flags)
        stats_ref[2 * heads_up :, rows] = flags
    for row in range(heads, heads_up):
        for first in (0, heads_up):
            stats_ref[first + row : first + row + 1, :] = jnp.zeros((1, stats_ref.shape[1]), F32)


def key_kernel(tiles, count, heads, heads_up, k_ref, v_ref, *refs):
    q_refs, g_refs, s_refs = refs[:count], refs[count : 2 * count], refs[2 * count : 3 * count]
    dk_ref, dv_ref = refs[3 * count :]
    causal = causal_tile()
    for b in range(len(tiles)):
        rows = block_rows(b)
        seers = [
            (d, n, level)
            for n, mine in enumerate(tiles)
            for d, block, level in mine
            if block == b
        ]
        for j in range(heads):
            cols = head_cols(j)
            ques = cat([q_refs[d][block_rows(n), cols] for d, n, _ in seers])
            grads = cat([g_refs[d][block_rows(n), cols] for d, n, _ in seers])
            raw = dot_nt(k_ref[rows, cols], ques)
            prob_grad = dot_nt(v_ref[rows, cols], grads)
            probs, score_grads = [], []
            for i, (d, n, level) in enumerate(seers):
                here = slice(i * BLOCK, (i + 1) * BLOCK)
                lse = s_refs[d][j : j + 1, block_rows(n)]
                delta = s_refs[d][heads_up + j : heads_up + j + 1, block_rows(n)]
                if level is None:
                    logits = jnp.where(causal, raw[:, here] * LOG2_SCALE - lse, MASKED)
                else:
                    row = 2 * heads_up + level
                    off = lse + (1.0 - s_refs[d][row : row + 1, block_rows(n)]) * (-MASKED)
                    logits = raw[:, here] * LOG2_SCALE - off
                prob = jnp.exp2(logits)
                probs.append(prob.astype(BF16))
                score_grads.append((prob * SCALE * (prob_grad[:, here] - delta)).astype(BF16))
            dv_ref[rows, cols] = dot(cat(probs, 1), grads).astype(BF16)
            dk_ref[rows, cols] = dot(cat(score_grads, 1), ques).astype(BF16)


class Stream:
    def __init__(self, pieces, held, sems):
        self.held = held
        self.copies = [
            pltpu.make_async_copy(piece, held.at[i], sems.at[i]) for i, piece in enumerate(pieces)
        ]
        for copy in self.copies[:2]:
            copy.start()

    def piece(self, i):
        self.copies[i].wait()
        if i + 2 < len(self.copies):
            self.copies[i + 2].start()
        return self.held.at[i]


def mixed_grad_kernel(count, given, place_ref, *refs):
    total = refs[0][...] if given else None
    c_refs, w_ref, out_ref, held, sems = refs[given : given + count], *refs[given + count :]
    depth = c_refs[0].shape[1]
    firsts = [pl.multiple_of(place_ref[i] * depth, depth) for i in range(count)]
    stream = Stream([w_ref.at[pl.ds(first, depth), :] for first in firsts], held, sems)
    for i in range(count):
        step = dot(c_refs[i][...], stream.piece(i)[...])
        total = step if total is None else total + step
    out_ref[...] = total.astype(out_ref.dtype)


def partial_kernel(split, place_ref, m_ref, w_ref, keep_ref, give_ref, held, sems):
    depth = keep_ref.shape[2]
    height = depth // split
    firsts = [place_ref[i] * depth + part * height for i in range(4) for part in range(split)]
    pieces = [w_ref.at[pl.ds(pl.multiple_of(first, height), height), :] for first in firsts]
    stream = Stream(pieces, held, sems)
    outs = [(give_ref, 0), (give_ref, 1), (keep_ref, 0), (keep_ref, 1)]
    for i, (out_ref, at) in enumerate(outs):
        for part in range(split):
            piece = stream.piece(i * split + part)
            cols = slice(part * height, (part + 1) * height)
            out_ref[at, :, cols] = dot_nt(m_ref[...], piece[...]).astype(BF16)


def weight_grad_kernel(which, given, place_ref, *refs):
    c_ref, m_refs, out_ref = refs[given], refs[given + 1 : -1], refs[-1]
    features = out_ref.shape[0]
    height = min(512, features)
    for first in range(0, features, height):
        rows = slice(first, first + height)
        total = refs[0][rows, :] if given else None
        fold = len(m_refs) // len(which)
        for i, p in enumerate(which):
            mixed = functools.reduce(jnp.add, [m[...] for m in m_refs[i * fold : (i + 1) * fold]])
            part = dot_tn(c_ref[place_ref[p], :, rows], mixed)
            total = part if total is None else total + part
        out_ref[rows, :] = total.astype(out_ref.dtype)


def cost(flops, bytes_accessed, exps=0, weight=1.0):
    return pl.CostEstimate(
        flops=int(flops * weight),
        bytes_accessed=int(bytes_accessed * weight),
        transcendentals=int(exps * weight),
    )


def kernel_call(body, name, scalars, arrays, out_shape, estimate, outside=(), scratch=()):
    smem = pl.BlockSpec(memory_space=pltpu.SMEM)
    vmem = pl.BlockSpec(memory_space=pltpu.VMEM)
    return pl.pallas_call(
        body,
        in_specs=[smem] * len(scalars)
        + [vmem] * len(arrays)
        + [pl.BlockSpec(memory_space=pltpu.HBM)] * len(outside),
        out_specs=jax.tree.map(lambda _: vmem, out_shape),
        out_shape=out_shape,
        scratch_shapes=list(scratch),
        compiler_params=pltpu.CompilerParams(
            vmem_limit_bytes=STREAM_LIMIT if outside else VMEM_LIMIT
        ),
        cost_estimate=estimate,
        name=name,
    )(*scalars, *arrays, *outside)


def weight_scratch(count, depth, columns):
    return [pltpu.VMEM((count, depth, columns), BF16), pltpu.SemaphoreType.DMA((count,))]


VMEM_LIMIT = 20 * 1024 * 1024
WEIGHTS = dict(mixed_grad=0.0, forward=0.0, partial=0.0, query=100.0, key=100.0, weight=0.0)
STREAM_LIMIT = 54 * 1024 * 1024


def two_by_two():
    return lax.axis_size("head") == 2 and lax.axis_size("rep") == 2


def features_here(value):
    heads, reps = lax.axis_size("head"), lax.axis_size("rep")
    if two_by_two():
        h, r = lax.axis_index("head"), lax.axis_index("rep")
        places = [2 * h + r, 2 * h + 1 - r, 2 * (1 - h) + r, 2 * (1 - h) + 1 - r]
        rest = swap(value, "head")
        return [value, swap(value, "rep")], rest, jnp.stack(places).astype(jnp.int32)
    count = heads * reps
    gathered = lax.all_gather(value, ("head", "rep"), axis=0)
    blocks = [gathered[i] for i in range(count)]
    return blocks[: count // 2], blocks[count // 2 :], jnp.arange(count, dtype=jnp.int32)


def other_features(rest, *others):
    if two_by_two():
        return [rest, swap(after(rest, *others), "rep")]
    return rest


def attended_partial(mixed_heads, out_weight, places, estimate):
    if two_by_two():
        rows = mixed_heads.shape[0]
        share = out_weight.shape[0] // 4
        order = jnp.stack([places[1], places[3], places[0], places[2]])
        return kernel_call(
            functools.partial(partial_kernel, 1),
            "attended_partial",
            [order],
            [mixed_heads],
            [jax.ShapeDtypeStruct((2, rows, share), BF16)] * 2,
            estimate,
            [out_weight],
            weight_scratch(4, share, mixed_heads.shape[1]),
        )
    partial_value = lax.dot_general(mixed_heads, out_weight, NT, preferred_element_type=F32)
    return [partial_value.astype(BF16)]


def core_sum(partial_products):
    if len(partial_products) == 1:
        return partial_products
    keep, give = partial_products
    got = swap(give, "rep")
    return [
        keep[0].astype(F32) + got[0].astype(F32),
        (keep[1].astype(F32) + got[1].astype(F32)).astype(BF16),
    ]


def chip_sum(shares, *others):
    if len(shares) == 1:
        return lax.psum_scatter(shares[0], ("head", "rep"), scatter_dimension=1, tiled=True)
    return (shares[0] + swap(after(shares[1], *others), "head").astype(F32)).astype(BF16)


def per_device(queries, keys, values, out_weight, level_mask, cotangent):
    rows, columns = queries.shape
    features = out_weight.shape[0]
    heads = columns // HEAD_DIM
    heads_up = -(-heads // 8) * 8
    blocks = rows // BLOCK
    peers = lax.axis_size("seq")
    place = lax.axis_index("seq")
    tiles = seen_tiles(blocks, peers)
    distances = sorted({d for mine in tiles for d, _, _ in mine})
    count = len(distances)
    slot = {d: i for i, d in enumerate(distances)}
    tiles = [[(slot[d], b, level) for d, b, level in mine] for mine in tiles]
    pairs = sum(len(mine) for mine in tiles)
    attention_flops = 2 * heads * pairs * BLOCK * BLOCK * HEAD_DIM
    array_bytes = 2 * rows * columns
    exps = heads * pairs * BLOCK * BLOCK
    like_queries = jax.ShapeDtypeStruct((rows, columns), BF16)

    def further(got, sign, *others):
        near, far = distances[len(got) - 1], distances[len(got)]
        return got + [shift(after(got[-1], *others), sign * (far - near))]

    block_ids = place * blocks + jnp.arange(blocks, dtype=jnp.int32)
    offsets = 2 ** jnp.arange(LEVELS, dtype=jnp.int32)
    use = ((block_ids[:, None] >= offsets[None]) & (level_mask == 1)).astype(jnp.int32)
    use = use.reshape(-1)

    kv_all = further([jnp.concatenate([keys, values])], 1)
    query_all = further([queries], -1)
    c_blocks, c_rest, c_places = features_here(cotangent)
    half = len(c_blocks)
    part_cols = cotangent.shape[1]
    mixed_sum = []
    for part in range(2):
        if part:
            c_blocks = c_blocks + other_features(c_rest, *mixed_sum, query_all[1])
        mine = slice(part * half, (part + 1) * half)
        mixed_sum = [
            kernel_call(
                functools.partial(mixed_grad_kernel, half, part),
                "mixed_grad",
                [c_places[mine]],
                [*mixed_sum, *c_blocks[mine]],
                jax.ShapeDtypeStruct((rows, columns), BF16 if part else F32),
                cost(rows * columns * features, columns * features, 0, WEIGHTS["mixed_grad"] * (1 - part)),
                [out_weight],
                weight_scratch(half, part_cols, columns),
            )
        ]
    mixed_grad = mixed_sum[0]
    group_count = len(c_blocks)
    while len(kv_all) < count:
        kv_all = further(kv_all, 1, mixed_grad)
    grad_all = further([mixed_grad], -1)
    while len(query_all) < count:
        query_all = further(query_all, -1, mixed_grad)
    while len(grad_all) < count:
        grad_all = further(grad_all, -1)

    h, r = lax.axis_index("head"), lax.axis_index("rep")
    n_head, n_rep = lax.axis_size("head"), lax.axis_size("rep")
    step_of = lambda i: (i // n_rep) + n_head * (i % n_rep)
    wanted = (place + step_of(h * n_rep + r)) % peers
    out_block = c_blocks[0]
    for i in range(1, group_count):
        out_block = jnp.where(c_places[i] == wanted, c_blocks[i], out_block)
    links = []
    for s in range(peers):
        for q in range(group_count):
            links.append((s * group_count + q, ((s + step_of(q)) % peers) * group_count + q))
    arrived = lax.ppermute(after(out_block, grad_all[1], kv_all[-1]), ("seq", "head", "rep"), links)

    mixed_heads, lse = kernel_call(
        functools.partial(forward_kernel, tiles, count, heads),
        "attention_forward",
        [use],
        [queries, *kv_all],
        [like_queries, jax.ShapeDtypeStruct((heads_up, rows), F32)],
        cost(2 * attention_flops, (2 * count + 2) * array_bytes, exps, WEIGHTS["forward"]),
    )

    near = {}
    if peers <= 4:
        near = {k: cyclic(mixed_heads, k) for k in sorted({1, peers - 1}) if 0 < k < peers}
    stats_shape = jax.ShapeDtypeStruct((2 * heads_up + 8, rows), F32)
    q_grad, stats = kernel_call(
        functools.partial(query_kernel, tiles, count, heads, heads_up),
        "attention_query_grad",
        [use],
        [after(queries, mixed_heads), mixed_grad, lse, *kv_all],
        [like_queries, stats_shape],
        cost(3 * attention_flops, (2 * count + 3) * array_bytes, exps, WEIGHTS["query"]),
    )
    stats_all = [stats] + [shift(stats, -d) for d in distances[1:]]
    partial_products = attended_partial(
        after(mixed_heads, query_all[-1], grad_all[-1]), out_weight, c_places, cost(2 * rows * columns * features, 2 * rows * features, 0, WEIGHTS["partial"])
    )
    shares = core_sum(partial_products)
    ct_across = swap(after(arrived, *partial_products), "head") if two_by_two() else arrived
    held = after(mixed_heads, ct_across, *near.values(), *stats_all[1:], *shares)
    if peers <= 4:
        mixed_all = [[mixed_heads]] + [[near[k]] if k in near else [] for k in range(1, peers)]
        if peers == 4:
            up = lax.ppermute(after(near[1], held), "seq", [(1, 2), (2, 3)])
            down = lax.ppermute(after(near[3], held), "seq", [(1, 0), (2, 1)])
            mixed_all[2] = [up, down]
    else:
        gathered = lax.all_gather(mixed_heads, "seq", axis=0)
        mixed_all = [
            [lax.dynamic_index_in_dim(gathered, (place - k) % peers, 0, False)]
            for k in range(peers)
        ]
    attended = chip_sum(shares, held)
    k_grad, v_grad = kernel_call(
        functools.partial(key_kernel, tiles, count, heads, heads_up),
        "attention_key_grad",
        [],
        [after(keys, held), values, *query_all, *grad_all, *stats_all],
        [like_queries] * 2,
        cost(4 * attention_flops, (2 * count + 4) * array_bytes, exps, WEIGHTS["key"]),
    )

    if two_by_two():
        ct_blocks = [arrived, swap(after(arrived, held), "rep"), *other_features(ct_across, held)]
    else:
        ct_blocks, ct_rest, _ = features_here(arrived)
        ct_blocks = ct_blocks + ct_rest
    ct = jnp.stack(ct_blocks)
    steps = step_of(c_places)
    ct_at = jnp.sum(
        jnp.where(steps[None] == jnp.arange(peers)[:, None], jnp.arange(group_count)[None], 0), 1
    ).astype(jnp.int32)
    early = sorted({0, 1, peers - 1}) if 2 < peers <= 4 else [0]
    late = [k for k in range(peers) if k not in early]
    weight_sum = []
    for part, which in enumerate((early, late)):
        if not which:
            weight_sum = [weight_sum[0].astype(BF16)]
            break
        ranges = [value for k in which for value in mixed_all[k]]
        if part:
            ranges[0] = after(ranges[0], k_grad, attended)
        weight_sum = [
            kernel_call(
                functools.partial(weight_grad_kernel, which, part),
                "weight_grad",
                [ct_at],
                [*weight_sum, ct, *ranges],
                jax.ShapeDtypeStruct((part_cols, columns), BF16 if part else F32),
                cost(2 * part_cols * columns * rows * len(which), array_bytes * len(which), 0, WEIGHTS["weight"]),
            )
        ]
    weight_grad = weight_sum[0]
    return (attended, q_grad, k_grad, v_grad, weight_grad)


def solution(mesh):
    shared = P(("groups", "seq"), ("head", "rep"))
    return jax.shard_map(
        per_device,
        mesh=mesh,
        in_specs=(shared, shared, shared, P(None, ("head", "rep")), P(("groups", "seq"), None), shared),
        out_specs=(shared,) * 5,
        check_vma=False,
    )
```

```python
import functools
import math

import jax
import jax.numpy as jnp
from jax import lax
from jax.experimental import pallas as pl
from jax.experimental.pallas import tpu as pltpu
from jax.sharding import PartitionSpec as P

HEAD_DIM = 128
BLOCK = 128
LEVELS = 5
SCALE = HEAD_DIM ** (-0.5)
LOG2_SCALE = SCALE * math.log2(math.e)
MASKED = -1e30

F32 = jnp.float32
BF16 = jnp.bfloat16
NT = (((1,), (1,)), ((), ()))
TN = (((0,), (0,)), ((), ()))


def shift(value, by):
    peers = lax.axis_size("seq")
    return lax.ppermute(
        value, "seq", [(i, i + by) for i in range(peers) if 0 <= i + by < peers]
    )


def cyclic(value, by):
    peers = lax.axis_size("seq")
    return lax.ppermute(value, "seq", [(i, (i + by) % peers) for i in range(peers)])


def swap(value, axis):
    return lax.ppermute(value, axis, [(0, 1), (1, 0)])


def dot(a, b):
    return jnp.dot(a, b, preferred_element_type=F32)


def dot_nt(a, b):
    return lax.dot_general(a, b, NT, preferred_element_type=F32)


def dot_tn(a, b):
    return lax.dot_general(a, b, TN, preferred_element_type=F32)


def after(value, *others):
    return lax.optimization_barrier((value, others))[0]


def seen_tiles(blocks, peers):
    tiles = []
    for n in range(blocks):
        mine = [(0, n, None)]
        for level in range(LEVELS):
            target = n - 2**level
            distance = -(target // blocks)
            if distance < peers:
                mine.append((distance, target % blocks, level))
        tiles.append(mine)
    return tiles


def block_rows(n):
    return pl.ds(n * BLOCK, BLOCK)


def head_cols(j):
    return slice(j * HEAD_DIM, (j + 1) * HEAD_DIM)


def cat(parts, axis=0):
    return parts[0] if len(parts) == 1 else jnp.concatenate(parts, axis)


def causal_tile():
    rows = lax.broadcasted_iota(jnp.int32, (BLOCK, BLOCK), 0)
    cols = lax.broadcasted_iota(jnp.int32, (BLOCK, BLOCK), 1)
    return rows <= cols


def forward_kernel(tiles, count, heads, use_ref, q_ref, *refs):
    kv_refs = refs[:count]
    mixed_ref, lse_ref = refs[count:]
    blocks = len(tiles)
    causal = causal_tile()
    for n, mine in enumerate(tiles):
        rows = block_rows(n)
        for j in range(heads):
            cols = head_cols(j)
            keys = cat([kv_refs[d][block_rows(b), cols] for d, b, _ in mine])
            vals = cat([kv_refs[d][block_rows(blocks + b), cols] for d, b, _ in mine])
            raw = dot_nt(keys, q_ref[rows, cols])
            parts = []
            for i, (_, _, level) in enumerate(mine):
                part = raw[i * BLOCK : (i + 1) * BLOCK]
                if level is None:
                    part = jnp.where(causal, part, MASKED)
                else:
                    part = part + jnp.where(use_ref[n * LEVELS + level] == 1, 0.0, MASKED)
                parts.append(part)
            top = jnp.max(functools.reduce(jnp.maximum, parts), 0, keepdims=True) * LOG2_SCALE
            grown = [jnp.exp2(part * LOG2_SCALE - top) for part in parts]
            total = jnp.sum(functools.reduce(jnp.add, grown), 0, keepdims=True)
            share = 1.0 / total
            prob = cat([(part * share).astype(BF16) for part in grown])
            mixed_ref[rows, cols] = dot_tn(prob, vals).astype(BF16)
            lse_ref[j : j + 1, rows] = top + jnp.log2(total)


def query_kernel(tiles, count, heads, heads_up, use_ref, q_ref, g_ref, lse_ref, *refs):
    kv_refs = refs[:count]
    dq_ref, stats_ref = refs[count:]
    blocks = len(tiles)
    causal = causal_tile()
    for n, mine in enumerate(tiles):
        rows = block_rows(n)
        for j in range(heads):
            cols = head_cols(j)
            keys = cat([kv_refs[d][block_rows(b), cols] for d, b, _ in mine])
            vals = cat([kv_refs[d][block_rows(blocks + b), cols] for d, b, _ in mine])
            lse = lse_ref[j : j + 1, rows]
            raw = dot_nt(keys, q_ref[rows, cols])
            prob_grad = dot_nt(vals, g_ref[rows, cols])
            probs, weighted = [], None
            for i, (_, _, level) in enumerate(mine):
                here = slice(i * BLOCK, (i + 1) * BLOCK)
                if level is None:
                    logits = jnp.where(causal, raw[here] * LOG2_SCALE - lse, MASKED)
                else:
                    off = lse + jnp.where(use_ref[n * LEVELS + level] == 1, 0.0, -MASKED)
                    logits = raw[here] * LOG2_SCALE - off
                prob = jnp.exp2(logits)
                probs.append(prob)
                part = prob * prob_grad[here]
                weighted = part if weighted is None else weighted + part
            delta = jnp.sum(weighted, 0, keepdims=True)
            score_grad = [
                (prob * SCALE * (prob_grad[i * BLOCK : (i + 1) * BLOCK] - delta)).astype(BF16)
                for i, prob in enumerate(probs)
            ]
            dq_ref[rows, cols] = dot_tn(cat(score_grad), keys).astype(BF16)
            stats_ref[j : j + 1, rows] = lse
            stats_ref[heads_up + j : heads_up + j + 1, rows] = delta
        flags = jnp.zeros((8, BLOCK), F32)
        level_row = lax.broadcasted_iota(jnp.int32, (8, BLOCK), 0)
        for level in range(LEVELS):
            flag = jnp.where(use_ref[n * LEVELS + level] == 1, 1.0, 0.0)
            flags = jnp.where(level_row == level, flag, flags)
        stats_ref[2 * heads_up :, rows] = flags
    for row in range(heads, heads_up):
        for first in (0, heads_up):
            stats_ref[first + row : first + row + 1, :] = jnp.zeros((1, stats_ref.shape[1]), F32)


def key_kernel(tiles, count, heads, heads_up, k_ref, v_ref, *refs):
    q_refs, g_refs, s_refs = refs[:count], refs[count : 2 * count], refs[2 * count : 3 * count]
    dk_ref, dv_ref = refs[3 * count :]
    causal = causal_tile()
    for b in range(len(tiles)):
        rows = block_rows(b)
        seers = [
            (d, n, level)
            for n, mine in enumerate(tiles)
            for d, block, level in mine
            if block == b
        ]
        for j in range(heads):
            cols = head_cols(j)
            ques = cat([q_refs[d][block_rows(n), cols] for d, n, _ in seers])
            grads = cat([g_refs[d][block_rows(n), cols] for d, n, _ in seers])
            raw = dot_nt(k_ref[rows, cols], ques)
            prob_grad = dot_nt(v_ref[rows, cols], grads)
            probs, score_grads = [], []
            for i, (d, n, level) in enumerate(seers):
                here = slice(i * BLOCK, (i + 1) * BLOCK)
                lse = s_refs[d][j : j + 1, block_rows(n)]
                delta = s_refs[d][heads_up + j : heads_up + j + 1, block_rows(n)]
                if level is None:
                    logits = jnp.where(causal, raw[:, here] * LOG2_SCALE - lse, MASKED)
                else:
                    row = 2 * heads_up + level
                    off = lse + (1.0 - s_refs[d][row : row + 1, block_rows(n)]) * (-MASKED)
                    logits = raw[:, here] * LOG2_SCALE - off
                prob = jnp.exp2(logits)
                probs.append(prob.astype(BF16))
                score_grads.append((prob * SCALE * (prob_grad[:, here] - delta)).astype(BF16))
            dv_ref[rows, cols] = dot(cat(probs, 1), grads).astype(BF16)
            dk_ref[rows, cols] = dot(cat(score_grads, 1), ques).astype(BF16)


class Stream:
    def __init__(self, pieces, held, sems):
        self.held = held
        self.copies = [
            pltpu.make_async_copy(piece, held.at[i], sems.at[i]) for i, piece in enumerate(pieces)
        ]
        for copy in self.copies[:2]:
            copy.start()

    def piece(self, i):
        self.copies[i].wait()
        if i + 2 < len(self.copies):
            self.copies[i + 2].start()
        return self.held.at[i]


def mixed_grad_kernel(count, given, place_ref, *refs):
    total = refs[0][...] if given else None
    c_refs, w_ref, out_ref, held, sems = refs[given : given + count], *refs[given + count :]
    depth = c_refs[0].shape[1]
    firsts = [pl.multiple_of(place_ref[i] * depth, depth) for i in range(count)]
    stream = Stream([w_ref.at[pl.ds(first, depth), :] for first in firsts], held, sems)
    for i in range(count):
        step = dot(c_refs[i][...], stream.piece(i)[...])
        total = step if total is None else total + step
    out_ref[...] = total.astype(out_ref.dtype)


def partial_kernel(split, place_ref, m_ref, w_ref, keep_ref, give_ref, held, sems):
    depth = keep_ref.shape[2]
    height = depth // split
    firsts = [place_ref[i] * depth + part * height for i in range(4) for part in range(split)]
    pieces = [w_ref.at[pl.ds(pl.multiple_of(first, height), height), :] for first in firsts]
    stream = Stream(pieces, held, sems)
    outs = [(give_ref, 0), (give_ref, 1), (keep_ref, 0), (keep_ref, 1)]
    for i, (out_ref, at) in enumerate(outs):
        for part in range(split):
            piece = stream.piece(i * split + part)
            cols = slice(part * height, (part + 1) * height)
            out_ref[at, :, cols] = dot_nt(m_ref[...], piece[...]).astype(BF16)


def weight_grad_kernel(which, given, place_ref, *refs):
    c_ref, m_refs, out_ref = refs[given], refs[given + 1 : -1], refs[-1]
    features = out_ref.shape[0]
    height = min(512, features)
    for first in range(0, features, height):
        rows = slice(first, first + height)
        total = refs[0][rows, :] if given else None
        fold = len(m_refs) // len(which)
        for i, p in enumerate(which):
            mixed = functools.reduce(jnp.add, [m[...] for m in m_refs[i * fold : (i + 1) * fold]])
            part = dot_tn(c_ref[place_ref[p], :, rows], mixed)
            total = part if total is None else total + part
        out_ref[rows, :] = total.astype(out_ref.dtype)


def cost(flops, bytes_accessed, exps=0, weight=1.0):
    return pl.CostEstimate(
        flops=int(flops * weight),
        bytes_accessed=int(bytes_accessed * weight),
        transcendentals=int(exps * weight),
    )


def kernel_call(body, name, scalars, arrays, out_shape, estimate, outside=(), scratch=()):
    smem = pl.BlockSpec(memory_space=pltpu.SMEM)
    vmem = pl.BlockSpec(memory_space=pltpu.VMEM)
    return pl.pallas_call(
        body,
        in_specs=[smem] * len(scalars)
        + [vmem] * len(arrays)
        + [pl.BlockSpec(memory_space=pltpu.HBM)] * len(outside),
        out_specs=jax.tree.map(lambda _: vmem, out_shape),
        out_shape=out_shape,
        scratch_shapes=list(scratch),
        compiler_params=pltpu.CompilerParams(
            vmem_limit_bytes=STREAM_LIMIT if outside else VMEM_LIMIT
        ),
        cost_estimate=estimate,
        name=name,
    )(*scalars, *arrays, *outside)


def weight_scratch(count, depth, columns):
    return [pltpu.VMEM((count, depth, columns), BF16), pltpu.SemaphoreType.DMA((count,))]


VMEM_LIMIT = 20 * 1024 * 1024
WEIGHTS = dict(mixed_grad=0.0, forward=0.0, partial=0.0, query=100.0, key=100.0, weight=0.0)
STREAM_LIMIT = 54 * 1024 * 1024


def two_by_two():
    return lax.axis_size("head") == 2 and lax.axis_size("rep") == 2


def features_here(value):
    heads, reps = lax.axis_size("head"), lax.axis_size("rep")
    if two_by_two():
        h, r = lax.axis_index("head"), lax.axis_index("rep")
        places = [2 * h + r, 2 * h + 1 - r, 2 * (1 - h) + r, 2 * (1 - h) + 1 - r]
        rest = swap(value, "head")
        return [value, swap(value, "rep")], rest, jnp.stack(places).astype(jnp.int32)
    count = heads * reps
    gathered = lax.all_gather(value, ("head", "rep"), axis=0)
    blocks = [gathered[i] for i in range(count)]
    return blocks[: count // 2], blocks[count // 2 :], jnp.arange(count, dtype=jnp.int32)


def other_features(rest, *others):
    if two_by_two():
        return [rest, swap(after(rest, *others), "rep")]
    return rest


def attended_partial(mixed_heads, out_weight, places, estimate):
    if two_by_two():
        rows = mixed_heads.shape[0]
        share = out_weight.shape[0] // 4
        order = jnp.stack([places[1], places[3], places[0], places[2]])
        return kernel_call(
            functools.partial(partial_kernel, 1),
            "attended_partial",
            [order],
            [mixed_heads],
            [jax.ShapeDtypeStruct((2, rows, share), BF16)] * 2,
            estimate,
            [out_weight],
            weight_scratch(4, share, mixed_heads.shape[1]),
        )
    partial_value = lax.dot_general(mixed_heads, out_weight, NT, preferred_element_type=F32)
    return [partial_value.astype(BF16)]


def core_sum(partial_products):
    if len(partial_products) == 1:
        return partial_products
    keep, give = partial_products
    got = swap(give, "rep")
    return [
        keep[0].astype(F32) + got[0].astype(F32),
        (keep[1].astype(F32) + got[1].astype(F32)).astype(BF16),
    ]


def chip_sum(shares, *others):
    if len(shares) == 1:
        return lax.psum_scatter(shares[0], ("head", "rep"), scatter_dimension=1, tiled=True)
    return (shares[0] + swap(after(shares[1], *others), "head").astype(F32)).astype(BF16)


def per_device(queries, keys, values, out_weight, level_mask, cotangent):
    rows, columns = queries.shape
    features = out_weight.shape[0]
    heads = columns // HEAD_DIM
    heads_up = -(-heads // 8) * 8
    blocks = rows // BLOCK
    peers = lax.axis_size("seq")
    place = lax.axis_index("seq")
    tiles = seen_tiles(blocks, peers)
    distances = sorted({d for mine in tiles for d, _, _ in mine})
    count = len(distances)
    slot = {d: i for i, d in enumerate(distances)}
    tiles = [[(slot[d], b, level) for d, b, level in mine] for mine in tiles]
    pairs = sum(len(mine) for mine in tiles)
    attention_flops = 2 * heads * pairs * BLOCK * BLOCK * HEAD_DIM
    array_bytes = 2 * rows * columns
    exps = heads * pairs * BLOCK * BLOCK
    like_queries = jax.ShapeDtypeStruct((rows, columns), BF16)

    def further(got, sign, *others):
        near, far = distances[len(got) - 1], distances[len(got)]
        return got + [shift(after(got[-1], *others), sign * (far - near))]

    block_ids = place * blocks + jnp.arange(blocks, dtype=jnp.int32)
    offsets = 2 ** jnp.arange(LEVELS, dtype=jnp.int32)
    use = ((block_ids[:, None] >= offsets[None]) & (level_mask == 1)).astype(jnp.int32)
    use = use.reshape(-1)

    kv_all = further([jnp.concatenate([keys, values])], 1)
    query_all = further([queries], -1)
    c_blocks, c_rest, c_places = features_here(cotangent)
    half = len(c_blocks)
    part_cols = cotangent.shape[1]
    mixed_sum = []
    for part in range(2):
        if part:
            c_blocks = c_blocks + other_features(c_rest, *mixed_sum, query_all[1])
        mine = slice(part * half, (part + 1) * half)
        mixed_sum = [
            kernel_call(
                functools.partial(mixed_grad_kernel, half, part),
                "mixed_grad",
                [c_places[mine]],
                [*mixed_sum, *c_blocks[mine]],
                jax.ShapeDtypeStruct((rows, columns), BF16 if part else F32),
                cost(rows * columns * features, columns * features, 0, WEIGHTS["mixed_grad"] * (1 - part)),
                [out_weight],
                weight_scratch(half, part_cols, columns),
            )
        ]
    mixed_grad = mixed_sum[0]
    group_count = len(c_blocks)
    while len(kv_all) < count:
        kv_all = further(kv_all, 1, mixed_grad)
    grad_all = further([mixed_grad], -1)
    while len(query_all) < count:
        query_all = further(query_all, -1, mixed_grad)
    while len(grad_all) < count:
        grad_all = further(grad_all, -1)

    h, r = lax.axis_index("head"), lax.axis_index("rep")
    n_head, n_rep = lax.axis_size("head"), lax.axis_size("rep")
    step_of = lambda i: (i // n_rep) + n_head * (i % n_rep)
    wanted = (place + step_of(h * n_rep + r)) % peers
    out_block = c_blocks[0]
    for i in range(1, group_count):
        out_block = jnp.where(c_places[i] == wanted, c_blocks[i], out_block)
    links = []
    for s in range(peers):
        for q in range(group_count):
            links.append((s * group_count + q, ((s + step_of(q)) % peers) * group_count + q))
    arrived = lax.ppermute(after(out_block, grad_all[1]), ("seq", "head", "rep"), links)

    mixed_heads, lse = kernel_call(
        functools.partial(forward_kernel, tiles, count, heads),
        "attention_forward",
        [use],
        [queries, *kv_all],
        [like_queries, jax.ShapeDtypeStruct((heads_up, rows), F32)],
        cost(2 * attention_flops, (2 * count + 2) * array_bytes, exps, WEIGHTS["forward"]),
    )

    near = {}
    if peers <= 4:
        near = {k: cyclic(mixed_heads, k) for k in sorted({1, peers - 1}) if 0 < k < peers}
    stats_shape = jax.ShapeDtypeStruct((2 * heads_up + 8, rows), F32)
    q_grad, stats = kernel_call(
        functools.partial(query_kernel, tiles, count, heads, heads_up),
        "attention_query_grad",
        [use],
        [after(queries, mixed_heads), mixed_grad, lse, *kv_all],
        [like_queries, stats_shape],
        cost(3 * attention_flops, (2 * count + 3) * array_bytes, exps, WEIGHTS["query"]),
    )
    stats_all = [stats] + [shift(stats, -d) for d in distances[1:]]
    partial_products = attended_partial(
        after(mixed_heads, query_all[-1], grad_all[-1]), out_weight, c_places, cost(2 * rows * columns * features, 2 * rows * features, 0, WEIGHTS["partial"])
    )
    shares = core_sum(partial_products)
    ct_across = swap(after(arrived, *partial_products), "head") if two_by_two() else arrived
    held = after(mixed_heads, ct_across, *near.values(), *stats_all[1:], *shares)
    if peers <= 4:
        mixed_all = [[mixed_heads]] + [[near[k]] if k in near else [] for k in range(1, peers)]
        if peers == 4:
            up = lax.ppermute(after(near[1], held), "seq", [(1, 2), (2, 3)])
            down = lax.ppermute(after(near[3], held), "seq", [(1, 0), (2, 1)])
            mixed_all[2] = [up, down]
    else:
        gathered = lax.all_gather(mixed_heads, "seq", axis=0)
        mixed_all = [
            [lax.dynamic_index_in_dim(gathered, (place - k) % peers, 0, False)]
            for k in range(peers)
        ]
    attended = chip_sum(shares, held)
    k_grad, v_grad = kernel_call(
        functools.partial(key_kernel, tiles, count, heads, heads_up),
        "attention_key_grad",
        [],
        [after(keys, held), values, *query_all, *grad_all, *stats_all],
        [like_queries] * 2,
        cost(4 * attention_flops, (2 * count + 4) * array_bytes, exps, WEIGHTS["key"]),
    )

    if two_by_two():
        ct_blocks = [arrived, swap(after(arrived, held), "rep"), *other_features(ct_across, held)]
    else:
        ct_blocks, ct_rest, _ = features_here(arrived)
        ct_blocks = ct_blocks + ct_rest
    ct = jnp.stack(ct_blocks)
    steps = step_of(c_places)
    ct_at = jnp.sum(
        jnp.where(steps[None] == jnp.arange(peers)[:, None], jnp.arange(group_count)[None], 0), 1
    ).astype(jnp.int32)
    early = sorted({0, 1, peers - 1}) if 2 < peers <= 4 else [0]
    late = [k for k in range(peers) if k not in early]
    weight_sum = []
    for part, which in enumerate((early, late)):
        if not which:
            weight_sum = [weight_sum[0].astype(BF16)]
            break
        ranges = [value for k in which for value in mixed_all[k]]
        if part:
            ranges[0] = after(ranges[0], k_grad, attended)
        weight_sum = [
            kernel_call(
                functools.partial(weight_grad_kernel, which, part),
                "weight_grad",
                [ct_at],
                [*weight_sum, ct, *ranges],
                jax.ShapeDtypeStruct((part_cols, columns), BF16 if part else F32),
                cost(2 * part_cols * columns * rows * len(which), array_bytes * len(which), 0, WEIGHTS["weight"]),
            )
        ]
    weight_grad = weight_sum[0]
    return (attended, q_grad, k_grad, v_grad, weight_grad)


def solution(mesh):
    shared = P(("groups", "seq"), ("head", "rep"))
    return jax.shard_map(
        per_device,
        mesh=mesh,
        in_specs=(shared, shared, shared, P(None, ("head", "rep")), P(("groups", "seq"), None), shared),
        out_specs=(shared,) * 5,
        check_vma=False,
    )
```
